32 devices in a mesh: gx: 4 (over x, core), gz: 8 (over z, y).
Axes of the slice: x: 2, y: 2, z: 4, core: 2. Of those that a mesh axis runs over, the one named last changes fastest.
Arguments:
- conserved: float32 [5, 16, 32, 128], P(None, 'gx', 'gz'), may hold values from -1.1 to 5.5, as said below
- jacobian: float32 [16, 32, 128], P('gx', 'gz'), may hold values from 0.5 to 2
- metric: float32 [3, 3, 16, 32, 128], P(None, None, 'gx', 'gz'), may hold values from -0.45 to 2.01, as said below
- x_master: int32 [8, 8, 32], P('gx', 'gz'), may hold values from 0 to 1, as said below
- x_flip: int32 [8, 8, 32], P('gx', 'gz'), may hold values from 0 to 7, as said below
- z_master: int32 [4, 16, 32], P('gx', 'gz'), may hold values from 0 to 1, as said below
- z_flip: int32 [4, 16, 32], P('gx', 'gz'), may hold values from 0 to 7, as said below
Outputs:
- rhs: float32 [5, 16, 32, 128], P(None, 'gx', 'gz')
The draws below stay inside these ranges and needn't reach their ends.
Inputs may be any that keep to these rules, and one draw needn't show every extreme that they name: conserved[0] is at least 0.6, and the pressure 0.4 (conserved[4] - 0.5 |conserved[1:4]|^2 / conserved[0]) is at least 0.6. metric[g, g] lies between 0.49 and 2.01; every other entry has magnitude at most 0.45. `x_master`: rows 2 t and 2 t + 1 hold the faces on the lower and upper streamwise boundary of tile t; 1 marks that tile t holds the master side. Row 2 t + 1 equals 1 minus row 2 t + 2 (rows taken cyclically), so each face has exactly one master. `x_flip`: rows as in x_master; row 2 t + 1 equals row 2 t + 2 (rows taken cyclically). `z_master`: columns 2 t and 2 t + 1 hold the faces on the lower and upper spanwise boundary of tile t; 1 marks that tile t holds the master side. Column 2 t + 1 equals 1 minus column 2 t + 2 (taken cyclically). `z_flip`: columns as in z_master; column 2 t + 1 equals column 2 t + 2 (taken cyclically).
All inputs are finite; a program needn't handle non-finite values.
Results may differ from the reference program's by a relative error of at most 0.0003.
Values sent between devices are 32-bit elements; how exact they have to be, the bound alone decides.
No kernel may reach another device: no remote copies, remote signals or barrier semaphores. Data moves between devices by JAX's collectives and lax.ppermute only.
A program may use at most 64 MiB of HBM per device.

```python
import math
import jax
import jax.numpy as jnp
import numpy as np
from jax import lax

CX = 1
CZ = 1
EY = 32
XTILES = 4
ZTILES = 8
XE = 4
ZE = 8
XN = 16
ZN = 32
YN = 128


def draw_conserved(key, part):
    subkeys = jax.random.split(key, 3)
    grid_dims = (XN, ZN, YN)
    density = jax.random.uniform(subkeys[0], grid_dims, jnp.float32, 0.8, 1.25)
    velocity = 0.3 * jax.random.truncated_normal(subkeys[1], -2.5, 2.5, (3,) + grid_dims, jnp.float32)
    pressure = jax.random.uniform(subkeys[2], grid_dims, jnp.float32, 0.8, 1.25)
    energy = pressure / 0.4 + 0.5 * density * jnp.sum(velocity * velocity, 0)
    return jnp.concatenate([density[None], density[None] * velocity, energy[None]], 0)


def draw_metric(key, part):
    subkeys = jax.random.split(key, 2)
    full_dims = (3, 3, XN, ZN, YN)
    stretch = jnp.exp(jax.random.uniform(subkeys[0], full_dims, jnp.float32, math.log(0.5), math.log(2.0)))
    spread = 0.3
    skew_part = jax.random.uniform(subkeys[1], full_dims, jnp.float32, -spread, spread)
    identity = jnp.eye(3, dtype=jnp.float32).reshape(3, 3, 1, 1, 1)
    return identity * stretch + (1.0 - identity) * skew_part


def draw_x_master(key, part):
    subkeys = jax.random.split(key, 2)
    tile_share = jax.random.randint(subkeys[0], (XTILES, 1, 1), 1, 10)
    vote_draw = jax.random.randint(subkeys[1], (XTILES, ZE, EY), 0, 10)
    lower_flags = (vote_draw < tile_share).astype(jnp.int32)
    upper_flags = 1 - jnp.roll(lower_flags, -1, 0)
    return jnp.stack([lower_flags, upper_flags], 1).reshape(2 * XTILES, ZE, EY)


def draw_x_flip(key, part):
    code_draw = jax.random.randint(key, (XTILES, ZE, EY), 0, 8)
    return jnp.stack([code_draw, jnp.roll(code_draw, -1, 0)], 1).reshape(2 * XTILES, ZE, EY)


def draw_z_master(key, part):
    subkeys = jax.random.split(key, 2)
    tile_share = jax.random.randint(subkeys[0], (1, ZTILES, 1), 1, 10)
    vote_draw = jax.random.randint(subkeys[1], (XE, ZTILES, EY), 0, 10)
    lower_flags = (vote_draw < tile_share).astype(jnp.int32)
    upper_flags = 1 - jnp.roll(lower_flags, -1, 1)
    return jnp.stack([lower_flags, upper_flags], 2).reshape(XE, 2 * ZTILES, EY)


def draw_z_flip(key, part):
    code_draw = jax.random.randint(key, (XE, ZTILES, EY), 0, 8)
    return jnp.stack([code_draw, jnp.roll(code_draw, -1, 1)], 2).reshape(XE, 2 * ZTILES, EY)


def steps_of(stream_key, dims, shards, least, high):
    def one(position, shards_of):
        heights = jax.random.uniform(jax.random.fold_in(jax.random.fold_in(stream_key, 6), position), (shards_of,), jnp.float32, least / len(shards), high / len(shards))
        return jnp.repeat(jnp.exp(heights), dims[position] // shards_of).reshape((-1,) + (1,) * (len(dims) - position - 1))

    factor_of = one(*shards[0])
    for cut in shards[1:]:
        factor_of = factor_of * one(*cut)
    return factor_of


def setup_inputs(seed: int = 0) -> dict:
    keys = jax.random.split(jax.random.key(seed), 8)
    conserved = draw_conserved(jax.random.fold_in(keys[7], 71), 0)
    jacobian = jnp.clip(jnp.exp(math.log(2.0) - 1.3862944 * jax.random.uniform(keys[1], (XN, ZN, YN), jnp.float32) ** steps_of(keys[1], (XN, ZN, YN), ((0, 4), (1, 8)), -0.2, 0.2)), 0.5, 2.0)
    metric = draw_metric(jax.random.fold_in(keys[7], 71), 0)
    x_master = draw_x_master(jax.random.fold_in(keys[7], 71), 0)
    x_flip = draw_x_flip(jax.random.fold_in(keys[7], 71), 0)
    z_master = draw_z_master(jax.random.fold_in(keys[7], 71), 0)
    z_flip = draw_z_flip(jax.random.fold_in(keys[7], 71), 0)
    return dict(conserved=conserved, jacobian=jacobian, metric=metric, x_master=x_master, x_flip=x_flip, z_master=z_master, z_flip=z_flip)


gamma_gas = 1.4
visc_coef = 0.1
prandtl = 0.72
edge_weight = 1.0 / 6.0
highest = lax.Precision.HIGHEST

def node_table():
    points = np.array([-1.0, -math.sqrt(0.2), math.sqrt(0.2), 1.0])
    scales = np.array([np.prod([points[row_index] - points[rest_index] for rest_index in range(4) if rest_index != row_index]) for row_index in range(4)])
    deriv_table = np.zeros((4, 4))
    for row_index in range(4):
        for col_index in range(4):
            if row_index != col_index:
                deriv_table[row_index, col_index] = scales[row_index] / (scales[col_index] * (points[row_index] - points[col_index]))
        deriv_table[row_index, row_index] = -np.sum(deriv_table[row_index])
    return deriv_table

def derive(values, axis_pos):
    moved_last = jnp.moveaxis(values, axis_pos, -1)
    length = moved_last.shape[-1]
    grouped = moved_last.reshape(moved_last.shape[:-1] + (length // 4, 4))
    result = jnp.einsum('...n,mn->...m', grouped, jnp.asarray(node_table(), jnp.float32), precision=highest)
    return jnp.moveaxis(result.reshape(moved_last.shape), -1, axis_pos)

def primitives(values):
    density = values[0]
    velocity = values[1:4] / density
    pressure = (gamma_gas - 1.0) * (values[4] - 0.5 * density * lax.optimization_barrier(jnp.sum(velocity * velocity, 0)))
    return (density, velocity, pressure)

def lifted_of(values):
    density, velocity, pressure = primitives(values)
    return jnp.concatenate([velocity, (pressure / density)[None]], 0)

def total_flux(values, gradient):
    density, velocity, pressure = primitives(values)
    slopes = gradient.reshape((4, 3) + gradient.shape[1:])
    divergence = slopes[0, 0] + slopes[1, 1] + slopes[2, 2]
    heat_coef = visc_coef * gamma_gas / ((gamma_gas - 1.0) * prandtl)
    directions = []
    for direction in range(3):
        stress = [visc_coef * (slopes[component, direction] + slopes[direction, component]) for component in range(3)]
        stress[direction] = stress[direction] - 2.0 / 3.0 * visc_coef * divergence
        moment = [values[1 + component] * velocity[direction] - stress[component] for component in range(3)]
        moment[direction] = moment[direction] + pressure
        viscous_work = velocity[0] * stress[0] + velocity[1] * stress[1] + velocity[2] * stress[2]
        energy_flux = (values[4] + pressure) * velocity[direction] - viscous_work - heat_coef * slopes[3, direction]
        directions.append(jnp.stack([values[1 + direction]] + moment + [energy_flux]))
    return jnp.stack(directions)

def normal_part(flux, normal):
    return flux[0] * normal[0] + flux[1] * normal[1] + flux[2] * normal[2]

def wave_bound(values, normal):
    density, velocity, pressure = primitives(values)
    normal_size = jnp.sqrt(lax.optimization_barrier(jnp.sum(normal * normal, 0)))
    return jnp.abs(lax.optimization_barrier(jnp.sum(velocity * normal, 0))) + jnp.sqrt(gamma_gas * pressure / density) * normal_size

def mirror(values):
    return jnp.concatenate([values[0:1], -values[1:4], values[4:]], 0)

def take_range(values, start_at, stop_at, axis_pos):
    return lax.slice_in_dim(values, start_at, stop_at, 1, axis_pos)

def face_layers(values, axis_pos):
    length = values.shape[axis_pos]
    lowers = lax.slice_in_dim(values, 0, length, 4, axis_pos)
    uppers = lax.slice_in_dim(values, 3, length, 4, axis_pos)
    return (lowers, uppers)

def place_faces(lowers, uppers, axis_pos):
    middle = jnp.zeros_like(lowers)
    stacked = jnp.stack([lowers, middle, middle, uppers], axis_pos + 1)
    merged_dims = list(lowers.shape)
    merged_dims[axis_pos] = merged_dims[axis_pos] * 4
    return stacked.reshape(merged_dims)

def orient(layer_in, code_in, axis_pos, inverse):
    fields = layer_in.shape[0]
    if axis_pos == 1:
        blocks = layer_in.reshape(fields, layer_in.shape[1], layer_in.shape[2] // 4, 4, layer_in.shape[3] // 4, 4)
        code_grid = code_in[None, :, :, None, :, None]
        axis_one, axis_two = (3, 5)
    else:
        blocks = layer_in.reshape(fields, layer_in.shape[1] // 4, 4, layer_in.shape[2], layer_in.shape[3] // 4, 4)
        code_grid = code_in[None, :, None, :, :, None]
        axis_one, axis_two = (2, 5)
    swap_bit = code_grid // 4 % 2 == 1
    first_bit = code_grid % 2 == 1
    second_bit = code_grid // 2 % 2 == 1
    if inverse:
        blocks = jnp.where(second_bit, jnp.flip(blocks, axis_two), blocks)
        blocks = jnp.where(first_bit, jnp.flip(blocks, axis_one), blocks)
        blocks = jnp.where(swap_bit, jnp.swapaxes(blocks, axis_one, axis_two), blocks)
    else:
        blocks = jnp.where(swap_bit, jnp.swapaxes(blocks, axis_one, axis_two), blocks)
        blocks = jnp.where(first_bit, jnp.flip(blocks, axis_one), blocks)
        blocks = jnp.where(second_bit, jnp.flip(blocks, axis_two), blocks)
    return blocks.reshape(layer_in.shape)

def node_mask(flags, axis_pos):
    if axis_pos == 1:
        return jnp.repeat(jnp.repeat(flags, 4, 1), 4, 2)
    return jnp.repeat(jnp.repeat(flags, 4, 0), 4, 2)

def edge_tables(masters, flip_codes, per_tile, tile_axis):
    tile_total = masters.shape[tile_axis] // 2
    lower_masters = lax.slice_in_dim(masters, 0, 2 * tile_total, 2, tile_axis)
    lower_flips = lax.slice_in_dim(flip_codes, 0, 2 * tile_total, 2, tile_axis)
    element_total = tile_total * per_tile
    element = jnp.arange(element_total)
    up_tile = (element + 1) // per_tile % tile_total
    low_tile = element // per_tile
    mask_dims = [1, 1, 1]
    mask_dims[tile_axis] = element_total
    up_edge = ((element + 1) % per_tile == 0).reshape(mask_dims)
    low_edge = (element % per_tile == 0).reshape(mask_dims)
    up_flag = jnp.take(lower_masters, up_tile, axis=tile_axis)
    low_flag = jnp.take(lower_masters, low_tile, axis=tile_axis)
    up_lead = jnp.logical_not(up_edge) | (up_flag == 0)
    low_lead = jnp.logical_not(low_edge) | (low_flag == 0)
    up_code = jnp.where(up_edge, jnp.take(lower_flips, up_tile, axis=tile_axis), 0)
    low_code = jnp.where(low_edge, jnp.take(lower_flips, low_tile, axis=tile_axis), 0)
    return (up_lead, up_code, low_lead, low_code)

def wall_record(conserved, metric):
    stacked = jnp.concatenate([conserved, metric[2]], 0)
    lowers, uppers = face_layers(stacked, 3)
    element_total = lowers.shape[3]
    partner_up = jnp.concatenate([take_range(lowers, 1, element_total, 3), mirror(take_range(uppers, element_total - 1, element_total, 3))], 3)
    partner_low = jnp.concatenate([mirror(take_range(lowers, 0, 1, 3)), take_range(uppers, 0, element_total - 1, 3)], 3)
    return (3, lowers, uppers, partner_low, partner_up, partner_low[5:8], uppers[5:8])

def lift_surface(own_values, other_values, normal, own_metric, side_sign):
    average = 0.5 * (own_values + other_values)
    terms = average[:, None] * normal[None] - own_values[:, None] * own_metric[None]
    return side_sign / edge_weight * terms.reshape((12,) + own_values.shape[1:])

def lift_all(records, lifted, metric, jacobian):
    gradient_sum = 0.0
    for record in records:
        axis_pos, lowers, uppers, partner_low, partner_up, normal_low, normal_up = record[:7]
        metric_rows = metric[axis_pos - 1]
        volume_terms = (lifted[:, None] * metric_rows[None]).reshape((12,) + lifted.shape[1:])
        surf_low = lift_surface(lifted_of(lowers[:5]), lifted_of(partner_low[:5]), normal_low, lowers[5:8], -1.0)
        surf_up = lift_surface(lifted_of(uppers[:5]), lifted_of(partner_up[:5]), normal_up, uppers[5:8], 1.0)
        gradient_sum = gradient_sum + derive(volume_terms, axis_pos) + place_faces(surf_low, surf_up, axis_pos)
    return gradient_sum / jacobian

def face_terms(own_state, other_state, own_half, other_half, normal, own_contra, upper_side):
    fastest = jnp.maximum(wave_bound(own_state, normal), wave_bound(other_state, normal))
    if upper_side:
        state_jump = other_state - own_state
        side_sign = 1.0
    else:
        state_jump = own_state - other_state
        side_sign = -1.0
    face_flux = 0.5 * (own_half + other_half) - 0.5 * fastest * state_jump
    return side_sign / edge_weight * (face_flux - own_contra)

def face_section(record, own_pair, other_pair, contra):
    axis_pos, lowers, uppers, partner_low, partner_up, normal_low, normal_up = record[:7]
    contra_low, contra_up = face_layers(contra, axis_pos)
    terms_low = face_terms(lowers[:5], partner_low[:5], own_pair[0], other_pair[0], normal_low, contra_low, False)
    terms_up = face_terms(uppers[:5], partner_up[:5], own_pair[1], other_pair[1], normal_up, contra_up, True)
    return derive(contra, axis_pos) + place_faces(terms_low, terms_up, axis_pos)

def reference(conserved, jacobian, metric, x_master, x_flip, z_master, z_flip):
    lifted = lifted_of(conserved)
    records = []
    for axis_pos, masters, flip_codes, per_tile in ((1, x_master, x_flip, CX), (2, z_master, z_flip, CZ)):
        up_lead, up_code, low_lead, low_code = edge_tables(masters, flip_codes, per_tile, axis_pos - 1)
        stacked = jnp.concatenate([conserved, metric[axis_pos - 1]], 0)
        lowers, uppers = face_layers(stacked, axis_pos)
        partner_up = orient(jnp.roll(lowers, -1, axis_pos), up_code, axis_pos, False)
        partner_low = orient(jnp.roll(uppers, 1, axis_pos), low_code, axis_pos, True)
        normal_up = jnp.where(node_mask(up_lead, axis_pos), uppers[5:8], partner_up[5:8])
        normal_low = jnp.where(node_mask(low_lead, axis_pos), partner_low[5:8], lowers[5:8])
        records.append((axis_pos, lowers, uppers, partner_low, partner_up, normal_low, normal_up, up_code, low_code))
    records.append(wall_record(conserved, metric))
    gradient = lift_all(records, lifted, metric, jacobian)
    volume_flux = total_flux(conserved, gradient)
    rhs_sum = 0.0
    for record in records:
        axis_pos, lowers, uppers, partner_low, partner_up, normal_low, normal_up = record[:7]
        grad_low, grad_up = face_layers(gradient, axis_pos)
        if axis_pos == 3:
            element_total = grad_low.shape[3]
            other_grad_low = jnp.concatenate([take_range(grad_low, 0, 1, 3), take_range(grad_up, 0, element_total - 1, 3)], 3)
            other_grad_up = jnp.concatenate([take_range(grad_low, 1, element_total, 3), take_range(grad_up, element_total - 1, element_total, 3)], 3)
        else:
            other_grad_up = orient(jnp.roll(grad_low, -1, axis_pos), record[7], axis_pos, False)
            other_grad_low = orient(jnp.roll(grad_up, 1, axis_pos), record[8], axis_pos, True)
        own_pair = (normal_part(total_flux(lowers[:5], grad_low), normal_low), normal_part(total_flux(uppers[:5], grad_up), normal_up))
        other_pair = (normal_part(total_flux(partner_low[:5], other_grad_low), normal_low), normal_part(total_flux(partner_up[:5], other_grad_up), normal_up))
        contra = normal_part(volume_flux, metric[axis_pos - 1])
        rhs_sum = rhs_sum + face_section(record, own_pair, other_pair, contra)
    return -rhs_sum / jacobian
```

```python
import math

import jax
import jax.numpy as jnp
import numpy as np
from jax import lax
from jax.experimental import pallas as pl
from jax.experimental.pallas import tpu as pltpu
from jax.sharding import PartitionSpec as P

gamma_gas = 1.4
visc_coef = 0.1
prandtl = 0.72
lift = 6.0
heat_coef = visc_coef * gamma_gas / ((gamma_gas - 1.0) * prandtl)
vmem_bytes = 8 << 20
whole = pl.BlockSpec(memory_space=pltpu.VMEM)


def node_table():
    points = np.array([-1.0, -math.sqrt(0.2), math.sqrt(0.2), 1.0])
    scales = np.array([np.prod([points[i] - points[k] for k in range(4) if k != i]) for i in range(4)])
    table = np.zeros((4, 4))
    for i in range(4):
        for k in range(4):
            if i != k:
                table[i, k] = scales[i] / (scales[k] * (points[i] - points[k]))
        table[i, i] = -np.sum(table[i])
    return table


def weak_table():
    table = node_table()
    table[0, 0] += lift
    table[3, 3] -= lift
    return table


def rows_of(lanes):
    return lax.broadcasted_iota(jnp.int32, (8, lanes), 0)


def lanes_of(lanes):
    return lax.broadcasted_iota(jnp.int32, (8, lanes), 1)


def pick4(index, values):
    out = jnp.full(index.shape, values[3], jnp.float32)
    for k in (2, 1, 0):
        out = jnp.where(index == k, jnp.float32(values[k]), out)
    return out


def shift_weights(index, table):
    weights = {}
    for shift in range(-3, 4):
        weights[shift] = pick4(index, [table[j, j - shift] if 0 <= j - shift < 4 else 0.0 for j in range(4)])
    return weights


class Frame:
    def __init__(self, lanes):
        self.lanes = lanes
        row = rows_of(lanes)
        lane = lanes_of(lanes)
        self.row, self.lane = row, lane
        self.low_half = row < 4
        self.point_row = row % 4
        self.point_lane = lane % 4

    def deriv_weights(self):
        table = weak_table()
        self.weights_z = shift_weights(self.point_row, table)
        self.weights_y = shift_weights(self.point_lane, table)
        pair = lambda top, bottom: jnp.where(self.low_half, jnp.float32(top), jnp.float32(bottom))
        self.weights_x = [
            [
                pair(table[2 * t, 2 * s], table[2 * t + 1, 2 * s + 1]),
                pair(table[2 * t, 2 * s + 1], table[2 * t + 1, 2 * s]),
            ]
            for t in range(2)
            for s in range(2)
        ]

    def swap(self, tile):
        return pltpu.roll(tile, 4, 0)

    def deriv_x(self, pair):
        a, b = pair
        a2, b2 = self.swap(a), self.swap(b)
        w = self.weights_x
        return [
            w[2 * t][0] * a + w[2 * t][1] * a2 + w[2 * t + 1][0] * b + w[2 * t + 1][1] * b2
            for t in range(2)
        ]

    def deriv_rows(self, tile):
        out = self.weights_z[0] * tile
        for shift in (-3, -2, -1, 1, 2, 3):
            out = out + self.weights_z[shift] * pltpu.roll(tile, shift % 8, 0)
        return out

    def deriv_lanes(self, tile):
        out = self.weights_y[0] * tile
        for shift in (-3, -2, -1, 1, 2, 3):
            out = out + self.weights_y[shift] * pltpu.roll(tile, shift % self.lanes, 1)
        return out

    def face_x(self, pair):
        return jnp.where(self.low_half, pair[0], pair[1])

    def face_z(self, pair):
        side = jnp.where(self.low_half, 0, 3)
        index = side + 4 * (self.point_row % 2)
        return jnp.where(self.point_row < 2, sub_gather(pair[0], index), sub_gather(pair[1], index))

    def spread_z(self, face):
        upper = jnp.where(self.point_row == 3, 4, 0)
        inner = jnp.where(self.low_half, 0, 1)
        return [sub_gather(face, upper + inner + 2 * t) for t in range(2)]

    def sides(self, low, up):
        return jnp.where(self.low_half, jnp.float32(low), jnp.float32(up))

    def sign_lanes(self):
        return jnp.where(
            self.point_lane == 3, jnp.float32(lift), jnp.where(self.point_lane == 0, jnp.float32(-lift), 0.0)
        )

    def sign_rows(self):
        return jnp.where(
            self.point_row == 3, jnp.float32(lift), jnp.where(self.point_row == 0, jnp.float32(-lift), 0.0)
        )


def sub_gather(tile, index):
    return jnp.take_along_axis(tile, index, axis=0)


def lane_gather(tile, index):
    return jnp.take_along_axis(tile, index, axis=1)


def primitive(state):
    inverse = 1.0 / state[0]
    velocity = [state[1 + j] * inverse for j in range(3)]
    kinetic = state[1] * velocity[0] + state[2] * velocity[1] + state[3] * velocity[2]
    pressure = (gamma_gas - 1.0) * (state[4] - 0.5 * kinetic)
    return velocity, pressure, pressure * inverse


def combos(values, rows):
    w0, w1, w2, w3 = values
    m0, m1, m2 = rows
    return [
        w0 * m0,
        w1 * m1,
        w2 * m2,
        w0 * m1 + w1 * m0,
        w0 * m2 + w2 * m0,
        w1 * m2 + w2 * m1,
        w3 * m0,
        w3 * m1,
        w3 * m2,
    ]


def normal_flux(state, velocity, pressure, slopes, normal):
    m0, m1, m2 = normal
    speed = velocity[0] * m0 + velocity[1] * m1 + velocity[2] * m2
    spread = (visc_coef * 2.0 / 3.0) * (slopes[0] + slopes[1] + slopes[2])
    t00, t11, t22 = [2.0 * visc_coef * slopes[d] - spread for d in range(3)]
    t01, t02, t12 = [visc_coef * slopes[3 + d] for d in range(3)]
    stress = [
        t00 * m0 + t01 * m1 + t02 * m2,
        t01 * m0 + t11 * m1 + t12 * m2,
        t02 * m0 + t12 * m1 + t22 * m2,
    ]
    heat = heat_coef * (slopes[6] * m0 + slopes[7] * m1 + slopes[8] * m2)
    work = velocity[0] * stress[0] + velocity[1] * stress[1] + velocity[2] * stress[2]
    out = [state[0] * speed]
    for j in range(3):
        out.append(state[1 + j] * speed + pressure * normal[j] - stress[j])
    out.append((state[4] + pressure) * speed - work - heat)
    return out, speed, heat


def wave(speed, theta, normal_size):
    return jnp.abs(speed) + jnp.sqrt(gamma_gas * theta) * normal_size


def size_of(normal):
    return jnp.sqrt(normal[0] * normal[0] + normal[1] * normal[1] + normal[2] * normal[2])


def pack(frame, fields, low_ref, up_ref):
    fields = list(fields)
    if len(fields) % 2:
        fields.append(fields[-1])
    for g in range(len(fields) // 2):
        a, b = fields[2 * g], fields[2 * g + 1]
        low_ref[8 * g : 8 * g + 8, :] = jnp.where(frame.low_half, a, frame.swap(b))
        up_ref[8 * g : 8 * g + 8, :] = jnp.where(frame.low_half, frame.swap(a), b)


def unpack(frame, left_ref, right_ref, count):
    fields = []
    for g in range((count + 1) // 2):
        left = left_ref[8 * g : 8 * g + 8, :]
        right = right_ref[8 * g : 8 * g + 8, :]
        fields.append(jnp.where(frame.low_half, left, frame.swap(right)))
        fields.append(jnp.where(frame.low_half, frame.swap(left), right))
    return fields[:count]


def spread_flags(frame, flags):
    count = flags.shape[-1]
    hit = lax.broadcasted_iota(jnp.int32, (count, frame.lanes), 0) == (
        lax.broadcasted_iota(jnp.int32, (count, frame.lanes), 1) // 4
    )
    wide = jnp.dot(
        flags.astype(jnp.float32), hit.astype(jnp.float32), preferred_element_type=jnp.float32
    )
    wide = (wide + 0.5).astype(jnp.int32)
    shape = (8, frame.lanes)
    return jnp.where(
        frame.low_half, jnp.broadcast_to(wide[0:1], shape), jnp.broadcast_to(wide[1:2], shape)
    )


def turn_indices(frame, code, forward_low):
    swap = (code & 4) != 0
    first = (code & 1) * 3
    second = ((code >> 1) & 1) * 3
    forward = frame.low_half if forward_low else jnp.logical_not(frame.low_half)
    flip_a = jnp.where(forward, second, first)
    flip_b = jnp.where(forward, first, second)
    row4, lane4 = frame.point_row, frame.point_lane
    lane_base = frame.lane - lane4
    row_base = frame.row - row4
    step1 = lane_base + jnp.where(swap, (lane4 - row4) & 3, lane4)
    step2 = row_base + jnp.where(swap, (lane4 - (row4 ^ flip_b)) & 3, row4 ^ first)
    step3 = lane_base + jnp.where(swap, ((lane4 ^ flip_a) + (row4 ^ flip_b)) & 3, lane4 ^ second)
    return step1, step2, step3


def turn(tile, indices):
    return lane_gather(sub_gather(lane_gather(tile, indices[0]), indices[1]), indices[2])


def load_pair(ref, f):
    return [ref[f, 0:8, :], ref[f, 8:16, :]]


def load_state(ref):
    pairs = [load_pair(ref, f) for f in range(5)]
    return [[pairs[f][t] for f in range(5)] for t in range(2)]


def load_rows(ref, g):
    pairs = [load_pair(ref, 3 * g + d) for d in range(3)]
    return [[pairs[d][t] for d in range(3)] for t in range(2)]


def by_field(tiles):
    return [[tiles[0][f], tiles[1][f]] for f in range(len(tiles[0]))]


def lane_partner(frame, tile, flip):
    before = pltpu.roll(tile, 1, 1)
    after = pltpu.roll(tile, frame.lanes - 1, 1)
    other = jnp.where(frame.point_lane == 3, after, before)
    wall = (frame.lane == 0) | (frame.lane == frame.lanes - 1)
    return jnp.where(wall, -tile if flip else tile, other)


def lane_normal(frame, rows):
    take_before = (frame.point_lane == 0) & (frame.lane != 0)
    return [jnp.where(take_before, pltpu.roll(r, 1, 1), r) for r in rows]


def first_kernel(cons, jac, met, xm_ref, xf_ref, grad_out, turned_out, low_out, up_out):
    frame = Frame(cons.shape[-1])
    frame.deriv_weights()
    state = load_state(cons)
    rows = [load_rows(met, g) for g in range(3)]
    lifted = []
    for t in range(2):
        velocity, _, theta = primitive(state[t])
        lifted.append(velocity + [theta])
    cx = by_field([combos(lifted[t], rows[0][t]) for t in range(2)])
    cz = by_field([combos(lifted[t], rows[1][t]) for t in range(2)])
    cy = by_field([combos(lifted[t], rows[2][t]) for t in range(2)])
    sign = frame.sign_lanes()
    lane_part = []
    for t in range(2):
        other = [lane_partner(frame, lifted[t][k], k < 3) for k in range(4)]
        mean = [0.5 * (lifted[t][k] + other[k]) for k in range(4)]
        lane_part.append(combos(mean, lane_normal(frame, rows[2][t])))
    grad = []
    for f in range(9):
        dx = frame.deriv_x(cx[f])
        grad.append(
            [
                dx[t]
                + frame.deriv_rows(cz[f][t])
                + frame.deriv_lanes(cy[f][t])
                + sign * lane_part[t][f]
                for t in range(2)
            ]
        )
    for f in range(9):
        for t in range(2):
            grad_out[f, 8 * t : 8 * t + 8, :] = grad[f][t]

    inverse = [1.0 / jac[0:8, :], 1.0 / jac[8:16, :]]
    state_f = by_field(state)
    code = spread_flags(frame, xf_ref[...])
    lead = spread_flags(frame, xm_ref[...]) == 1
    indices = turn_indices(frame, code, True)
    own_x = [frame.face_x(p) for p in state_f + by_field(rows[0])]
    turned = [turn(p, indices) for p in own_x + [frame.face_x(inverse)]]
    for f in range(9):
        turned_out[8 * f : 8 * f + 8, :] = turned[f]
    velocity, _, theta = primitive(turned[:5])
    line = velocity + [theta]
    outer = (frame.point_row == 0) | (frame.point_row == 3)
    pick = jnp.where(frame.low_half, 0, 3) + jnp.where(frame.point_row >= 2, 4, 0)
    merge = lambda a, b: jnp.where(outer, sub_gather(a, pick), sub_gather(b, pick))
    zero = jnp.zeros_like(line[0])
    edges = [merge(line[0], line[1]), merge(line[2], line[3])]
    for d in range(3):
        edges.append(
            merge(jnp.where(lead, turned[5 + d], zero), jnp.where(lead, own_x[5 + d], zero))
        )
    faces = [frame.face_z(p) for p in state_f + by_field(rows[1]) + [inverse] + grad]
    pack(frame, faces + edges, low_out, up_out)


def second_kernel(
    cons, met, zm_ref, zf_ref, xf_ref, grad_in, turned_in, left, right, grad_out, low_out, up_out
):
    frame = Frame(cons.shape[-1])
    code = spread_flags(frame, zf_ref[...])
    lead = spread_flags(frame, zm_ref[...]) == 1
    indices = turn_indices(frame, code, False)
    got = unpack(frame, left, right, 23)
    other = [turn(p, indices) for p in got[:8]]
    own = [frame.face_z(load_pair(cons, f)) for f in range(5)]
    own_rows = [frame.face_z(load_pair(met, 3 + d)) for d in range(3)]
    velocity, _, theta = primitive(own)
    velocity2, _, theta2 = primitive(other[:5])
    mean = [0.5 * (a + b) for a, b in zip(velocity + [theta], velocity2 + [theta2])]
    normal = [jnp.where(lead, own_rows[d], other[5 + d]) for d in range(3)]
    part = combos(mean, normal)
    sign = frame.sign_rows()
    faces = []
    x_code = spread_flags(frame, xf_ref[...])
    x_indices = turn_indices(frame, x_code, True)
    for f in range(9):
        spread = frame.spread_z(part[f])
        total = [grad_in[f, 8 * t : 8 * t + 8, :] + sign * spread[t] for t in range(2)]
        for t in range(2):
            grad_out[f, 8 * t : 8 * t + 8, :] = total[t]
        faces.append(turn(frame.face_x(total), x_indices))
    turned = [turned_in[8 * f : 8 * f + 8, :] for f in range(9)]
    odd = frame.point_row % 2
    high = jnp.where(frame.point_row >= 2, 4, 0)
    both = high + jnp.where(frame.low_half, odd, 3 - odd)
    outer = high + jnp.where(frame.low_half, 0, 3)
    lines = [sub_gather(got[18], both), sub_gather(got[19], both)]
    lines.append(jnp.where(odd == 0, sub_gather(got[20], outer), sub_gather(got[21], outer)))
    lines.append(sub_gather(got[22], outer))
    pack(frame, turned + faces + lines, low_out, up_out)


def third_kernel(
    cons, jac, met, xm_ref, zm_ref, zf_ref, grad_in, left_z, right_z, left_x, right_x, out
):
    frame = Frame(cons.shape[-1])
    frame.deriv_weights()
    state = load_state(cons)
    state_f = by_field(state)
    rows = [load_rows(met, g) for g in range(3)]
    inverse = [1.0 / jac[0:8, :], 1.0 / jac[8:16, :]]
    prims = [primitive(state[t]) for t in range(2)]
    got_z = unpack(frame, left_z, right_z, 23)
    got_x = unpack(frame, left_x, right_x, 22)
    x_lead = spread_flags(frame, xm_ref[...]) == 1
    z_lead = spread_flags(frame, zm_ref[...]) == 1
    z_indices = turn_indices(frame, spread_flags(frame, zf_ref[...]), False)
    face_sign = frame.sides(-lift, lift)
    side_sign = frame.sides(-1.0, 1.0)

    own = [frame.face_x(p) for p in state_f]
    own_rows = [frame.face_x(p) for p in by_field(rows[0])]
    own_prim = primitive(own)
    other = got_x[:5]
    other_prim = primitive(other)
    normal_x = [jnp.where(x_lead, own_rows[d], got_x[5 + d]) for d in range(3)]
    mean = [
        0.5 * (a + b)
        for a, b in zip(own_prim[0] + [own_prim[2]], other_prim[0] + [other_prim[2]])
    ]
    part = combos(mean, normal_x)
    slopes = []
    for f in range(9):
        lifted_part = face_sign * part[f]
        zero = jnp.zeros_like(lifted_part)
        tiles = [
            grad_in[f, 0:8, :] + jnp.where(frame.low_half, lifted_part, zero),
            grad_in[f, 8:16, :] + jnp.where(frame.low_half, zero, lifted_part),
        ]
        slopes.append([tiles[t] * inverse[t] for t in range(2)])
    own_slopes = [frame.face_x(p) for p in slopes]
    other_slopes = [(got_x[9 + f] - face_sign * part[f]) * got_x[8] for f in range(9)]

    def face_flux(own, own_prim, own_slopes, other, other_prim, other_slopes, normal):
        size = size_of(normal)
        flux1, speed1, _ = normal_flux(own, own_prim[0], own_prim[1], own_slopes, normal)
        flux2, speed2, _ = normal_flux(other, other_prim[0], other_prim[1], other_slopes, normal)
        fastest = jnp.maximum(wave(speed1, own_prim[2], size), wave(speed2, other_prim[2], size))
        half = 0.5 * side_sign * fastest
        return [
            0.5 * (flux1[c] + flux2[c]) - half * (other[c] - own[c]) for c in range(5)
        ]

    flux_x = face_flux(own, own_prim, own_slopes, other, other_prim, other_slopes, normal_x)

    edge_a = jnp.where(frame.low_half, 0, 2) + jnp.where(frame.point_row >= 2, 4, 0)
    edge_b = edge_a + 1
    lines = [
        sub_gather(got_x[18], edge_a),
        sub_gather(got_x[18], edge_b),
        sub_gather(got_x[19], edge_a),
        sub_gather(got_x[19], edge_b),
    ]
    line_rows = [
        sub_gather(got_x[20], edge_a),
        sub_gather(got_x[20], edge_b),
        sub_gather(got_x[21], edge_a),
    ]
    own_edge = jnp.where(frame.low_half, 0, 4) + jnp.where(frame.point_row >= 2, 2, 1)
    line_rows = [line_rows[d] + sub_gather(got_z[20 + d], own_edge) for d in range(3)]
    raw_prim = primitive(got_z[:5])
    edge_mean = [0.5 * (a + b) for a, b in zip(raw_prim[0] + [raw_prim[2]], lines)]
    edge_part = combos(edge_mean, line_rows)
    edge_sign = frame.sign_rows()
    other_grad = [turn(got_z[9 + f] + edge_sign * edge_part[f], z_indices) for f in range(9)]
    turned = [turn(p, z_indices) for p in got_z[:9]]
    other = turned[:5]
    other_prim = primitive(other)
    own = [frame.face_z(p) for p in state_f]
    own_prim = primitive(own)
    own_rows = [frame.face_z(p) for p in by_field(rows[1])]
    normal_z = [jnp.where(z_lead, own_rows[d], turned[5 + d]) for d in range(3)]
    mean = [
        0.5 * (a + b)
        for a, b in zip(own_prim[0] + [own_prim[2]], other_prim[0] + [other_prim[2]])
    ]
    part = combos(mean, normal_z)
    other_slopes = [(other_grad[f] - face_sign * part[f]) * turned[8] for f in range(9)]
    own_slopes = [frame.face_z(p) for p in slopes]
    flux_z = face_flux(own, own_prim, own_slopes, other, other_prim, other_slopes, normal_z)

    slopes_t = [[slopes[f][t] for f in range(9)] for t in range(2)]
    sign_y = frame.sign_lanes()
    up_lane = frame.point_lane == 3
    wall = (frame.lane == 0) | (frame.lane == frame.lanes - 1)
    volume = []
    lane_flux = []
    for t in range(2):
        velocity, pressure, theta = prims[t]
        volume.append(
            [normal_flux(state[t], velocity, pressure, slopes_t[t], rows[g][t])[0] for g in range(3)]
        )
        normal = lane_normal(frame, rows[2][t])
        half, speed, heat = normal_flux(state[t], velocity, pressure, slopes_t[t], normal)
        own_wave = wave(speed, theta, size_of(normal))
        fastest = jnp.maximum(own_wave, lane_partner(frame, own_wave, False))
        mirrored = [-half[0], half[1], half[2], half[3], -half[4] - 2.0 * heat]
        direction = jnp.where(up_lane, jnp.float32(0.5), jnp.float32(-0.5)) * fastest
        result = []
        for c in range(5):
            other_half = jnp.where(wall, mirrored[c], lane_partner(frame, half[c], False))
            other_state = lane_partner(frame, state[t][c], 1 <= c <= 3)
            result.append(
                0.5 * (half[c] + other_half) - direction * (other_state - state[t][c])
            )
        lane_flux.append(result)
    row_sign = frame.sign_rows()
    for c in range(5):
        dx = frame.deriv_x([volume[t][0][c] for t in range(2)])
        spread = frame.spread_z(flux_z[c])
        side = face_sign * flux_x[c]
        zero = jnp.zeros_like(side)
        for t in range(2):
            total = (
                dx[t]
                + frame.deriv_rows(volume[t][1][c])
                + frame.deriv_lanes(volume[t][2][c])
                + sign_y * lane_flux[t][c]
                + row_sign * spread[t]
                + (jnp.where(frame.low_half, side, zero) if t == 0 else jnp.where(frame.low_half, zero, side))
            )
            out[c, 8 * t : 8 * t + 8, :] = -total * inverse[t]


def call(kernel, outs, *args):
    return pl.pallas_call(
        kernel,
        out_shape=[jax.ShapeDtypeStruct(s, jnp.float32) for s in outs],
        in_specs=[whole] * len(args),
        out_specs=[whole] * len(outs),
        compiler_params=pltpu.CompilerParams(vmem_limit_bytes=vmem_bytes),
    )(*args)


def exchange(low, up, axis):
    count = lax.axis_size(axis)
    from_left = lax.ppermute(up, axis, [(i, (i + 1) % count) for i in range(count)])
    from_right = lax.ppermute(low, axis, [((i + 1) % count, i) for i in range(count)])
    return from_left, from_right


def local(conserved, jacobian, metric, x_master, x_flip, z_master, z_flip):
    lanes = conserved.shape[-1]
    nodes = conserved.shape[1] * conserved.shape[2]
    assert conserved.shape[1:3] == (4, 4)
    cons = conserved.reshape(5, nodes, lanes)
    jac = jacobian.reshape(nodes, lanes)
    met = metric.reshape(9, nodes, lanes)
    xm, xf, zm, zf = [a.reshape(2, a.shape[-1]) for a in (x_master, x_flip, z_master, z_flip)]
    grad, turned, low_z, up_z = call(
        first_kernel,
        [(9, nodes, lanes), (72, lanes), (96, lanes), (96, lanes)],
        cons, jac, met, xm, xf,
    )
    left_z, right_z = exchange(low_z, up_z, "gz")
    grad, low_x, up_x = call(
        second_kernel,
        [(9, nodes, lanes), (88, lanes), (88, lanes)],
        cons, met, zm, zf, xf, grad, turned, left_z, right_z,
    )
    left_x, right_x = exchange(low_x, up_x, "gx")
    (rhs,) = call(
        third_kernel,
        [(5, nodes, lanes)],
        cons, jac, met, xm, zm, zf, grad, left_z, right_z, left_x, right_x,
    )
    return rhs.reshape(conserved.shape)


def solution(mesh):
    in_specs = (
        P(None, "gx", "gz", None),
        P("gx", "gz", None),
        P(None, None, "gx", "gz", None),
        P("gx", "gz", None),
        P("gx", "gz", None),
        P("gx", "gz", None),
        P("gx", "gz", None),
    )
    out_specs = P(None, "gx", "gz", None)
    return jax.shard_map(local, mesh=mesh, in_specs=in_specs, out_specs=out_specs, check_vma=False)
```

```python
import math

import jax
import jax.numpy as jnp
import numpy as np
from jax import lax
from jax.experimental import pallas as pl
from jax.experimental.pallas import tpu as pltpu
from jax.sharding import PartitionSpec as P

gamma_gas = 1.4
visc_coef = 0.1
prandtl = 0.72
lift = 6.0
heat_coef = visc_coef * gamma_gas / ((gamma_gas - 1.0) * prandtl)
vmem_bytes = 8 << 20
whole = pl.BlockSpec(memory_space=pltpu.VMEM)


def node_table():
    points = np.array([-1.0, -math.sqrt(0.2), math.sqrt(0.2), 1.0])
    scales = np.array([np.prod([points[i] - points[k] for k in range(4) if k != i]) for i in range(4)])
    table = np.zeros((4, 4))
    for i in range(4):
        for k in range(4):
            if i != k:
                table[i, k] = scales[i] / (scales[k] * (points[i] - points[k]))
        table[i, i] = -np.sum(table[i])
    return table


def weak_table():
    table = node_table()
    table[0, 0] += lift
    table[3, 3] -= lift
    return table


def rows_of(lanes):
    return lax.broadcasted_iota(jnp.int32, (8, lanes), 0)


def lanes_of(lanes):
    return lax.broadcasted_iota(jnp.int32, (8, lanes), 1)


def pick4(index, values):
    out = jnp.full(index.shape, values[3], jnp.float32)
    for k in (2, 1, 0):
        out = jnp.where(index == k, jnp.float32(values[k]), out)
    return out


def shift_weights(index, table):
    weights = {}
    for shift in range(-3, 4):
        weights[shift] = pick4(index, [table[j, j - shift] if 0 <= j - shift < 4 else 0.0 for j in range(4)])
    return weights


class Frame:
    def __init__(self, lanes):
        self.lanes = lanes
        row = rows_of(lanes)
        lane = lanes_of(lanes)
        self.row, self.lane = row, lane
        self.low_half = row < 4
        self.point_row = row % 4
        self.point_lane = lane % 4

    def deriv_weights(self):
        table = weak_table()
        self.weights_z = shift_weights(self.point_row, table)
        self.weights_y = shift_weights(self.point_lane, table)
        pair = lambda top, bottom: jnp.where(self.low_half, jnp.float32(top), jnp.float32(bottom))
        self.weights_x = [
            [
                pair(table[2 * t, 2 * s], table[2 * t + 1, 2 * s + 1]),
                pair(table[2 * t, 2 * s + 1], table[2 * t + 1, 2 * s]),
            ]
            for t in range(2)
            for s in range(2)
        ]

    def swap(self, tile):
        return pltpu.roll(tile, 4, 0)

    def deriv_x(self, pair):
        a, b = pair
        a2, b2 = self.swap(a), self.swap(b)
        w = self.weights_x
        return [
            w[2 * t][0] * a + w[2 * t][1] * a2 + w[2 * t + 1][0] * b + w[2 * t + 1][1] * b2
            for t in range(2)
        ]

    def deriv_rows(self, tile):
        out = self.weights_z[0] * tile
        for shift in (-3, -2, -1, 1, 2, 3):
            out = out + self.weights_z[shift] * pltpu.roll(tile, shift % 8, 0)
        return out

    def deriv_lanes(self, tile):
        out = self.weights_y[0] * tile
        for shift in (-3, -2, -1, 1, 2, 3):
            out = out + self.weights_y[shift] * pltpu.roll(tile, shift % self.lanes, 1)
        return out

    def face_x(self, pair):
        return jnp.where(self.low_half, pair[0], pair[1])

    def face_z(self, pair):
        side = jnp.where(self.low_half, 0, 3)
        index = side + 4 * (self.point_row % 2)
        return jnp.where(self.point_row < 2, sub_gather(pair[0], index), sub_gather(pair[1], index))

    def spread_z(self, face):
        upper = jnp.where(self.point_row == 3, 4, 0)
        inner = jnp.where(self.low_half, 0, 1)
        return [sub_gather(face, upper + inner + 2 * t) for t in range(2)]

    def sides(self, low, up):
        return jnp.where(self.low_half, jnp.float32(low), jnp.float32(up))

    def sign_lanes(self):
        return jnp.where(
            self.point_lane == 3, jnp.float32(lift), jnp.where(self.point_lane == 0, jnp.float32(-lift), 0.0)
        )

    def sign_rows(self):
        return jnp.where(
            self.point_row == 3, jnp.float32(lift), jnp.where(self.point_row == 0, jnp.float32(-lift), 0.0)
        )


def sub_gather(tile, index):
    return jnp.take_along_axis(tile, index, axis=0)


def lane_gather(tile, index):
    return jnp.take_along_axis(tile, index, axis=1)


def primitive(state):
    inverse = 1.0 / state[0]
    velocity = [state[1 + j] * inverse for j in range(3)]
    kinetic = state[1] * velocity[0] + state[2] * velocity[1] + state[3] * velocity[2]
    pressure = (gamma_gas - 1.0) * (state[4] - 0.5 * kinetic)
    return velocity, pressure, pressure * inverse


def combos(values, rows):
    w0, w1, w2, w3 = values
    m0, m1, m2 = rows
    return [
        w0 * m0,
        w1 * m1,
        w2 * m2,
        w0 * m1 + w1 * m0,
        w0 * m2 + w2 * m0,
        w1 * m2 + w2 * m1,
        w3 * m0,
        w3 * m1,
        w3 * m2,
    ]


def plain_flux(state, velocity, pressure, normal):
    speed = velocity[0] * normal[0] + velocity[1] * normal[1] + velocity[2] * normal[2]
    out = [state[0] * speed]
    for j in range(3):
        out.append(state[1 + j] * speed + pressure * normal[j])
    out.append((state[4] + pressure) * speed)
    return out, speed


def drag_flux(velocity, slopes, normal):
    m0, m1, m2 = normal
    spread = (visc_coef * 2.0 / 3.0) * (slopes[0] + slopes[1] + slopes[2])
    t00, t11, t22 = [2.0 * visc_coef * slopes[d] - spread for d in range(3)]
    t01, t02, t12 = [visc_coef * slopes[3 + d] for d in range(3)]
    stress = [
        t00 * m0 + t01 * m1 + t02 * m2,
        t01 * m0 + t11 * m1 + t12 * m2,
        t02 * m0 + t12 * m1 + t22 * m2,
    ]
    heat = heat_coef * (slopes[6] * m0 + slopes[7] * m1 + slopes[8] * m2)
    work = velocity[0] * stress[0] + velocity[1] * stress[1] + velocity[2] * stress[2]
    return stress + [work + heat], heat


def wave(speed, theta, normal_size):
    return jnp.abs(speed) + jnp.sqrt(gamma_gas * theta) * normal_size


def size_of(normal):
    return jnp.sqrt(normal[0] * normal[0] + normal[1] * normal[1] + normal[2] * normal[2])


def pack(frame, fields, low_ref, up_ref):
    fields = list(fields)
    if len(fields) % 2:
        fields.append(fields[-1])
    for g in range(len(fields) // 2):
        a, b = fields[2 * g], fields[2 * g + 1]
        low_ref[8 * g : 8 * g + 8, :] = jnp.where(frame.low_half, a, frame.swap(b))
        up_ref[8 * g : 8 * g + 8, :] = jnp.where(frame.low_half, frame.swap(a), b)


def unpack(frame, left_ref, right_ref, count):
    fields = []
    for g in range((count + 1) // 2):
        left = left_ref[8 * g : 8 * g + 8, :]
        right = right_ref[8 * g : 8 * g + 8, :]
        fields.append(jnp.where(frame.low_half, left, frame.swap(right)))
        fields.append(jnp.where(frame.low_half, frame.swap(left), right))
    return fields[:count]


def spread_flags(frame, flags):
    count = flags.shape[-1]
    hit = lax.broadcasted_iota(jnp.int32, (count, frame.lanes), 0) == (
        lax.broadcasted_iota(jnp.int32, (count, frame.lanes), 1) // 4
    )
    wide = jnp.dot(
        flags.astype(jnp.float32), hit.astype(jnp.float32), preferred_element_type=jnp.float32
    )
    wide = (wide + 0.5).astype(jnp.int32)
    shape = (8, frame.lanes)
    return jnp.where(
        frame.low_half, jnp.broadcast_to(wide[0:1], shape), jnp.broadcast_to(wide[1:2], shape)
    )


def turn_indices(frame, code, forward_low):
    swap = (code & 4) != 0
    first = (code & 1) * 3
    second = ((code >> 1) & 1) * 3
    forward = frame.low_half if forward_low else jnp.logical_not(frame.low_half)
    flip_a = jnp.where(forward, second, first)
    flip_b = jnp.where(forward, first, second)
    row4, lane4 = frame.point_row, frame.point_lane
    lane_base = frame.lane - lane4
    row_base = frame.row - row4
    step1 = lane_base + jnp.where(swap, (lane4 - row4) & 3, lane4)
    step2 = row_base + jnp.where(swap, (lane4 - (row4 ^ flip_b)) & 3, row4 ^ first)
    step3 = lane_base + jnp.where(swap, ((lane4 ^ flip_a) + (row4 ^ flip_b)) & 3, lane4 ^ second)
    return step1, step2, step3


def turn(tile, indices):
    return lane_gather(sub_gather(lane_gather(tile, indices[0]), indices[1]), indices[2])


def load_pair(ref, f):
    return [ref[f, 0:8, :], ref[f, 8:16, :]]


def load_state(ref):
    pairs = [load_pair(ref, f) for f in range(5)]
    return [[pairs[f][t] for f in range(5)] for t in range(2)]


def load_rows(ref, g):
    pairs = [load_pair(ref, 3 * g + d) for d in range(3)]
    return [[pairs[d][t] for d in range(3)] for t in range(2)]


def by_field(tiles):
    return [[tiles[0][f], tiles[1][f]] for f in range(len(tiles[0]))]


def lane_partner(frame, tile, flip):
    before = pltpu.roll(tile, 1, 1)
    after = pltpu.roll(tile, frame.lanes - 1, 1)
    other = jnp.where(frame.point_lane == 3, after, before)
    wall = (frame.lane == 0) | (frame.lane == frame.lanes - 1)
    return jnp.where(wall, -tile if flip else tile, other)


def lane_normal(frame, rows):
    take_before = (frame.point_lane == 0) & (frame.lane != 0)
    return [jnp.where(take_before, pltpu.roll(r, 1, 1), r) for r in rows]


def first_kernel(
    cons_in, jac_in, met_in, xm_in, xf_in, zm_in, zf_in,
    cons, jac, met, zm_out, zf_out, index_out, grad_out, turned_out, low_out, up_out,
    xm_ref, xf_ref, sems,
):
    copies = [
        pltpu.make_async_copy(a, b, sems.at[i])
        for i, (a, b) in enumerate(
            [
                (met_in, met),
                (cons_in, cons),
                (jac_in, jac),
                (xf_in, xf_ref),
                (xm_in, xm_ref),
                (zf_in, zf_out),
                (zm_in, zm_out),
            ]
        )
    ]
    for c in copies:
        c.start()
    frame = Frame(cons.shape[-1])
    frame.deriv_weights()
    for c in copies[::-1]:
        c.wait()
    state = load_state(cons)
    rows = [load_rows(met, g) for g in range(3)]
    lifted = []
    for t in range(2):
        velocity, _, theta = primitive(state[t])
        lifted.append(velocity + [theta])
    cx = by_field([combos(lifted[t], rows[0][t]) for t in range(2)])
    cz = by_field([combos(lifted[t], rows[1][t]) for t in range(2)])
    cy = by_field([combos(lifted[t], rows[2][t]) for t in range(2)])
    sign = frame.sign_lanes()
    lane_part = []
    for t in range(2):
        other = [lane_partner(frame, lifted[t][k], k < 3) for k in range(4)]
        mean = [0.5 * (lifted[t][k] + other[k]) for k in range(4)]
        lane_part.append(combos(mean, lane_normal(frame, rows[2][t])))
    grad = []
    for f in range(9):
        dx = frame.deriv_x(cx[f])
        grad.append(
            [
                dx[t]
                + frame.deriv_rows(cz[f][t])
                + frame.deriv_lanes(cy[f][t])
                + sign * lane_part[t][f]
                for t in range(2)
            ]
        )
    for f in range(9):
        for t in range(2):
            grad_out[f, 8 * t : 8 * t + 8, :] = grad[f][t]

    inverse = [1.0 / jac[0:8, :], 1.0 / jac[8:16, :]]
    state_f = by_field(state)
    code = spread_flags(frame, xf_ref[...])
    master = spread_flags(frame, xm_ref[...])
    lead = master == 1
    indices = turn_indices(frame, code, True)
    for k in range(3):
        index_out[8 * k : 8 * k + 8, :] = indices[k]
    index_out[24:32, :] = master
    own_x = [frame.face_x(p) for p in state_f + by_field(rows[0])]
    turned = [turn(p, indices) for p in own_x + [frame.face_x(inverse)]]
    for f in range(9):
        turned_out[8 * f : 8 * f + 8, :] = turned[f]
    velocity, _, theta = primitive(turned[:5])
    line = velocity + [theta]
    outer = (frame.point_row == 0) | (frame.point_row == 3)
    pick = jnp.where(frame.low_half, 0, 3) + jnp.where(frame.point_row >= 2, 4, 0)
    merge = lambda a, b: jnp.where(outer, sub_gather(a, pick), sub_gather(b, pick))
    zero = jnp.zeros_like(line[0])
    edges = [merge(line[0], line[1]), merge(line[2], line[3])]
    for d in range(3):
        edges.append(
            merge(jnp.where(lead, turned[5 + d], zero), jnp.where(lead, own_x[5 + d], zero))
        )
    faces = [frame.face_z(p) for p in state_f + by_field(rows[1]) + [inverse] + grad]
    pack(frame, faces + edges, low_out, up_out)


def first_cover(cons, met, zm_ref, zf_ref, index_out, part_out):
    frame = Frame(cons.shape[-1])
    frame.deriv_weights()
    indices = turn_indices(frame, spread_flags(frame, zf_ref[...]), False)
    for k in range(3):
        index_out[8 * k : 8 * k + 8, :] = indices[k]
    index_out[24:32, :] = spread_flags(frame, zm_ref[...])
    state = load_state(cons)
    rows = [load_rows(met, g) for g in range(3)]
    sign_y = frame.sign_lanes()
    up_lane = frame.point_lane == 3
    wall = (frame.lane == 0) | (frame.lane == frame.lanes - 1)
    volume = []
    lane_flux = []
    for t in range(2):
        velocity, pressure, theta = primitive(state[t])
        volume.append([plain_flux(state[t], velocity, pressure, rows[g][t])[0] for g in range(3)])
        normal = lane_normal(frame, rows[2][t])
        half, speed = plain_flux(state[t], velocity, pressure, normal)
        own_wave = wave(speed, theta, size_of(normal))
        fastest = jnp.maximum(own_wave, lane_partner(frame, own_wave, False))
        mirrored = [-half[0], half[1], half[2], half[3], -half[4]]
        direction = jnp.where(up_lane, jnp.float32(0.5), jnp.float32(-0.5)) * fastest
        result = []
        for c in range(5):
            other_half = jnp.where(wall, mirrored[c], lane_partner(frame, half[c], False))
            other_state = lane_partner(frame, state[t][c], 1 <= c <= 3)
            result.append(0.5 * (half[c] + other_half) - direction * (other_state - state[t][c]))
        lane_flux.append(result)
    for c in range(5):
        dx = frame.deriv_x([volume[t][0][c] for t in range(2)])
        for t in range(2):
            part_out[c, 8 * t : 8 * t + 8, :] = (
                dx[t]
                + frame.deriv_rows(volume[t][1][c])
                + frame.deriv_lanes(volume[t][2][c])
                + sign_y * lane_flux[t][c]
            )


def load_indices(ref):
    return [ref[8 * k : 8 * k + 8, :] for k in range(3)]


def mean_of(prim1, prim2):
    return [0.5 * (a + b) for a, b in zip(prim1[0] + [prim1[2]], prim2[0] + [prim2[2]])]


def first_of_pair(frame):
    return jnp.full((8, frame.lanes), lax.axis_index("gx") % 2) == 0


def second_kernel(
    cons, met, x_index, z_index, grad_in, turned_in, left, right, grad_out, part_out, near_out, far_out
):
    frame = Frame(cons.shape[-1])
    lead = z_index[24:32, :] == 1
    indices = load_indices(z_index)
    x_indices = load_indices(x_index)
    got = unpack(frame, left, right, 23)
    other = [turn(p, indices) for p in got[:8]]
    own = [frame.face_z(load_pair(cons, f)) for f in range(5)]
    own_rows = [frame.face_z(load_pair(met, 3 + d)) for d in range(3)]
    normal = [jnp.where(lead, own_rows[d], other[5 + d]) for d in range(3)]
    part = combos(mean_of(primitive(own), primitive(other[:5])), normal)
    sign = frame.sign_rows()
    faces = []
    for f in range(9):
        spread = frame.spread_z(part[f])
        total = [grad_in[f, 8 * t : 8 * t + 8, :] + sign * spread[t] for t in range(2)]
        for t in range(2):
            grad_out[f, 8 * t : 8 * t + 8, :] = total[t]
        faces.append(turn(frame.face_x(total), x_indices))
        part_out[8 * f : 8 * f + 8, :] = part[f]
    turned = [turned_in[8 * f : 8 * f + 8, :] for f in range(9)]
    odd = frame.point_row % 2
    high = jnp.where(frame.point_row >= 2, 4, 0)
    both = high + jnp.where(frame.low_half, odd, 3 - odd)
    outer = high + jnp.where(frame.low_half, 0, 3)
    lines = [sub_gather(got[18], both), sub_gather(got[19], both)]
    lines.append(jnp.where(odd == 0, sub_gather(got[20], outer), sub_gather(got[21], outer)))
    lines.append(sub_gather(got[22], outer))
    lower = first_of_pair(frame)
    fields = turned + faces + lines
    for g in range(len(fields) // 2):
        a, b = fields[2 * g], fields[2 * g + 1]
        low = jnp.where(frame.low_half, a, frame.swap(b))
        up = jnp.where(frame.low_half, frame.swap(a), b)
        near_out[8 * g : 8 * g + 8, :] = jnp.where(lower, up, low)
        far_out[8 * g : 8 * g + 8, :] = jnp.where(lower, low, up)


def plain_face(own, own_prim, other, other_prim, normal, side_sign):
    size = size_of(normal)
    flux1, speed1 = plain_flux(own, own_prim[0], own_prim[1], normal)
    flux2, speed2 = plain_flux(other, other_prim[0], other_prim[1], normal)
    fastest = jnp.maximum(wave(speed1, own_prim[2], size), wave(speed2, other_prim[2], size))
    half = 0.5 * side_sign * fastest
    return [0.5 * (flux1[c] + flux2[c]) - half * (other[c] - own[c]) for c in range(5)]


def second_cover(cons, met, z_index, part_in, left, right, part_out, face_out):
    frame = Frame(cons.shape[-1])
    lead = z_index[24:32, :] == 1
    indices = load_indices(z_index)
    got = unpack(frame, left, right, 9)
    turned = [turn(p, indices) for p in got]
    other = turned[:5]
    other_prim = primitive(other)
    own = [frame.face_z(load_pair(cons, f)) for f in range(5)]
    own_rows = [frame.face_z(load_pair(met, 3 + d)) for d in range(3)]
    own_prim = primitive(own)
    normal = [jnp.where(lead, own_rows[d], turned[5 + d]) for d in range(3)]
    flux = plain_face(own, own_prim, other, other_prim, normal, frame.sides(-1.0, 1.0))
    sign = frame.sign_rows()
    for c in range(5):
        spread = frame.spread_z(flux[c])
        for t in range(2):
            part_out[c, 8 * t : 8 * t + 8, :] = part_in[c, 8 * t : 8 * t + 8, :] + sign * spread[t]
    for i, tile in enumerate(own_prim[0] + other_prim[0] + normal + [turned[8]]):
        face_out[8 * i : 8 * i + 8, :] = tile


def third_kernel(
    cons, jac, met, x_index, z_index, grad_in, lift_in, part_in, face_in,
    left_z, right_z, near_x, far_x, out,
):
    frame = Frame(cons.shape[-1])
    frame.deriv_weights()
    state = load_state(cons)
    state_f = by_field(state)
    rows = [load_rows(met, g) for g in range(3)]
    inverse = [1.0 / jac[0:8, :], 1.0 / jac[8:16, :]]
    got_z = unpack(frame, left_z, right_z, 23)
    lower = first_of_pair(frame)
    got_x = []
    for g in range(11):
        near = near_x[8 * g : 8 * g + 8, :]
        far = far_x[8 * g : 8 * g + 8, :]
        left = jnp.where(lower, far, near)
        right = jnp.where(lower, near, far)
        got_x.append(jnp.where(frame.low_half, left, frame.swap(right)))
        got_x.append(jnp.where(frame.low_half, frame.swap(left), right))
    x_lead = x_index[24:32, :] == 1
    z_indices = load_indices(z_index)
    face_sign = frame.sides(-lift, lift)

    own = [frame.face_x(p) for p in state_f]
    own_rows = [frame.face_x(p) for p in by_field(rows[0])]
    own_prim = primitive(own)
    other = got_x[:5]
    other_prim = primitive(other)
    normal_x = [jnp.where(x_lead, own_rows[d], got_x[5 + d]) for d in range(3)]
    part = combos(mean_of(own_prim, other_prim), normal_x)
    slopes = []
    for f in range(9):
        lifted_part = face_sign * part[f]
        zero = jnp.zeros_like(lifted_part)
        tiles = [
            grad_in[f, 0:8, :] + jnp.where(frame.low_half, lifted_part, zero),
            grad_in[f, 8:16, :] + jnp.where(frame.low_half, zero, lifted_part),
        ]
        slopes.append([tiles[t] * inverse[t] for t in range(2)])
    own_slopes = [frame.face_x(p) for p in slopes]
    other_slopes = [(got_x[9 + f] - face_sign * part[f]) * got_x[8] for f in range(9)]
    flux_x = plain_face(own, own_prim, other, other_prim, normal_x, frame.sides(-1.0, 1.0))
    drag1 = drag_flux(own_prim[0], own_slopes, normal_x)[0]
    drag2 = drag_flux(other_prim[0], other_slopes, normal_x)[0]
    flux_x = [flux_x[0]] + [flux_x[1 + c] - 0.5 * (drag1[c] + drag2[c]) for c in range(4)]

    edge_a = jnp.where(frame.low_half, 0, 2) + jnp.where(frame.point_row >= 2, 4, 0)
    edge_b = edge_a + 1
    lines = [
        sub_gather(got_x[18], edge_a),
        sub_gather(got_x[18], edge_b),
        sub_gather(got_x[19], edge_a),
        sub_gather(got_x[19], edge_b),
    ]
    line_rows = [
        sub_gather(got_x[20], edge_a),
        sub_gather(got_x[20], edge_b),
        sub_gather(got_x[21], edge_a),
    ]
    own_edge = jnp.where(frame.low_half, 0, 4) + jnp.where(frame.point_row >= 2, 2, 1)
    line_rows = [line_rows[d] + sub_gather(got_z[20 + d], own_edge) for d in range(3)]
    raw_prim = primitive(got_z[:5])
    edge_mean = [0.5 * (a + b) for a, b in zip(raw_prim[0] + [raw_prim[2]], lines)]
    edge_part = combos(edge_mean, line_rows)
    edge_sign = frame.sign_rows()
    other_grad = [turn(got_z[9 + f] + edge_sign * edge_part[f], z_indices) for f in range(9)]
    face = [face_in[8 * i : 8 * i + 8, :] for i in range(10)]
    normal_z = face[6:9]
    other_slopes = [
        (other_grad[f] - face_sign * lift_in[8 * f : 8 * f + 8, :]) * face[9] for f in range(9)
    ]
    own_slopes = [frame.face_z(p) for p in slopes]
    drag1 = drag_flux(face[0:3], own_slopes, normal_z)[0]
    drag2 = drag_flux(face[3:6], other_slopes, normal_z)[0]
    drag_z = [0.5 * (drag1[c] + drag2[c]) for c in range(4)]

    slopes_t = [[slopes[f][t] for f in range(9)] for t in range(2)]
    sign_y = frame.sign_lanes()
    wall = (frame.lane == 0) | (frame.lane == frame.lanes - 1)
    volume = []
    lane_flux = []
    for t in range(2):
        velocity = primitive(state[t])[0]
        volume.append([drag_flux(velocity, slopes_t[t], rows[g][t])[0] for g in range(3)])
        normal = lane_normal(frame, rows[2][t])
        half, heat = drag_flux(velocity, slopes_t[t], normal)
        mirrored = [half[0], half[1], half[2], 2.0 * heat - half[3]]
        result = []
        for c in range(4):
            other_half = jnp.where(wall, mirrored[c], lane_partner(frame, half[c], False))
            result.append(0.5 * (half[c] + other_half))
        lane_flux.append(result)
    row_sign = frame.sign_rows()
    for c in range(5):
        side = face_sign * flux_x[c]
        zero = jnp.zeros_like(side)
        sides = [jnp.where(frame.low_half, side, zero), jnp.where(frame.low_half, zero, side)]
        totals = [part_in[c, 8 * t : 8 * t + 8, :] + sides[t] for t in range(2)]
        if c > 0:
            k = c - 1
            dx = frame.deriv_x([volume[t][0][k] for t in range(2)])
            spread = frame.spread_z(drag_z[k])
            for t in range(2):
                totals[t] = totals[t] - (
                    dx[t]
                    + frame.deriv_rows(volume[t][1][k])
                    + frame.deriv_lanes(volume[t][2][k])
                    + sign_y * lane_flux[t][k]
                    + row_sign * spread[t]
                )
        for t in range(2):
            out[c, 8 * t : 8 * t + 8, :] = -totals[t] * inverse[t]


def shaped(*shape, dtype=jnp.float32):
    return jax.ShapeDtypeStruct(shape, dtype)


def call(kernel, outs, *args, in_specs=None, scratch=(), flops=0):
    return pl.pallas_call(
        kernel,
        out_shape=outs,
        in_specs=in_specs or [whole] * len(args),
        out_specs=[whole] * len(outs),
        scratch_shapes=scratch,
        compiler_params=pltpu.CompilerParams(vmem_limit_bytes=vmem_bytes),
        cost_estimate=pl.CostEstimate(flops=flops, bytes_accessed=200_000, transcendentals=0),
    )(*args)


def exchange(low, up, axis):
    count = lax.axis_size(axis)
    from_left = lax.ppermute(up, axis, [(i, (i + 1) % count) for i in range(count)])
    from_right = lax.ppermute(low, axis, [((i + 1) % count, i) for i in range(count)])
    return from_left, from_right


def exchange_pairs(near, far, axis):
    count = lax.axis_size(axis)
    assert count % 2 == 0
    swaps = [[], []]
    for k in range(count):
        a, b = k, (k + 1) % count
        swaps[k % 2] += [(a, b), (b, a)]
    got_far = lax.ppermute(far, axis, swaps[1])
    got_near = lax.ppermute(near, axis, swaps[0])
    return got_near, got_far


def local(conserved, jacobian, metric, x_master, x_flip, z_master, z_flip):
    lanes = conserved.shape[-1]
    nodes = conserved.shape[1] * conserved.shape[2]
    assert conserved.shape[1:3] == (4, 4)
    cons = conserved.reshape(5, nodes, lanes)
    jac = jacobian.reshape(nodes, lanes)
    met = metric.reshape(9, nodes, lanes)
    xm, xf, zm, zf = [a.reshape(2, a.shape[-1]) for a in (x_master, x_flip, z_master, z_flip)]
    flag = (2, xm.shape[-1])
    cons, jac, met, zm, zf, x_index, grad, turned, low_z, up_z = call(
        first_kernel,
        [
            shaped(5, nodes, lanes),
            shaped(nodes, lanes),
            shaped(9, nodes, lanes),
            shaped(*flag, dtype=jnp.int32),
            shaped(*flag, dtype=jnp.int32),
            shaped(32, lanes, dtype=jnp.int32),
            shaped(9, nodes, lanes),
            shaped(72, lanes),
            shaped(96, lanes),
            shaped(96, lanes),
        ],
        *[pltpu.with_memory_space_constraint(a, pltpu.HBM) for a in (cons, jac, met, xm, xf, zm, zf)],
        in_specs=[pl.BlockSpec(memory_space=pltpu.HBM)] * 7,
        scratch=[
            pltpu.VMEM(flag, jnp.int32),
            pltpu.VMEM(flag, jnp.int32),
            pltpu.SemaphoreType.DMA((7,)),
        ],
        flops=1_000_000,
    )
    left_z, right_z = exchange(low_z, up_z, "gz")
    z_index, part = call(
        first_cover,
        [shaped(32, lanes, dtype=jnp.int32), shaped(5, nodes, lanes)],
        cons, met, zm, zf,
        flops=1_000_000,
    )
    grad, lift_z, near_x, far_x = call(
        second_kernel,
        [shaped(9, nodes, lanes), shaped(72, lanes), shaped(88, lanes), shaped(88, lanes)],
        cons, met, x_index, z_index, grad, turned, left_z, right_z,
        flops=1_000_000,
    )
    near_x, far_x = exchange_pairs(near_x, far_x, "gx")
    part, face = call(
        second_cover,
        [shaped(5, nodes, lanes), shaped(80, lanes)],
        cons, met, z_index, part, left_z, right_z,
        flops=1_000_000,
    )
    (rhs,) = call(
        third_kernel,
        [shaped(5, nodes, lanes)],
        cons, jac, met, x_index, z_index, grad, lift_z, part, face, left_z, right_z, near_x, far_x,
        flops=1_000_000,
    )
    return rhs.reshape(conserved.shape)


def solution(mesh):
    in_specs = (
        P(None, "gx", "gz", None),
        P("gx", "gz", None),
        P(None, None, "gx", "gz", None),
        P("gx", "gz", None),
        P("gx", "gz", None),
        P("gx", "gz", None),
        P("gx", "gz", None),
    )
    out_specs = P(None, "gx", "gz", None)
    return jax.shard_map(local, mesh=mesh, in_specs=in_specs, out_specs=out_specs, check_vma=False)
```

```python
import math

import jax
import jax.numpy as jnp
import numpy as np
from jax import lax
from jax.experimental import pallas as pl
from jax.experimental.pallas import tpu as pltpu
from jax.sharding import PartitionSpec as P


gamma_gas = 1.4
visc_coef = 0.1
prandtl = 0.72
lift = 6.0
heat_coef = visc_coef * gamma_gas / ((gamma_gas - 1.0) * prandtl)
vmem_bytes = 8 << 20
whole = pl.BlockSpec(memory_space=pltpu.VMEM)


def node_table():
    points = np.array([-1.0, -math.sqrt(0.2), math.sqrt(0.2), 1.0])
    scales = np.array([np.prod([points[i] - points[k] for k in range(4) if k != i]) for i in range(4)])
    table = np.zeros((4, 4))
    for i in range(4):
        for k in range(4):
            if i != k:
                table[i, k] = scales[i] / (scales[k] * (points[i] - points[k]))
        table[i, i] = -np.sum(table[i])
    return table


def weak_table():
    table = node_table()
    table[0, 0] += lift
    table[3, 3] -= lift
    return table


def rows_of(lanes):
    return lax.broadcasted_iota(jnp.int32, (8, lanes), 0)


def lanes_of(lanes):
    return lax.broadcasted_iota(jnp.int32, (8, lanes), 1)


def pick4(index, values):
    out = jnp.full(index.shape, values[3], jnp.float32)
    for k in (2, 1, 0):
        out = jnp.where(index == k, jnp.float32(values[k]), out)
    return out


def shift_weights(index, table):
    weights = {}
    for shift in range(-3, 4):
        weights[shift] = pick4(index, [table[j, j - shift] if 0 <= j - shift < 4 else 0.0 for j in range(4)])
    return weights


class Frame:
    def __init__(self, lanes):
        self.lanes = lanes
        row = rows_of(lanes)
        lane = lanes_of(lanes)
        self.row, self.lane = row, lane
        self.low_half = row < 4
        self.point_row = row % 4
        self.point_lane = lane % 4

    def deriv_weights(self):
        table = weak_table()
        self.weights_z = shift_weights(self.point_row, table)
        self.weights_y = shift_weights(self.point_lane, table)
        pair = lambda top, bottom: jnp.where(self.low_half, jnp.float32(top), jnp.float32(bottom))
        self.weights_x = [
            [
                pair(table[2 * t, 2 * s], table[2 * t + 1, 2 * s + 1]),
                pair(table[2 * t, 2 * s + 1], table[2 * t + 1, 2 * s]),
            ]
            for t in range(2)
            for s in range(2)
        ]

    def swap(self, tile):
        return pltpu.roll(tile, 4, 0)

    def deriv_x(self, pair):
        a, b = pair
        a2, b2 = self.swap(a), self.swap(b)
        w = self.weights_x
        return [
            w[2 * t][0] * a + w[2 * t][1] * a2 + w[2 * t + 1][0] * b + w[2 * t + 1][1] * b2
            for t in range(2)
        ]

    def deriv_rows(self, tile):
        out = self.weights_z[0] * tile
        for shift in (-3, -2, -1, 1, 2, 3):
            out = out + self.weights_z[shift] * pltpu.roll(tile, shift % 8, 0)
        return out

    def lane_matrix(self):
        shape = (self.lanes, self.lanes)
        to = lax.broadcasted_iota(jnp.int32, shape, 1)
        gap = to - lax.broadcasted_iota(jnp.int32, shape, 0)
        full = jnp.zeros(shape, jnp.float32)
        for shift in range(-3, 4):
            full = jnp.where(gap == shift, jnp.broadcast_to(self.weights_y[shift][0:1], shape), full)
        high = full.astype(jnp.bfloat16)
        low = (full - high.astype(jnp.float32)).astype(jnp.bfloat16)
        top = jnp.concatenate([high, low], 1)
        bottom = jnp.concatenate([high, jnp.zeros(shape, jnp.bfloat16)], 1)
        return jnp.concatenate([top, bottom], 0)

    def deriv_lanes_all(self, tiles, matrix):
        values = jnp.concatenate(tiles, 0)
        high = values.astype(jnp.bfloat16)
        low = (values - high.astype(jnp.float32)).astype(jnp.bfloat16)
        wide = jnp.dot(
            jnp.concatenate([high, low], 1), matrix, preferred_element_type=jnp.float32
        )
        out = wide[:, : self.lanes] + wide[:, self.lanes :]
        return [out[8 * i : 8 * i + 8] for i in range(len(tiles))]

    def deriv_lanes(self, tile):
        out = self.weights_y[0] * tile
        for shift in (-3, -2, -1, 1, 2, 3):
            out = out + self.weights_y[shift] * pltpu.roll(tile, shift % self.lanes, 1)
        return out

    def face_x(self, pair):
        return jnp.where(self.low_half, pair[0], pair[1])

    def face_z(self, pair, swapped=False):
        side = jnp.where(self.low_half, 3, 0) if swapped else jnp.where(self.low_half, 0, 3)
        index = side + 4 * (self.point_row % 2)
        return jnp.where(self.point_row < 2, sub_gather(pair[0], index), sub_gather(pair[1], index))

    def spread_z(self, face):
        upper = jnp.where(self.point_row == 3, 4, 0)
        inner = jnp.where(self.low_half, 0, 1)
        return [sub_gather(face, upper + inner + 2 * t) for t in range(2)]

    def sides(self, low, up):
        return jnp.where(self.low_half, jnp.float32(low), jnp.float32(up))

    def sign_lanes(self):
        return jnp.where(
            self.point_lane == 3, jnp.float32(lift), jnp.where(self.point_lane == 0, jnp.float32(-lift), 0.0)
        )

    def sign_rows(self):
        return jnp.where(
            self.point_row == 3, jnp.float32(lift), jnp.where(self.point_row == 0, jnp.float32(-lift), 0.0)
        )


def sub_gather(tile, index):
    return jnp.take_along_axis(tile, index, axis=0)


def lane_gather(tile, index):
    return jnp.take_along_axis(tile, index, axis=1)


def primitive(state):
    inverse = 1.0 / state[0]
    velocity = [state[1 + j] * inverse for j in range(3)]
    kinetic = state[1] * velocity[0] + state[2] * velocity[1] + state[3] * velocity[2]
    pressure = (gamma_gas - 1.0) * (state[4] - 0.5 * kinetic)
    return velocity, pressure, pressure * inverse


def combos(values, rows):
    w0, w1, w2, w3 = values
    m0, m1, m2 = rows
    return [
        w0 * m0,
        w1 * m1,
        w2 * m2,
        w0 * m1 + w1 * m0,
        w0 * m2 + w2 * m0,
        w1 * m2 + w2 * m1,
        w3 * m0,
        w3 * m1,
        w3 * m2,
    ]


def plain_flux(state, velocity, pressure, normal):
    speed = velocity[0] * normal[0] + velocity[1] * normal[1] + velocity[2] * normal[2]
    out = [state[0] * speed]
    for j in range(3):
        out.append(state[1 + j] * speed + pressure * normal[j])
    out.append((state[4] + pressure) * speed)
    return out, speed


def drag_flux(velocity, slopes, normal):
    m0, m1, m2 = normal
    spread = (visc_coef * 2.0 / 3.0) * (slopes[0] + slopes[1] + slopes[2])
    t00, t11, t22 = [2.0 * visc_coef * slopes[d] - spread for d in range(3)]
    t01, t02, t12 = [visc_coef * slopes[3 + d] for d in range(3)]
    stress = [
        t00 * m0 + t01 * m1 + t02 * m2,
        t01 * m0 + t11 * m1 + t12 * m2,
        t02 * m0 + t12 * m1 + t22 * m2,
    ]
    heat = heat_coef * (slopes[6] * m0 + slopes[7] * m1 + slopes[8] * m2)
    work = velocity[0] * stress[0] + velocity[1] * stress[1] + velocity[2] * stress[2]
    return stress + [work + heat], heat


def wave(speed, theta, normal_size):
    return jnp.abs(speed) + jnp.sqrt(gamma_gas * theta) * normal_size


def size_of(normal):
    return jnp.sqrt(normal[0] * normal[0] + normal[1] * normal[1] + normal[2] * normal[2])


def paired(frame, swapped_a, b):
    low = jnp.where(frame.low_half, b, swapped_a)
    up = jnp.where(frame.low_half, swapped_a, b)
    return low, up


def pack(frame, fields, low_ref, up_ref):
    fields = list(fields)
    if len(fields) % 2:
        fields.append(fields[-1])
    for g in range(len(fields) // 2):
        low, up = paired(frame, fields[2 * g], fields[2 * g + 1])
        low_ref[8 * g : 8 * g + 8, :] = low
        up_ref[8 * g : 8 * g + 8, :] = up


def unpack(frame, left_ref, right_ref, count):
    fields = []
    for g in range((count + 1) // 2):
        left = left_ref[8 * g : 8 * g + 8, :]
        right = right_ref[8 * g : 8 * g + 8, :]
        fields.append(jnp.where(frame.low_half, left, right))
        fields.append(jnp.where(frame.low_half, right, left))
    return fields[:count]


def first_of_pair(frame):
    return jnp.full((8, frame.lanes), lax.axis_index("gx") % 2) == 0


def pack_pairs(frame, fields, near_ref, far_ref):
    lower = first_of_pair(frame)
    fields = fields + [fields[-1]] * (len(fields) % 2)
    for g in range(len(fields) // 2):
        low, up = paired(frame, fields[2 * g], fields[2 * g + 1])
        near_ref[8 * g : 8 * g + 8, :] = jnp.where(lower, up, low)
        far_ref[8 * g : 8 * g + 8, :] = jnp.where(lower, low, up)


def unpack_pairs(frame, near_ref, far_ref, count):
    straight = first_of_pair(frame) == frame.low_half
    fields = []
    for g in range((count + 1) // 2):
        near = near_ref[8 * g : 8 * g + 8, :]
        far = far_ref[8 * g : 8 * g + 8, :]
        fields.append(jnp.where(straight, far, near))
        fields.append(jnp.where(straight, near, far))
    return fields[:count]


def spread_flags(frame, flags):
    count = flags.shape[-1]
    hit = lax.broadcasted_iota(jnp.int32, (count, frame.lanes), 0) == (
        lax.broadcasted_iota(jnp.int32, (count, frame.lanes), 1) // 4
    )
    wide = jnp.dot(
        flags.astype(jnp.float32), hit.astype(jnp.float32), preferred_element_type=jnp.float32
    )
    wide = (wide + 0.5).astype(jnp.int32)
    shape = (8, frame.lanes)
    return jnp.where(
        frame.low_half, jnp.broadcast_to(wide[0:1], shape), jnp.broadcast_to(wide[1:2], shape)
    )


def turn_indices(frame, code, forward_low):
    swap = (code & 4) != 0
    first = (code & 1) * 3
    second = ((code >> 1) & 1) * 3
    forward = frame.low_half if forward_low else jnp.logical_not(frame.low_half)
    flip_a = jnp.where(forward, second, first)
    flip_b = jnp.where(forward, first, second)
    row4, lane4 = frame.point_row, frame.point_lane
    lane_base = frame.lane - lane4
    row_base = frame.row - row4
    step1 = lane_base + jnp.where(swap, (lane4 - row4) & 3, lane4)
    step2 = row_base + jnp.where(swap, (lane4 - (row4 ^ flip_b)) & 3, row4 ^ first)
    step3 = lane_base + jnp.where(swap, ((lane4 ^ flip_a) + (row4 ^ flip_b)) & 3, lane4 ^ second)
    return step1, step2, step3


def turn(tile, indices):
    return lane_gather(sub_gather(lane_gather(tile, indices[0]), indices[1]), indices[2])


def store_indices(frame, ref, indices, master):
    step1, step2, step3 = indices
    stack_tiles(ref, [step1, step2, step3, frame.swap(step1), step2 ^ 4, master])


def load_indices(ref):
    step1, step2, step3, swapped1, swapped2, _ = take_tiles(ref, 0, 6)
    return (step1, step2, step3), (swapped1, swapped2, step3)


def turn_all(fields, both, first=0):
    return [turn(p, both[(first + i) % 2]) for i, p in enumerate(fields)]


def straight(frame, fields):
    return [frame.swap(p) if i % 2 else p for i, p in enumerate(fields)]


def stack_tiles(ref, tiles):
    for i, tile in enumerate(tiles):
        ref[8 * i : 8 * i + 8, :] = tile


def take_tiles(ref, first, last):
    return [ref[8 * i : 8 * i + 8, :] for i in range(first, last)]


def load_pair(ref, f):
    return [ref[f, 0:8, :], ref[f, 8:16, :]]


def load_state(ref):
    pairs = [load_pair(ref, f) for f in range(5)]
    return [[pairs[f][t] for f in range(5)] for t in range(2)]


def load_rows(ref, g):
    pairs = [load_pair(ref, 3 * g + d) for d in range(3)]
    return [[pairs[d][t] for d in range(3)] for t in range(2)]


def by_field(tiles):
    return [[tiles[0][f], tiles[1][f]] for f in range(len(tiles[0]))]


def lane_partner(frame, tile, flip):
    step = jnp.where(frame.point_lane == 3, 1, -1)
    other = lane_gather(tile, jnp.clip(frame.lane + step, 0, frame.lanes - 1))
    wall = (frame.lane == 0) | (frame.lane == frame.lanes - 1)
    return jnp.where(wall, -tile if flip else tile, other)


def lane_normal(frame, rows):
    take_before = (frame.point_lane == 0) & (frame.lane != 0)
    return [jnp.where(take_before, pltpu.roll(r, 1, 1), r) for r in rows]


def first_kernel(
    cons_in, jac_in, met_in, xm_in, xf_in, zm_in, zf_in,
    cons, jac, met, zm_out, zf_out, matrix_out, x_index, grad_out, low_out, up_out,
    xm_ref, xf_ref, sems,
):
    moves = [
        (xf_in, xf_ref),
        (zf_in, zf_out),
        (xm_in, xm_ref),
        (zm_in, zm_out),
        (cons_in, cons),
        (jac_in, jac),
        (met_in.at[0:3], met.at[0:3]),
        (met_in.at[3:6], met.at[3:6]),
        (met_in.at[6:9], met.at[6:9]),
    ]
    copies = [pltpu.make_async_copy(a, b, sems.at[i]) for i, (a, b) in enumerate(moves)]
    for c in copies:
        c.start()
    frame = Frame(cons.shape[-1])
    frame.deriv_weights()
    matrix_out[...] = frame.lane_matrix()
    for c in copies[:4]:
        c.wait()
    x_turn = turn_indices(frame, spread_flags(frame, xf_ref[...]), True)
    z_turn = turn_indices(frame, spread_flags(frame, zf_out[...]), True)
    master = spread_flags(frame, xm_ref[...])
    store_indices(frame, x_index, x_turn, master)
    for c in copies[4:]:
        c.wait()
    state = load_state(cons)
    state_f = by_field(state)
    lifted = []
    for t in range(2):
        velocity, _, theta = primitive(state[t])
        lifted.append(velocity + [theta])
    inverse = [1.0 / jac[0:8, :], 1.0 / jac[8:16, :]]
    z_turned = [turn(frame.face_z(p), z_turn) for p in state_f]
    x_turned = [turn(frame.face_x(p), x_turn) for p in state_f]
    rows = [load_rows(met, g) for g in range(3)]
    cx = by_field([combos(lifted[t], rows[0][t]) for t in range(2)])
    cz = by_field([combos(lifted[t], rows[1][t]) for t in range(2)])
    cy = by_field([combos(lifted[t], rows[2][t]) for t in range(2)])
    sign = frame.sign_lanes()
    lane_part = []
    for t in range(2):
        other = [lane_partner(frame, lifted[t][k], k < 3) for k in range(4)]
        mean = [0.5 * (lifted[t][k] + other[k]) for k in range(4)]
        lane_part.append(combos(mean, lane_normal(frame, rows[2][t])))
    grad = []
    dy = frame.deriv_lanes_all([cy[f][t] for f in range(9) for t in range(2)], matrix_out[...])
    for f in range(9):
        dx = frame.deriv_x(cx[f])
        grad.append(
            [
                dx[t]
                + frame.deriv_rows(cz[f][t])
                + dy[2 * f + t]
                + sign * lane_part[t][f]
                for t in range(2)
            ]
        )
    for f in range(9):
        for t in range(2):
            grad_out[f, 8 * t : 8 * t + 8, :] = grad[f][t]

    lead = master == 1
    own_rows = [frame.face_x(p) for p in by_field(rows[0])]
    turned_rows = [turn(p, x_turn) for p in own_rows]
    velocity, _, theta = primitive(x_turned)
    line = velocity + [theta]
    outer = (frame.point_row == 0) | (frame.point_row == 3)
    right = jnp.where(frame.point_row >= 2, 4, 0)
    picks = [right + jnp.where(frame.low_half, 3, 0), right + jnp.where(frame.low_half, 0, 3)]
    merge = lambda i, a, b: jnp.where(outer, sub_gather(a, picks[i % 2]), sub_gather(b, picks[i % 2]))
    zero = jnp.zeros_like(line[0])
    edges = [merge(0, line[0], line[1]), merge(1, line[2], line[3])]
    for d in range(3):
        edges.append(
            merge(d, jnp.where(lead, turned_rows[d], zero), jnp.where(lead, own_rows[d], zero))
        )
    faces = z_turned + [turn(frame.face_z(p), z_turn) for p in by_field(rows[1])]
    faces = [frame.swap(p) if i % 2 == 0 else p for i, p in enumerate(faces)]
    faces = faces + [
        frame.face_z(p, swapped=i % 2 == 0) for i, p in enumerate([inverse] + grad)
    ]
    pack(frame, faces + edges, low_out, up_out)


def first_cover(
    cons, jac, met, zm_ref, zf_ref, x_index, grad_in, z_index, face_out, near_out, far_out
):
    frame = Frame(cons.shape[-1])
    x_turn = load_indices(x_index)[0]
    fields = [load_pair(cons, f) for f in range(5)] + [load_pair(met, d) for d in range(3)]
    fields.append([1.0 / jac[0:8, :], 1.0 / jac[8:16, :]])
    fields = [turn(frame.face_x(p), x_turn) for p in fields]
    fields = [frame.swap(p) if i % 2 == 0 else p for i, p in enumerate(fields)]
    pack_pairs(frame, fields, near_out, far_out)
    for f in range(9):
        tile = turn(frame.face_x(load_pair(grad_in, f)), x_turn)
        face_out[8 * f : 8 * f + 8, :] = frame.swap(tile) if f % 2 == 0 else tile
    z_turn = turn_indices(frame, spread_flags(frame, zf_ref[...]), False)
    store_indices(frame, z_index, z_turn, spread_flags(frame, zm_ref[...]))


def mean_of(prim1, prim2):
    return [0.5 * (a + b) for a, b in zip(prim1[0] + [prim1[2]], prim2[0] + [prim2[2]])]


def second_kernel(
    cons, met, x_index, z_index, grad_in, x_face, left, right, grad_out, part_out, near_out, far_out
):
    frame = Frame(cons.shape[-1])
    lead = z_index[40:48, :] == 1
    x_turn = load_indices(x_index)[0]
    got = unpack(frame, left, right, 23)
    other = straight(frame, got[:8])
    own = [frame.face_z(load_pair(cons, f)) for f in range(5)]
    own_rows = [frame.face_z(load_pair(met, 3 + d)) for d in range(3)]
    normal = [jnp.where(lead, own_rows[d], other[5 + d]) for d in range(3)]
    part = combos(mean_of(primitive(own), primitive(other[:5])), normal)
    stack_tiles(part_out, part)
    across = jnp.where(frame.low_half, 0, 3) + jnp.where(frame.point_row >= 2, 4, 0)
    sign = frame.sign_rows()
    fields = take_tiles(x_face, 0, 9)
    for f in range(9):
        tile = turn(sign * sub_gather(part[f], across), x_turn)
        fields[f] = fields[f] + (frame.swap(tile) if f % 2 == 0 else tile)
    odd = frame.point_row % 2
    high = jnp.where(frame.point_row >= 2, 4, 0)

    def passed(low):
        return high + jnp.where(low, odd, 3 - odd), high + jnp.where(low, 0, 3)

    pair_a, outer_a = passed(jnp.logical_not(frame.low_half))
    pair_b, outer_b = passed(frame.low_half)
    fields.append(sub_gather(got[18], pair_b))
    fields.append(sub_gather(got[19], pair_a ^ 4))
    fields.append(
        jnp.where(odd == 0, sub_gather(got[20], outer_b), sub_gather(got[21], outer_b ^ 4))
    )
    fields.append(sub_gather(got[22], outer_a))
    pack_pairs(frame, fields, near_out, far_out)
    for f in range(9):
        spread = frame.spread_z(part[f])
        for t in range(2):
            grad_out[f, 8 * t : 8 * t + 8, :] = (
                grad_in[f, 8 * t : 8 * t + 8, :] + sign * spread[t]
            )


def plain_face(own, own_prim, other, other_prim, normal, side_sign):
    size = size_of(normal)
    flux1, speed1 = plain_flux(own, own_prim[0], own_prim[1], normal)
    flux2, speed2 = plain_flux(other, other_prim[0], other_prim[1], normal)
    fastest = jnp.maximum(wave(speed1, own_prim[2], size), wave(speed2, other_prim[2], size))
    half = 0.5 * side_sign * fastest
    return [0.5 * (flux1[c] + flux2[c]) - half * (other[c] - own[c]) for c in range(5)]


def second_cover(cons, met, z_index, lift_in, left, right, part_out, face_out, normal_out):
    frame = Frame(cons.shape[-1])
    lead = z_index[40:48, :] == 1
    both = load_indices(z_index)
    got = unpack(frame, left, right, 23)
    turned = straight(frame, got[:8]) + turn_all(got[8:18], both)
    other = turned[:5]
    other_prim = primitive(other)
    own = [frame.face_z(load_pair(cons, f)) for f in range(5)]
    own_rows = [frame.face_z(load_pair(met, 3 + d)) for d in range(3)]
    own_prim = primitive(own)
    normal = [jnp.where(lead, own_rows[d], turned[5 + d]) for d in range(3)]
    flux = plain_face(own, own_prim, other, other_prim, normal, frame.sides(-1.0, 1.0))
    sign = frame.sign_rows()
    plain_z = [frame.spread_z(flux[c]) for c in range(5)]
    face_sign = frame.sides(-lift, lift)
    slopes = [(turned[9 + f] - face_sign * lift_in[8 * f : 8 * f + 8, :]) * turned[8] for f in range(9)]
    edge_scale = turn(sign, both[0]) * turned[8]
    own_edge = jnp.where(frame.low_half, 0, 4) + jnp.where(frame.point_row >= 2, 2, 1)
    own_lines = [sub_gather(got[20 + d], own_edge ^ 4 if d == 1 else own_edge) for d in range(3)]
    stack_tiles(
        face_out,
        own_prim[0]
        + other_prim[0]
        + [other_prim[2]]
        + normal
        + drag_flux(other_prim[0], slopes, normal)[0]
        + own_lines
        + [edge_scale],
    )

    frame.deriv_weights()
    state = load_state(cons)
    rows = [load_rows(met, g) for g in range(3)]
    sign_y = frame.sign_lanes()
    up_lane = frame.point_lane == 3
    wall = (frame.lane == 0) | (frame.lane == frame.lanes - 1)
    volume = []
    lane_flux = []
    for t in range(2):
        velocity, pressure, theta = primitive(state[t])
        volume.append([plain_flux(state[t], velocity, pressure, rows[g][t])[0] for g in range(3)])
        normal = lane_normal(frame, rows[2][t])
        for d in range(3):
            normal_out[d, 8 * t : 8 * t + 8, :] = normal[d]
        half, speed = plain_flux(state[t], velocity, pressure, normal)
        own_wave = wave(speed, theta, size_of(normal))
        fastest = jnp.maximum(own_wave, lane_partner(frame, own_wave, False))
        mirrored = [-half[0], half[1], half[2], half[3], -half[4]]
        direction = jnp.where(up_lane, jnp.float32(0.5), jnp.float32(-0.5)) * fastest
        result = []
        for c in range(5):
            other_half = jnp.where(wall, mirrored[c], lane_partner(frame, half[c], False))
            other_state = lane_partner(frame, state[t][c], 1 <= c <= 3)
            result.append(0.5 * (half[c] + other_half) - direction * (other_state - state[t][c]))
        lane_flux.append(result)
    for c in range(5):
        dx = frame.deriv_x([volume[t][0][c] for t in range(2)])
        for t in range(2):
            part_out[c, 8 * t : 8 * t + 8, :] = (
                sign * plain_z[c][t]
                + dx[t]
                + frame.deriv_rows(volume[t][1][c])
                + frame.deriv_lanes(volume[t][2][c])
                + sign_y * lane_flux[t][c]
            )


def third_kernel(
    cons, jac, met, x_index, z_index, grad_in, part_in, z_face, y_normal, matrix,
    near_one, far_one, near_two, far_two, out
):
    frame = Frame(cons.shape[-1])
    frame.deriv_weights()
    state = load_state(cons)
    state_f = by_field(state)
    rows = [load_rows(met, g) for g in range(3)]
    inverse = [1.0 / jac[0:8, :], 1.0 / jac[8:16, :]]
    got = unpack_pairs(frame, near_two, far_two, 13)
    x_lead = x_index[40:48, :] == 1
    turned = straight(frame, unpack_pairs(frame, near_one, far_one, 9)) + straight(frame, got[:9])
    face_sign = frame.sides(-lift, lift)

    own = [frame.face_x(p) for p in state_f]
    own_rows = [frame.face_x(p) for p in by_field(rows[0])]
    own_prim = primitive(own)
    other = turned[:5]
    other_prim = primitive(other)
    normal_x = [jnp.where(x_lead, own_rows[d], turned[5 + d]) for d in range(3)]
    part = combos(mean_of(own_prim, other_prim), normal_x)
    slopes = []
    for f in range(9):
        lifted_part = face_sign * part[f]
        zero = jnp.zeros_like(lifted_part)
        tiles = [
            grad_in[f, 0:8, :] + jnp.where(frame.low_half, lifted_part, zero),
            grad_in[f, 8:16, :] + jnp.where(frame.low_half, zero, lifted_part),
        ]
        slopes.append([tiles[t] * inverse[t] for t in range(2)])
    own_slopes = [frame.face_x(p) for p in slopes]
    other_slopes = [(turned[9 + f] - face_sign * part[f]) * turned[8] for f in range(9)]
    flux_x = plain_face(own, own_prim, other, other_prim, normal_x, frame.sides(-1.0, 1.0))
    drag1 = drag_flux(own_prim[0], own_slopes, normal_x)[0]
    drag2 = drag_flux(other_prim[0], other_slopes, normal_x)[0]
    flux_x = [flux_x[0]] + [flux_x[1 + c] - 0.5 * (drag1[c] + drag2[c]) for c in range(4)]

    edge_a = jnp.where(frame.low_half, 0, 2) + jnp.where(frame.point_row >= 2, 4, 0)
    edge_b = edge_a + 1
    lines = [
        sub_gather(got[9], edge_a ^ 4),
        sub_gather(got[9], edge_b ^ 4),
        sub_gather(got[10], edge_a),
        sub_gather(got[10], edge_b),
        sub_gather(got[11], edge_a ^ 4),
        sub_gather(got[11], edge_b ^ 4),
        sub_gather(got[12], edge_a),
    ]
    face = take_tiles(z_face, 0, 18)
    lines[4:] = [lines[4 + d] + face[14 + d] for d in range(3)]
    z_indices = load_indices(z_index)[0]
    lines = [turn(p, z_indices) for p in lines]
    mean = [0.5 * (a + b) for a, b in zip(face[3:7], lines[:4])]
    edge_slopes = [face[17] * p for p in combos(mean, lines[4:])]
    normal_z = face[7:10]
    own_slopes = [frame.face_z(p) for p in slopes]
    drag1 = drag_flux(face[0:3], own_slopes, normal_z)[0]
    drag2 = drag_flux(face[3:6], edge_slopes, normal_z)[0]
    drag_z = [0.5 * (drag1[c] + face[10 + c] + drag2[c]) for c in range(4)]

    slopes_t = [[slopes[f][t] for f in range(9)] for t in range(2)]
    sign_y = frame.sign_lanes()
    wall = (frame.lane == 0) | (frame.lane == frame.lanes - 1)
    volume = []
    lane_flux = []
    for t in range(2):
        velocity = primitive(state[t])[0]
        volume.append([drag_flux(velocity, slopes_t[t], rows[g][t])[0] for g in range(3)])
        normal = [y_normal[d, 8 * t : 8 * t + 8, :] for d in range(3)]
        half, heat = drag_flux(velocity, slopes_t[t], normal)
        mirrored = [half[0], half[1], half[2], 2.0 * heat - half[3]]
        result = []
        for c in range(4):
            other_half = jnp.where(wall, mirrored[c], lane_partner(frame, half[c], False))
            result.append(0.5 * (half[c] + other_half))
        lane_flux.append(result)
    row_sign = frame.sign_rows()
    dy = frame.deriv_lanes_all(
        [volume[t][2][k] for k in range(4) for t in range(2)], matrix[...]
    )
    for c in range(5):
        side = face_sign * flux_x[c]
        zero = jnp.zeros_like(side)
        sides = [jnp.where(frame.low_half, side, zero), jnp.where(frame.low_half, zero, side)]
        totals = [part_in[c, 8 * t : 8 * t + 8, :] + sides[t] for t in range(2)]
        if c > 0:
            k = c - 1
            dx = frame.deriv_x([volume[t][0][k] for t in range(2)])
            spread = frame.spread_z(drag_z[k])
            for t in range(2):
                totals[t] = totals[t] - (
                    dx[t]
                    + frame.deriv_rows(volume[t][1][k])
                    + dy[2 * k + t]
                    + sign_y * lane_flux[t][k]
                    + row_sign * spread[t]
                )
        for t in range(2):
            out[c, 8 * t : 8 * t + 8, :] = -totals[t] * inverse[t]


def shaped(*shape, dtype=jnp.float32):
    return jax.ShapeDtypeStruct(shape, dtype)


def call(kernel, outs, *args, in_specs=None, scratch=()):
    return pl.pallas_call(
        kernel,
        out_shape=outs,
        in_specs=in_specs or [whole] * len(args),
        out_specs=[whole] * len(outs),
        scratch_shapes=scratch,
        compiler_params=pltpu.CompilerParams(vmem_limit_bytes=vmem_bytes),
        cost_estimate=pl.CostEstimate(flops=1_000_000, bytes_accessed=200_000, transcendentals=0),
    )(*args)


def exchange(low, up, axis):
    count = lax.axis_size(axis)
    from_left = lax.ppermute(up, axis, [(i, (i + 1) % count) for i in range(count)])
    from_right = lax.ppermute(low, axis, [((i + 1) % count, i) for i in range(count)])
    return from_left, from_right


def exchange_pairs(near, far, axis):
    count = lax.axis_size(axis)
    assert count % 2 == 0
    swaps = [[], []]
    for k in range(count):
        a, b = k, (k + 1) % count
        swaps[k % 2] += [(a, b), (b, a)]
    got_far = lax.ppermute(far, axis, swaps[1])
    got_near = lax.ppermute(near, axis, swaps[0])
    return got_near, got_far


def local(conserved, jacobian, metric, x_master, x_flip, z_master, z_flip):
    lanes = conserved.shape[-1]
    nodes = conserved.shape[1] * conserved.shape[2]
    assert conserved.shape[1:3] == (4, 4)
    cons = conserved.reshape(5, nodes, lanes)
    jac = jacobian.reshape(nodes, lanes)
    met = metric.reshape(9, nodes, lanes)
    xm, xf, zm, zf = [a.reshape(2, a.shape[-1]) for a in (x_master, x_flip, z_master, z_flip)]
    flag = (2, xm.shape[-1])
    nodal9, nodal5 = shaped(9, nodes, lanes), shaped(5, nodes, lanes)
    flags = shaped(*flag, dtype=jnp.int32)
    index = shaped(48, lanes, dtype=jnp.int32)
    matrix_shape = shaped(2 * lanes, 2 * lanes, dtype=jnp.bfloat16)
    cons, jac, met, zm, zf, matrix, x_index, grad, low_z, up_z = call(
        first_kernel,
        [nodal5, shaped(nodes, lanes), nodal9]
        + [flags] * 2
        + [matrix_shape, index, nodal9]
        + [shaped(96, lanes)] * 2,
        *[pltpu.with_memory_space_constraint(a, pltpu.HBM) for a in (cons, jac, met, xm, xf, zm, zf)],
        in_specs=[pl.BlockSpec(memory_space=pltpu.HBM)] * 7,
        scratch=[
            pltpu.VMEM(flag, jnp.int32),
            pltpu.VMEM(flag, jnp.int32),
            pltpu.SemaphoreType.DMA((9,)),
        ],
    )
    left_z, right_z = exchange(low_z, up_z, "gz")
    z_index, x_face, near_one, far_one = call(
        first_cover,
        [index, shaped(72, lanes)] + [shaped(40, lanes)] * 2,
        cons, jac, met, zm, zf, x_index, grad,
    )
    near_one, far_one = exchange_pairs(near_one, far_one, "gx")
    grad, lift_z, near_two, far_two = call(
        second_kernel,
        [nodal9, shaped(72, lanes), shaped(56, lanes), shaped(56, lanes)],
        cons, met, x_index, z_index, grad, x_face, left_z, right_z,
    )
    near_two, far_two = exchange_pairs(near_two, far_two, "gx")
    part, z_face, y_normal = call(
        second_cover,
        [nodal5, shaped(144, lanes), shaped(3, nodes, lanes)],
        cons, met, z_index, lift_z, left_z, right_z,
    )
    (rhs,) = call(
        third_kernel,
        [nodal5],
        cons, jac, met, x_index, z_index, grad, part, z_face, y_normal, matrix,
        near_one, far_one, near_two, far_two,
    )
    return rhs.reshape(conserved.shape)


def solution(mesh):
    in_specs = (
        P(None, "gx", "gz", None),
        P("gx", "gz", None),
        P(None, None, "gx", "gz", None),
        P("gx", "gz", None),
        P("gx", "gz", None),
        P("gx", "gz", None),
        P("gx", "gz", None),
    )
    out_specs = P(None, "gx", "gz", None)
    return jax.shard_map(local, mesh=mesh, in_specs=in_specs, out_specs=out_specs, check_vma=False)
```

```python
import math

import jax
import jax.numpy as jnp
import numpy as np
from jax import lax
from jax.experimental import pallas as pl
from jax.experimental.pallas import tpu as pltpu
from jax.sharding import PartitionSpec as P


gamma_gas = 1.4
visc_coef = 0.1
prandtl = 0.72
lift = 6.0
heat_coef = visc_coef * gamma_gas / ((gamma_gas - 1.0) * prandtl)
vmem_bytes = 8 << 20
whole = pl.BlockSpec(memory_space=pltpu.VMEM)


def node_table():
    points = np.array([-1.0, -math.sqrt(0.2), math.sqrt(0.2), 1.0])
    scales = np.array([np.prod([points[i] - points[k] for k in range(4) if k != i]) for i in range(4)])
    table = np.zeros((4, 4))
    for i in range(4):
        for k in range(4):
            if i != k:
                table[i, k] = scales[i] / (scales[k] * (points[i] - points[k]))
        table[i, i] = -np.sum(table[i])
    return table


def weak_table():
    table = node_table()
    table[0, 0] += lift
    table[3, 3] -= lift
    return table


def rows_of(lanes):
    return lax.broadcasted_iota(jnp.int32, (8, lanes), 0)


def lanes_of(lanes):
    return lax.broadcasted_iota(jnp.int32, (8, lanes), 1)


def pick4(index, values):
    out = jnp.full(index.shape, values[3], jnp.float32)
    for k in (2, 1, 0):
        out = jnp.where(index == k, jnp.float32(values[k]), out)
    return out


def shift_weights(index, table):
    weights = {}
    for shift in range(-3, 4):
        weights[shift] = pick4(index, [table[j, j - shift] if 0 <= j - shift < 4 else 0.0 for j in range(4)])
    return weights


def three_parts(values):
    parts = []
    for _ in range(3):
        part = values.astype(jnp.bfloat16)
        values = values - part.astype(jnp.float32)
        parts.append(part)
    return parts


class Frame:
    def __init__(self, lanes):
        self.lanes = lanes
        row = rows_of(lanes)
        lane = lanes_of(lanes)
        self.row, self.lane = row, lane
        self.low_half = row < 4
        self.point_row = row % 4
        self.point_lane = lane % 4

    def deriv_weights(self):
        table = weak_table()
        self.weights_z = shift_weights(self.point_row, table)
        self.weights_y = shift_weights(self.point_lane, table)
        pair = lambda top, bottom: jnp.where(self.low_half, jnp.float32(top), jnp.float32(bottom))
        self.weights_x = [
            [
                pair(table[2 * t, 2 * s], table[2 * t + 1, 2 * s + 1]),
                pair(table[2 * t, 2 * s + 1], table[2 * t + 1, 2 * s]),
            ]
            for t in range(2)
            for s in range(2)
        ]

    def swap(self, tile):
        return pltpu.roll(tile, 4, 0)

    def deriv_x(self, pair):
        a, b = pair
        a2, b2 = self.swap(a), self.swap(b)
        w = self.weights_x
        return [
            w[2 * t][0] * a + w[2 * t][1] * a2 + w[2 * t + 1][0] * b + w[2 * t + 1][1] * b2
            for t in range(2)
        ]

    def deriv_rows(self, tile):
        out = self.weights_z[0] * tile
        for shift in (-3, -2, -1, 1, 2, 3):
            out = out + self.weights_z[shift] * pltpu.roll(tile, shift % 8, 0)
        return out

    def lane_matrix(self):
        shape = (self.lanes, self.lanes)
        to = lax.broadcasted_iota(jnp.int32, shape, 1)
        gap = to - lax.broadcasted_iota(jnp.int32, shape, 0)
        full = jnp.zeros(shape, jnp.float32)
        for shift in range(-3, 4):
            full = jnp.where(gap == shift, jnp.broadcast_to(self.weights_y[shift][0:1], shape), full)
        high, middle, low = three_parts(full)
        top = jnp.concatenate([high, middle, high], 1)
        bottom = jnp.concatenate([high, middle, low], 1)
        return jnp.concatenate([top, bottom], 0)

    def deriv_lanes_all(self, tiles, matrix):
        high, middle, low = three_parts(jnp.concatenate(tiles, 0))
        n = self.lanes
        wide = jnp.dot(
            jnp.concatenate([high, middle], 1), matrix[:, : 2 * n], preferred_element_type=jnp.float32
        )
        rest = jnp.dot(
            jnp.concatenate([low, high], 1), matrix[:, 2 * n :], preferred_element_type=jnp.float32
        )
        out = wide[:, :n] + (wide[:, n:] + rest)
        return [out[8 * i : 8 * i + 8] for i in range(len(tiles))]

    def deriv_lanes(self, tile):
        out = self.weights_y[0] * tile
        for shift in (-3, -2, -1, 1, 2, 3):
            out = out + self.weights_y[shift] * pltpu.roll(tile, shift % self.lanes, 1)
        return out

    def face_x(self, pair):
        return jnp.where(self.low_half, pair[0], pair[1])

    def face_z(self, pair, swapped=False):
        side = jnp.where(self.low_half, 3, 0) if swapped else jnp.where(self.low_half, 0, 3)
        index = side + 4 * (self.point_row % 2)
        return jnp.where(self.point_row < 2, sub_gather(pair[0], index), sub_gather(pair[1], index))

    def spread_z(self, face):
        upper = jnp.where(self.point_row == 3, 4, 0)
        inner = jnp.where(self.low_half, 0, 1)
        return [sub_gather(face, upper + inner + 2 * t) for t in range(2)]

    def sides(self, low, up):
        return jnp.where(self.low_half, jnp.float32(low), jnp.float32(up))

    def sign_lanes(self):
        return jnp.where(
            self.point_lane == 3, jnp.float32(lift), jnp.where(self.point_lane == 0, jnp.float32(-lift), 0.0)
        )

    def sign_rows(self):
        return jnp.where(
            self.point_row == 3, jnp.float32(lift), jnp.where(self.point_row == 0, jnp.float32(-lift), 0.0)
        )


def sub_gather(tile, index):
    return jnp.take_along_axis(tile, index, axis=0)


def lane_gather(tile, index):
    return jnp.take_along_axis(tile, index, axis=1)


def primitive(state):
    inverse = 1.0 / state[0]
    velocity = [state[1 + j] * inverse for j in range(3)]
    kinetic = state[1] * velocity[0] + state[2] * velocity[1] + state[3] * velocity[2]
    pressure = (gamma_gas - 1.0) * (state[4] - 0.5 * kinetic)
    return velocity, pressure, pressure * inverse


def combos(values, rows):
    w0, w1, w2, w3 = values
    m0, m1, m2 = rows
    return [
        w0 * m0,
        w1 * m1,
        w2 * m2,
        w0 * m1 + w1 * m0,
        w0 * m2 + w2 * m0,
        w1 * m2 + w2 * m1,
        w3 * m0,
        w3 * m1,
        w3 * m2,
    ]


def plain_flux(state, velocity, pressure, normal):
    speed = velocity[0] * normal[0] + velocity[1] * normal[1] + velocity[2] * normal[2]
    out = [state[0] * speed]
    for j in range(3):
        out.append(state[1 + j] * speed + pressure * normal[j])
    out.append((state[4] + pressure) * speed)
    return out, speed


def traction(slopes, normal):
    m0, m1, m2 = normal
    spread = (visc_coef * 2.0 / 3.0) * (slopes[0] + slopes[1] + slopes[2])
    t00, t11, t22 = [2.0 * visc_coef * slopes[d] - spread for d in range(3)]
    t01, t02, t12 = [visc_coef * slopes[3 + d] for d in range(3)]
    return [
        t00 * m0 + t01 * m1 + t02 * m2,
        t01 * m0 + t11 * m1 + t12 * m2,
        t02 * m0 + t12 * m1 + t22 * m2,
        heat_coef * (slopes[6] * m0 + slopes[7] * m1 + slopes[8] * m2),
    ]


def drag_of(velocity, forces):
    work = velocity[0] * forces[0] + velocity[1] * forces[1] + velocity[2] * forces[2]
    return forces[:3] + [work + forces[3]]


def drag_flux(velocity, slopes, normal):
    forces = traction(slopes, normal)
    return drag_of(velocity, forces), forces[3]


def wave(speed, theta, normal_size):
    return jnp.abs(speed) + jnp.sqrt(gamma_gas * theta) * normal_size


def size_of(normal):
    return jnp.sqrt(normal[0] * normal[0] + normal[1] * normal[1] + normal[2] * normal[2])


def paired(frame, swapped_a, b):
    low = jnp.where(frame.low_half, b, swapped_a)
    up = jnp.where(frame.low_half, swapped_a, b)
    return low, up


def pack(frame, fields, low_ref, up_ref):
    fields = list(fields)
    if len(fields) % 2:
        fields.append(fields[-1])
    for g in range(len(fields) // 2):
        low, up = paired(frame, fields[2 * g], fields[2 * g + 1])
        low_ref[8 * g : 8 * g + 8, :] = low
        up_ref[8 * g : 8 * g + 8, :] = up


def unpack(frame, left_ref, right_ref, count):
    fields = []
    for g in range((count + 1) // 2):
        left = left_ref[8 * g : 8 * g + 8, :]
        right = right_ref[8 * g : 8 * g + 8, :]
        fields.append(jnp.where(frame.low_half, left, right))
        fields.append(jnp.where(frame.low_half, right, left))
    return fields[:count]


def first_of_pair(frame):
    return jnp.full((8, frame.lanes), lax.axis_index("gx") % 2) == 0


def pack_pairs(frame, fields, near_ref, far_ref):
    lower = first_of_pair(frame)
    fields = fields + [fields[-1]] * (len(fields) % 2)
    for g in range(len(fields) // 2):
        low, up = paired(frame, fields[2 * g], fields[2 * g + 1])
        near_ref[8 * g : 8 * g + 8, :] = jnp.where(lower, up, low)
        far_ref[8 * g : 8 * g + 8, :] = jnp.where(lower, low, up)


def unpack_pairs(frame, near_ref, far_ref, count):
    straight = first_of_pair(frame) == frame.low_half
    fields = []
    for g in range((count + 1) // 2):
        near = near_ref[8 * g : 8 * g + 8, :]
        far = far_ref[8 * g : 8 * g + 8, :]
        fields.append(jnp.where(straight, far, near))
        fields.append(jnp.where(straight, near, far))
    return fields[:count]


def spread_flags(frame, flags):
    count = flags.shape[-1]
    hit = lax.broadcasted_iota(jnp.int32, (count, frame.lanes), 0) == (
        lax.broadcasted_iota(jnp.int32, (count, frame.lanes), 1) // 4
    )
    wide = jnp.dot(
        flags.astype(jnp.float32), hit.astype(jnp.float32), preferred_element_type=jnp.float32
    )
    wide = (wide + 0.5).astype(jnp.int32)
    shape = (8, frame.lanes)
    return jnp.where(
        frame.low_half, jnp.broadcast_to(wide[0:1], shape), jnp.broadcast_to(wide[1:2], shape)
    )


def turn_indices(frame, code, forward_low):
    swap = (code & 4) != 0
    first = (code & 1) * 3
    second = ((code >> 1) & 1) * 3
    forward = frame.low_half if forward_low else jnp.logical_not(frame.low_half)
    flip_a = jnp.where(forward, second, first)
    flip_b = jnp.where(forward, first, second)
    row4, lane4 = frame.point_row, frame.point_lane
    lane_base = frame.lane - lane4
    row_base = frame.row - row4
    step1 = lane_base + jnp.where(swap, (lane4 - row4) & 3, lane4)
    step2 = row_base + jnp.where(swap, (lane4 - (row4 ^ flip_b)) & 3, row4 ^ first)
    step3 = lane_base + jnp.where(swap, ((lane4 ^ flip_a) + (row4 ^ flip_b)) & 3, lane4 ^ second)
    return step1, step2, step3


def turn(tile, indices):
    return lane_gather(sub_gather(lane_gather(tile, indices[0]), indices[1]), indices[2])


def store_indices(frame, ref, indices, master):
    step1, step2, step3 = indices
    stack_tiles(ref, [step1, step2, step3, frame.swap(step1), step2 ^ 4, master])


def load_indices(ref):
    step1, step2, step3, swapped1, swapped2, _ = take_tiles(ref, 0, 6)
    return (step1, step2, step3), (swapped1, swapped2, step3)


def turn_all(fields, both, first=0):
    return [turn(p, both[(first + i) % 2]) for i, p in enumerate(fields)]


def straight(frame, fields):
    return [frame.swap(p) if i % 2 else p for i, p in enumerate(fields)]


def stack_tiles(ref, tiles):
    for i, tile in enumerate(tiles):
        ref[8 * i : 8 * i + 8, :] = tile


def take_tiles(ref, first, last):
    return [ref[8 * i : 8 * i + 8, :] for i in range(first, last)]


def load_pair(ref, f):
    return [ref[f, 0:8, :], ref[f, 8:16, :]]


def load_state(ref):
    pairs = [load_pair(ref, f) for f in range(5)]
    return [[pairs[f][t] for f in range(5)] for t in range(2)]


def load_rows(ref, g):
    pairs = [load_pair(ref, 3 * g + d) for d in range(3)]
    return [[pairs[d][t] for d in range(3)] for t in range(2)]


def by_field(tiles):
    return [[tiles[0][f], tiles[1][f]] for f in range(len(tiles[0]))]


def lane_partner(frame, tile, flip):
    step = jnp.where(frame.point_lane == 3, 1, -1)
    other = lane_gather(tile, jnp.clip(frame.lane + step, 0, frame.lanes - 1))
    wall = (frame.lane == 0) | (frame.lane == frame.lanes - 1)
    return jnp.where(wall, -tile if flip else tile, other)


def lane_normal(frame, rows):
    take_before = (frame.point_lane == 0) & (frame.lane != 0)
    return [jnp.where(take_before, pltpu.roll(r, 1, 1), r) for r in rows]


def split_nodal(nodal):
    return nodal.at[0:5], nodal.at[5], nodal.at[6:15]


def first_kernel(
    cons_in, jac_in, met_in, xm_in, xf_in, zm_in, zf_in,
    nodal, flags, matrix_out, x_index, grad_out, low_out, up_out, sems,
):
    cons, jac, met = split_nodal(nodal)
    flag_moves = [(a, flags.at[i]) for i, a in enumerate((xf_in, zf_in, xm_in, zm_in))]
    moves = [(cons_in, cons), (jac_in, jac)]
    moves += [(met_in.at[3 * g : 3 * g + 3], met.at[3 * g : 3 * g + 3]) for g in range(3)]
    for a, b in flag_moves:
        pltpu.make_async_copy(a, b, sems.at[0]).start()
    for a, b in moves:
        pltpu.make_async_copy(a, b, sems.at[1]).start()
    frame = Frame(cons.shape[-1])
    frame.deriv_weights()
    matrix_out[...] = frame.lane_matrix()
    pltpu.make_async_copy(flags, flags, sems.at[0]).wait()
    x_turn = turn_indices(frame, spread_flags(frame, flags[0]), True)
    z_turn = turn_indices(frame, spread_flags(frame, flags[1]), True)
    master = spread_flags(frame, flags[2])
    store_indices(frame, x_index, x_turn, master)
    z_lead = spread_flags(frame, flags[3]) == 1
    pltpu.make_async_copy(nodal, nodal, sems.at[1]).wait()
    state = load_state(cons)
    state_f = by_field(state)
    lifted = []
    for t in range(2):
        velocity, _, theta = primitive(state[t])
        lifted.append(velocity + [theta])
    inverse = [1.0 / jac[0:8, :], 1.0 / jac[8:16, :]]
    z_turned = [turn(frame.face_z(p), z_turn) for p in state_f]
    x_turned = [turn(frame.face_x(p), x_turn) for p in state_f]
    rows = [load_rows(met, g) for g in range(3)]
    cx = by_field([combos(lifted[t], rows[0][t]) for t in range(2)])
    cz = by_field([combos(lifted[t], rows[1][t]) for t in range(2)])
    cy = by_field([combos(lifted[t], rows[2][t]) for t in range(2)])
    sign = frame.sign_lanes()
    lane_part = []
    for t in range(2):
        other = [lane_partner(frame, lifted[t][k], k < 3) for k in range(4)]
        mean = [0.5 * (lifted[t][k] + other[k]) for k in range(4)]
        lane_part.append(combos(mean, lane_normal(frame, rows[2][t])))
    grad = []
    dy = frame.deriv_lanes_all([cy[f][t] for f in range(9) for t in range(2)], matrix_out[...])
    for f in range(9):
        dx = frame.deriv_x(cx[f])
        grad.append(
            [
                dx[t]
                + frame.deriv_rows(cz[f][t])
                + dy[2 * f + t]
                + sign * lane_part[t][f]
                for t in range(2)
            ]
        )
    for f in range(9):
        for t in range(2):
            grad_out[f, 8 * t : 8 * t + 8, :] = grad[f][t]

    lead = master == 1
    own_rows = [frame.face_x(p) for p in by_field(rows[0])]
    turned_rows = [turn(p, x_turn) for p in own_rows]
    velocity, _, theta = primitive(x_turned)
    line = velocity + [theta]
    outer = (frame.point_row == 0) | (frame.point_row == 3)
    right = jnp.where(frame.point_row >= 2, 4, 0)
    picks = [right + jnp.where(frame.low_half, 3, 0), right + jnp.where(frame.low_half, 0, 3)]
    merge = lambda i, a, b: jnp.where(outer, sub_gather(a, picks[i % 2]), sub_gather(b, picks[i % 2]))
    zero = jnp.zeros_like(line[0])
    edges = [merge(1, line[0], line[1]), merge(0, line[2], line[3])]
    for d in range(3):
        edges.append(
            merge(d + 1, jnp.where(lead, turned_rows[d], zero), jnp.where(lead, own_rows[d], zero))
        )
    z_rows = [frame.face_z(p) for p in by_field(rows[1])]
    slots = [frame.face_z(p) for p in grad]
    known = [turn(p, z_turn) for p in z_rows] + traction(slots, z_rows)
    slots = [jnp.where(z_lead, a, b) for a, b in zip(known, slots)] + slots[7:]
    faces = z_turned + [frame.face_z(inverse)] + slots
    faces = [frame.swap(p) if i % 2 == 0 else p for i, p in enumerate(faces)]
    pack(frame, faces + edges, low_out, up_out)


def first_cover(
    nodal, flags, x_index, grad_in, z_index, x_back, face_out, near_out, far_out
):
    cons, jac, met = split_nodal(nodal)
    frame = Frame(cons.shape[-1])
    x_turn = load_indices(x_index)[0]
    fields = [load_pair(cons, f) for f in range(5)] + [load_pair(met, d) for d in range(3)]
    fields.append([1.0 / jac[0:8, :], 1.0 / jac[8:16, :]])
    fields = [turn(frame.face_x(p), x_turn) for p in fields]
    fields = [frame.swap(p) if i % 2 == 0 else p for i, p in enumerate(fields)]
    pack_pairs(frame, fields, near_out, far_out)
    for f in range(9):
        tile = frame.face_x(load_pair(grad_in, f))
        face_out[8 * f : 8 * f + 8, :] = frame.swap(tile) if f % 2 == 0 else tile
    z_turn = turn_indices(frame, spread_flags(frame, flags[1]), False)
    store_indices(frame, z_index, z_turn, spread_flags(frame, flags[3]))
    x_return = turn_indices(frame, spread_flags(frame, flags[0]), False)
    store_indices(frame, x_back, x_return, take_tiles(x_index, 5, 6)[0])


def mean_of(prim1, prim2):
    return [0.5 * (a + b) for a, b in zip(prim1[0] + [prim1[2]], prim2[0] + [prim2[2]])]


def second_kernel(
    nodal, z_index, grad_in, x_face, near_in, left, right,
    grad_out, part_out, near_out, far_out
):
    cons, _, met = split_nodal(nodal)
    frame = Frame(cons.shape[-1])
    lead = z_index[40:48, :] == 1
    got = unpack(frame, left, right, 20)
    other = straight(frame, got[:9])
    own = [frame.face_z(load_pair(cons, f)) for f in range(5)]
    own_rows = [frame.face_z(load_pair(met, 3 + d)) for d in range(3)]
    normal = [jnp.where(lead, own_rows[d], other[6 + d]) for d in range(3)]
    part = combos(mean_of(primitive(own), primitive(other[:5])), normal)
    stack_tiles(part_out, part)
    right = jnp.where(frame.point_row >= 2, 4, 0)
    across = [right + jnp.where(frame.low_half, 3, 0), right + jnp.where(frame.low_half, 0, 3)]
    sign = frame.sign_rows()
    fields = take_tiles(x_face, 0, 9)
    for f in range(9):
        fields[f] = fields[f] + sign * sub_gather(part[f], across[f % 2])
    odd = frame.point_row % 2
    high = jnp.where(frame.point_row >= 2, 4, 0)

    def passed(low):
        return high + jnp.where(low, odd, 3 - odd), high + jnp.where(low, 0, 3)

    pair_a, outer_a = passed(jnp.logical_not(frame.low_half))
    pair_b, outer_b = passed(frame.low_half)
    fields.append(sub_gather(got[15], pair_b ^ 4))
    fields.append(sub_gather(got[16], pair_a))
    fields.append(
        jnp.where(odd == 0, sub_gather(got[17], outer_b ^ 4), sub_gather(got[18], outer_b))
    )
    fields.append(sub_gather(got[19], outer_a ^ 4))
    static = near_in.shape[0]
    near_out[:static, :] = near_in[...]
    pack_pairs(frame, fields, near_out.at[static:], far_out)
    for f in range(9):
        spread = frame.spread_z(part[f])
        for t in range(2):
            grad_out[f, 8 * t : 8 * t + 8, :] = (
                grad_in[f, 8 * t : 8 * t + 8, :] + sign * spread[t]
            )


def plain_face(own, own_prim, other, other_prim, normal, side_sign):
    size = size_of(normal)
    flux1, speed1 = plain_flux(own, own_prim[0], own_prim[1], normal)
    flux2, speed2 = plain_flux(other, other_prim[0], other_prim[1], normal)
    fastest = jnp.maximum(wave(speed1, own_prim[2], size), wave(speed2, other_prim[2], size))
    half = 0.5 * side_sign * fastest
    return [0.5 * (flux1[c] + flux2[c]) - half * (other[c] - own[c]) for c in range(5)]


def second_cover(nodal, z_index, lift_in, left, right, part_out, face_out, normal_out):
    cons, _, met = split_nodal(nodal)
    frame = Frame(cons.shape[-1])
    lead = z_index[40:48, :] == 1
    both = load_indices(z_index)
    got = unpack(frame, left, right, 20)
    turned = straight(frame, got[:9])
    scale, *slots = turn_all(got[5:15], both, 5)
    other = turned[:5]
    other_prim = primitive(other)
    own = [frame.face_z(load_pair(cons, f)) for f in range(5)]
    own_rows = [frame.face_z(load_pair(met, 3 + d)) for d in range(3)]
    own_prim = primitive(own)
    normal = [jnp.where(lead, own_rows[d], turned[6 + d]) for d in range(3)]
    flux = plain_face(own, own_prim, other, other_prim, normal, frame.sides(-1.0, 1.0))
    sign = frame.sign_rows()
    plain_z = [frame.spread_z(flux[c]) for c in range(5)]
    face_sign = frame.sides(-lift, lift)
    forces = [jnp.where(lead, a, b) for a, b in zip(traction(slots, normal), slots[3:7])]
    lifts = traction([face_sign * p for p in take_tiles(lift_in, 0, 9)], normal)
    forces = [scale * (a - b) for a, b in zip(forces, lifts)]
    edge_scale = turn(sign, both[0]) * scale
    own_edge = jnp.where(frame.low_half, 0, 4) + jnp.where(frame.point_row >= 2, 2, 1)
    own_lines = [sub_gather(got[17 + d], own_edge if d == 1 else own_edge ^ 4) for d in range(3)]
    stack_tiles(
        face_out,
        own_prim[0]
        + other_prim[0]
        + [other_prim[2]]
        + normal
        + drag_of(other_prim[0], forces)
        + own_lines
        + [edge_scale],
    )

    frame.deriv_weights()
    state = load_state(cons)
    rows = [load_rows(met, g) for g in range(3)]
    sign_y = frame.sign_lanes()
    up_lane = frame.point_lane == 3
    wall = (frame.lane == 0) | (frame.lane == frame.lanes - 1)
    volume = []
    lane_flux = []
    for t in range(2):
        velocity, pressure, theta = primitive(state[t])
        volume.append([plain_flux(state[t], velocity, pressure, rows[g][t])[0] for g in range(3)])
        normal = lane_normal(frame, rows[2][t])
        for d in range(3):
            normal_out[d, 8 * t : 8 * t + 8, :] = normal[d]
        half, speed = plain_flux(state[t], velocity, pressure, normal)
        own_wave = wave(speed, theta, size_of(normal))
        fastest = jnp.maximum(own_wave, lane_partner(frame, own_wave, False))
        mirrored = [-half[0], half[1], half[2], half[3], -half[4]]
        direction = jnp.where(up_lane, jnp.float32(0.5), jnp.float32(-0.5)) * fastest
        result = []
        for c in range(5):
            other_half = jnp.where(wall, mirrored[c], lane_partner(frame, half[c], False))
            other_state = lane_partner(frame, state[t][c], 1 <= c <= 3)
            result.append(0.5 * (half[c] + other_half) - direction * (other_state - state[t][c]))
        lane_flux.append(result)
    for c in range(5):
        dx = frame.deriv_x([volume[t][0][c] for t in range(2)])
        for t in range(2):
            part_out[c, 8 * t : 8 * t + 8, :] = (
                sign * plain_z[c][t]
                + dx[t]
                + frame.deriv_rows(volume[t][1][c])
                + frame.deriv_lanes(volume[t][2][c])
                + sign_y * lane_flux[t][c]
            )


def third_kernel(
    nodal, x_index, z_index, grad_in, part_in, z_face, y_normal, matrix,
    far_one, near_two, far_two, out
):
    cons, jac, met = split_nodal(nodal)
    frame = Frame(cons.shape[-1])
    frame.deriv_weights()
    state = load_state(cons)
    state_f = by_field(state)
    rows = [load_rows(met, g) for g in range(3)]
    inverse = [1.0 / jac[0:8, :], 1.0 / jac[8:16, :]]
    static = far_one.shape[0]
    got = unpack_pairs(frame, near_two.at[static:], far_two, 13)
    x_lead = x_index[40:48, :] == 1
    turned = straight(frame, unpack_pairs(frame, near_two.at[:static], far_one, 9))
    turned = turned + turn_all(got[:9], load_indices(x_index))
    face_sign = frame.sides(-lift, lift)

    own = [frame.face_x(p) for p in state_f]
    own_rows = [frame.face_x(p) for p in by_field(rows[0])]
    own_prim = primitive(own)
    other = turned[:5]
    other_prim = primitive(other)
    normal_x = [jnp.where(x_lead, own_rows[d], turned[5 + d]) for d in range(3)]
    part = combos(mean_of(own_prim, other_prim), normal_x)
    slopes = []
    for f in range(9):
        lifted_part = face_sign * part[f]
        zero = jnp.zeros_like(lifted_part)
        tiles = [
            grad_in[f, 0:8, :] + jnp.where(frame.low_half, lifted_part, zero),
            grad_in[f, 8:16, :] + jnp.where(frame.low_half, zero, lifted_part),
        ]
        slopes.append([tiles[t] * inverse[t] for t in range(2)])
    own_slopes = [frame.face_x(p) for p in slopes]
    other_slopes = [(turned[9 + f] - face_sign * part[f]) * turned[8] for f in range(9)]
    flux_x = plain_face(own, own_prim, other, other_prim, normal_x, frame.sides(-1.0, 1.0))
    drag1 = drag_flux(own_prim[0], own_slopes, normal_x)[0]
    drag2 = drag_flux(other_prim[0], other_slopes, normal_x)[0]
    flux_x = [flux_x[0]] + [flux_x[1 + c] - 0.5 * (drag1[c] + drag2[c]) for c in range(4)]

    edge_a = jnp.where(frame.low_half, 0, 2) + jnp.where(frame.point_row >= 2, 4, 0)
    edge_b = edge_a + 1
    lines = [
        sub_gather(got[9], edge_a ^ 4),
        sub_gather(got[9], edge_b ^ 4),
        sub_gather(got[10], edge_a),
        sub_gather(got[10], edge_b),
        sub_gather(got[11], edge_a ^ 4),
        sub_gather(got[11], edge_b ^ 4),
        sub_gather(got[12], edge_a),
    ]
    face = take_tiles(z_face, 0, 18)
    lines[4:] = [lines[4 + d] + face[14 + d] for d in range(3)]
    z_indices = load_indices(z_index)[0]
    lines = [turn(p, z_indices) for p in lines]
    mean = [0.5 * (a + b) for a, b in zip(face[3:7], lines[:4])]
    edge_slopes = [face[17] * p for p in combos(mean, lines[4:])]
    normal_z = face[7:10]
    own_slopes = [frame.face_z(p) for p in slopes]
    drag1 = drag_flux(face[0:3], own_slopes, normal_z)[0]
    drag2 = drag_flux(face[3:6], edge_slopes, normal_z)[0]
    drag_z = [0.5 * (drag1[c] + face[10 + c] + drag2[c]) for c in range(4)]

    slopes_t = [[slopes[f][t] for f in range(9)] for t in range(2)]
    sign_y = frame.sign_lanes()
    wall = (frame.lane == 0) | (frame.lane == frame.lanes - 1)
    volume = []
    lane_flux = []
    for t in range(2):
        velocity = primitive(state[t])[0]
        volume.append([drag_flux(velocity, slopes_t[t], rows[g][t])[0] for g in range(3)])
        normal = [y_normal[d, 8 * t : 8 * t + 8, :] for d in range(3)]
        half, heat = drag_flux(velocity, slopes_t[t], normal)
        mirrored = [half[0], half[1], half[2], 2.0 * heat - half[3]]
        result = []
        for c in range(4):
            other_half = jnp.where(wall, mirrored[c], lane_partner(frame, half[c], False))
            result.append(0.5 * (half[c] + other_half))
        lane_flux.append(result)
    row_sign = frame.sign_rows()
    dy = frame.deriv_lanes_all(
        [volume[t][2][k] for k in range(4) for t in range(2)], matrix[...]
    )
    for c in range(5):
        side = face_sign * flux_x[c]
        zero = jnp.zeros_like(side)
        sides = [jnp.where(frame.low_half, side, zero), jnp.where(frame.low_half, zero, side)]
        totals = [part_in[c, 8 * t : 8 * t + 8, :] + sides[t] for t in range(2)]
        if c > 0:
            k = c - 1
            dx = frame.deriv_x([volume[t][0][k] for t in range(2)])
            spread = frame.spread_z(drag_z[k])
            for t in range(2):
                totals[t] = totals[t] - (
                    dx[t]
                    + frame.deriv_rows(volume[t][1][k])
                    + dy[2 * k + t]
                    + sign_y * lane_flux[t][k]
                    + row_sign * spread[t]
                )
        for t in range(2):
            out[c, 8 * t : 8 * t + 8, :] = -totals[t] * inverse[t]


def shaped(*shape, dtype=jnp.float32):
    return jax.ShapeDtypeStruct(shape, dtype)


def call(kernel, outs, *args, in_specs=None, scratch=()):
    return pl.pallas_call(
        kernel,
        out_shape=outs,
        in_specs=in_specs or [whole] * len(args),
        out_specs=[whole] * len(outs),
        scratch_shapes=scratch,
        compiler_params=pltpu.CompilerParams(vmem_limit_bytes=vmem_bytes),
        cost_estimate=pl.CostEstimate(flops=1_000_000, bytes_accessed=200_000, transcendentals=0),
    )(*args)


def exchange(low, up, axis):
    count = lax.axis_size(axis)
    from_left = lax.ppermute(up, axis, [(i, (i + 1) % count) for i in range(count)])
    from_right = lax.ppermute(low, axis, [((i + 1) % count, i) for i in range(count)])
    return from_left, from_right


def exchange_pairs(values, axis, far):
    count = lax.axis_size(axis)
    assert count % 2 == 0
    swaps = []
    for k in range(far, count, 2):
        a, b = k, (k + 1) % count
        swaps += [(a, b), (b, a)]
    return lax.ppermute(values, axis, swaps)


def local(conserved, jacobian, metric, x_master, x_flip, z_master, z_flip):
    lanes = conserved.shape[-1]
    nodes = conserved.shape[1] * conserved.shape[2]
    assert conserved.shape[1:3] == (4, 4)
    cons = conserved.reshape(5, nodes, lanes)
    jac = jacobian.reshape(nodes, lanes)
    met = metric.reshape(9, nodes, lanes)
    xm, xf, zm, zf = [a.reshape(2, a.shape[-1]) for a in (x_master, x_flip, z_master, z_flip)]
    flag = (2, xm.shape[-1])
    nodal9, nodal5 = shaped(9, nodes, lanes), shaped(5, nodes, lanes)
    index = shaped(48, lanes, dtype=jnp.int32)
    matrix_shape = shaped(2 * lanes, 3 * lanes, dtype=jnp.bfloat16)
    nodal, flags, matrix, x_index, grad, low_z, up_z = call(
        first_kernel,
        [
            shaped(15, nodes, lanes),
            shaped(4, *flag, dtype=jnp.int32),
            matrix_shape,
            index,
            nodal9,
            shaped(80, lanes),
            shaped(80, lanes),
        ],
        *[pltpu.with_memory_space_constraint(a, pltpu.HBM) for a in (cons, jac, met, xm, xf, zm, zf)],
        in_specs=[pl.BlockSpec(memory_space=pltpu.HBM)] * 7,
        scratch=[pltpu.SemaphoreType.DMA((2,))],
    )
    left_z, right_z = exchange(low_z, up_z, "gz")
    z_index, x_back, x_face, near_one, far_one = call(
        first_cover,
        [index, index, shaped(72, lanes)] + [shaped(40, lanes)] * 2,
        nodal, flags, x_index, grad,
    )
    far_one = exchange_pairs(far_one, "gx", 1)
    grad, lift_z, near_two, far_two = call(
        second_kernel,
        [nodal9, shaped(72, lanes), shaped(96, lanes), shaped(56, lanes)],
        nodal, z_index, grad, x_face, near_one, left_z, right_z,
    )
    far_two = exchange_pairs(far_two, "gx", 1)
    near_two = exchange_pairs(near_two, "gx", 0)
    part, z_face, y_normal = call(
        second_cover,
        [nodal5, shaped(144, lanes), shaped(3, nodes, lanes)],
        nodal, z_index, lift_z, left_z, right_z,
    )
    (rhs,) = call(
        third_kernel,
        [nodal5],
        nodal, x_back, z_index, grad, part, z_face, y_normal, matrix,
        far_one, near_two, far_two,
    )
    return rhs.reshape(conserved.shape)


def solution(mesh):
    in_specs = (
        P(None, "gx", "gz", None),
        P("gx", "gz", None),
        P(None, None, "gx", "gz", None),
        P("gx", "gz", None),
        P("gx", "gz", None),
        P("gx", "gz", None),
        P("gx", "gz", None),
    )
    out_specs = P(None, "gx", "gz", None)
    return jax.shard_map(local, mesh=mesh, in_specs=in_specs, out_specs=out_specs, check_vma=False)
```

```python
import math

import jax
import jax.numpy as jnp
import numpy as np
from jax import lax
from jax.experimental import pallas as pl
from jax.experimental.pallas import tpu as pltpu
from jax.sharding import PartitionSpec as P


gamma_gas = 1.4
visc_coef = 0.1
prandtl = 0.72
lift = 6.0
heat_coef = visc_coef * gamma_gas / ((gamma_gas - 1.0) * prandtl)
vmem_bytes = 8 << 20
whole = pl.BlockSpec(memory_space=pltpu.VMEM)


def node_table():
    points = np.array([-1.0, -math.sqrt(0.2), math.sqrt(0.2), 1.0])
    scales = np.array([np.prod([points[i] - points[k] for k in range(4) if k != i]) for i in range(4)])
    table = np.zeros((4, 4))
    for i in range(4):
        for k in range(4):
            if i != k:
                table[i, k] = scales[i] / (scales[k] * (points[i] - points[k]))
        table[i, i] = -np.sum(table[i])
    return table


def weak_table():
    table = node_table()
    table[0, 0] += lift
    table[3, 3] -= lift
    return table


def rows_of(lanes):
    return lax.broadcasted_iota(jnp.int32, (8, lanes), 0)


def lanes_of(lanes):
    return lax.broadcasted_iota(jnp.int32, (8, lanes), 1)


def pick4(index, values):
    out = jnp.full(index.shape, values[3], jnp.float32)
    for k in (2, 1, 0):
        out = jnp.where(index == k, jnp.float32(values[k]), out)
    return out


def shift_weights(index, table):
    weights = {}
    for shift in range(-3, 4):
        weights[shift] = pick4(index, [table[j, j - shift] if 0 <= j - shift < 4 else 0.0 for j in range(4)])
    return weights


def three_parts(values):
    parts = []
    for _ in range(3):
        part = values.astype(jnp.bfloat16)
        values = values - part.astype(jnp.float32)
        parts.append(part)
    return parts


class Frame:
    def __init__(self, lanes):
        self.lanes = lanes
        row = rows_of(lanes)
        lane = lanes_of(lanes)
        self.row, self.lane = row, lane
        self.low_half = row < 4
        self.point_row = row % 4
        self.point_lane = lane % 4

    def deriv_weights(self):
        table = weak_table()
        self.weights_z = shift_weights(self.point_row, table)
        self.weights_y = shift_weights(self.point_lane, table)
        pair = lambda top, bottom: jnp.where(self.low_half, jnp.float32(top), jnp.float32(bottom))
        self.weights_x = [
            [
                pair(table[2 * t, 2 * s], table[2 * t + 1, 2 * s + 1]),
                pair(table[2 * t, 2 * s + 1], table[2 * t + 1, 2 * s]),
            ]
            for t in range(2)
            for s in range(2)
        ]

    def swap(self, tile):
        return pltpu.roll(tile, 4, 0)

    def deriv_x(self, pair):
        a, b = pair
        a2, b2 = self.swap(a), self.swap(b)
        w = self.weights_x
        return [
            w[2 * t][0] * a + w[2 * t][1] * a2 + w[2 * t + 1][0] * b + w[2 * t + 1][1] * b2
            for t in range(2)
        ]

    def deriv_rows(self, tile):
        out = self.weights_z[0] * tile
        for shift in (-3, -2, -1, 1, 2, 3):
            out = out + self.weights_z[shift] * pltpu.roll(tile, shift % 8, 0)
        return out

    def lane_matrix(self):
        shape = (self.lanes, self.lanes)
        to = lax.broadcasted_iota(jnp.int32, shape, 1)
        gap = to - lax.broadcasted_iota(jnp.int32, shape, 0)
        full = jnp.zeros(shape, jnp.float32)
        for shift in range(-3, 4):
            full = jnp.where(gap == shift, jnp.broadcast_to(self.weights_y[shift][0:1], shape), full)
        high, middle, low = three_parts(full)
        top = jnp.concatenate([high, middle, high], 1)
        bottom = jnp.concatenate([high, middle, low], 1)
        return jnp.concatenate([top, bottom], 0)

    def deriv_lanes_all(self, tiles, matrix):
        high, middle, low = three_parts(jnp.concatenate(tiles, 0))
        n = self.lanes
        wide = jnp.dot(
            jnp.concatenate([high, middle], 1), matrix[:, : 2 * n], preferred_element_type=jnp.float32
        )
        rest = jnp.dot(
            jnp.concatenate([low, high], 1), matrix[:, 2 * n :], preferred_element_type=jnp.float32
        )
        out = wide[:, :n] + (wide[:, n:] + rest)
        return [out[8 * i : 8 * i + 8] for i in range(len(tiles))]

    def deriv_lanes(self, tile):
        out = self.weights_y[0] * tile
        for shift in (-3, -2, -1, 1, 2, 3):
            out = out + self.weights_y[shift] * pltpu.roll(tile, shift % self.lanes, 1)
        return out

    def face_x(self, pair):
        return jnp.where(self.low_half, pair[0], pair[1])

    def face_z(self, pair, swapped=False):
        side = jnp.where(self.low_half, 3, 0) if swapped else jnp.where(self.low_half, 0, 3)
        index = side + 4 * (self.point_row % 2)
        return jnp.where(self.point_row < 2, sub_gather(pair[0], index), sub_gather(pair[1], index))

    def spread_z(self, face):
        upper = jnp.where(self.point_row == 3, 4, 0)
        inner = jnp.where(self.low_half, 0, 1)
        return [sub_gather(face, upper + inner + 2 * t) for t in range(2)]

    def sides(self, low, up):
        return jnp.where(self.low_half, jnp.float32(low), jnp.float32(up))

    def sign_lanes(self):
        return jnp.where(
            self.point_lane == 3, jnp.float32(lift), jnp.where(self.point_lane == 0, jnp.float32(-lift), 0.0)
        )

    def sign_rows(self):
        return jnp.where(
            self.point_row == 3, jnp.float32(lift), jnp.where(self.point_row == 0, jnp.float32(-lift), 0.0)
        )


def sub_gather(tile, index):
    return jnp.take_along_axis(tile, index, axis=0)


def lane_gather(tile, index):
    return jnp.take_along_axis(tile, index, axis=1)


def primitive(state):
    inverse = 1.0 / state[0]
    velocity = [state[1 + j] * inverse for j in range(3)]
    kinetic = state[1] * velocity[0] + state[2] * velocity[1] + state[3] * velocity[2]
    pressure = (gamma_gas - 1.0) * (state[4] - 0.5 * kinetic)
    return velocity, pressure, pressure * inverse


def combos(values, rows):
    w0, w1, w2, w3 = values
    m0, m1, m2 = rows
    return [
        w0 * m0,
        w1 * m1,
        w2 * m2,
        w0 * m1 + w1 * m0,
        w0 * m2 + w2 * m0,
        w1 * m2 + w2 * m1,
        w3 * m0,
        w3 * m1,
        w3 * m2,
    ]


def plain_flux(state, velocity, pressure, normal):
    speed = velocity[0] * normal[0] + velocity[1] * normal[1] + velocity[2] * normal[2]
    out = [state[0] * speed]
    for j in range(3):
        out.append(state[1 + j] * speed + pressure * normal[j])
    out.append((state[4] + pressure) * speed)
    return out, speed


def traction(slopes, normal):
    m0, m1, m2 = normal
    spread = (visc_coef * 2.0 / 3.0) * (slopes[0] + slopes[1] + slopes[2])
    t00, t11, t22 = [2.0 * visc_coef * slopes[d] - spread for d in range(3)]
    t01, t02, t12 = [visc_coef * slopes[3 + d] for d in range(3)]
    return [
        t00 * m0 + t01 * m1 + t02 * m2,
        t01 * m0 + t11 * m1 + t12 * m2,
        t02 * m0 + t12 * m1 + t22 * m2,
        heat_coef * (slopes[6] * m0 + slopes[7] * m1 + slopes[8] * m2),
    ]


def drag_of(velocity, forces):
    work = velocity[0] * forces[0] + velocity[1] * forces[1] + velocity[2] * forces[2]
    return forces[:3] + [work + forces[3]]


def drag_flux(velocity, slopes, normal):
    forces = traction(slopes, normal)
    return drag_of(velocity, forces), forces[3]


def wave(speed, theta, normal_size):
    return jnp.abs(speed) + jnp.sqrt(gamma_gas * theta) * normal_size


def size_of(normal):
    return jnp.sqrt(normal[0] * normal[0] + normal[1] * normal[1] + normal[2] * normal[2])


def paired(frame, swapped_a, b):
    low = jnp.where(frame.low_half, b, swapped_a)
    up = jnp.where(frame.low_half, swapped_a, b)
    return low, up


def pack(frame, fields, low_ref, up_ref):
    fields = list(fields)
    if len(fields) % 2:
        fields.append(fields[-1])
    for g in range(len(fields) // 2):
        low, up = paired(frame, fields[2 * g], fields[2 * g + 1])
        low_ref[8 * g : 8 * g + 8, :] = low
        up_ref[8 * g : 8 * g + 8, :] = up


def unpack(frame, left_ref, right_ref, count):
    fields = []
    for g in range((count + 1) // 2):
        left = left_ref[8 * g : 8 * g + 8, :]
        right = right_ref[8 * g : 8 * g + 8, :]
        fields.append(jnp.where(frame.low_half, left, right))
        fields.append(jnp.where(frame.low_half, right, left))
    return fields[:count]


def first_of_pair(frame):
    return jnp.full((8, frame.lanes), lax.axis_index("gx") % 2) == 0


def pack_pairs(frame, fields, near_ref, far_ref):
    lower = first_of_pair(frame)
    fields = fields + [fields[-1]] * (len(fields) % 2)
    for g in range(len(fields) // 2):
        low, up = paired(frame, fields[2 * g], fields[2 * g + 1])
        near_ref[8 * g : 8 * g + 8, :] = jnp.where(lower, up, low)
        far_ref[8 * g : 8 * g + 8, :] = jnp.where(lower, low, up)


def unpack_pairs(frame, near_ref, far_ref, count):
    straight = first_of_pair(frame) == frame.low_half
    fields = []
    for g in range((count + 1) // 2):
        near = near_ref[8 * g : 8 * g + 8, :]
        far = far_ref[8 * g : 8 * g + 8, :]
        fields.append(jnp.where(straight, far, near))
        fields.append(jnp.where(straight, near, far))
    return fields[:count]


def spread_flags(frame, flags):
    count = flags.shape[-1]
    hit = lax.broadcasted_iota(jnp.int32, (count, frame.lanes), 0) == (
        lax.broadcasted_iota(jnp.int32, (count, frame.lanes), 1) // 4
    )
    wide = jnp.dot(
        flags.astype(jnp.float32), hit.astype(jnp.float32), preferred_element_type=jnp.float32
    )
    wide = (wide + 0.5).astype(jnp.int32)
    shape = (8, frame.lanes)
    return jnp.where(
        frame.low_half, jnp.broadcast_to(wide[0:1], shape), jnp.broadcast_to(wide[1:2], shape)
    )


def turn_indices(frame, code, forward_low):
    swap = (code & 4) != 0
    first = (code & 1) * 3
    second = ((code >> 1) & 1) * 3
    forward = frame.low_half if forward_low else jnp.logical_not(frame.low_half)
    flip_a = jnp.where(forward, second, first)
    flip_b = jnp.where(forward, first, second)
    row4, lane4 = frame.point_row, frame.point_lane
    lane_base = frame.lane - lane4
    row_base = frame.row - row4
    step1 = lane_base + jnp.where(swap, (lane4 - row4) & 3, lane4)
    step2 = row_base + jnp.where(swap, (lane4 - (row4 ^ flip_b)) & 3, row4 ^ first)
    step3 = lane_base + jnp.where(swap, ((lane4 ^ flip_a) + (row4 ^ flip_b)) & 3, lane4 ^ second)
    return step1, step2, step3


def turn(tile, indices):
    return lane_gather(sub_gather(lane_gather(tile, indices[0]), indices[1]), indices[2])


def store_indices(frame, ref, indices, master):
    step1, step2, step3 = indices
    stack_tiles(ref, [step1, step2, step3, frame.swap(step1), step2 ^ 4, master])


def load_indices(ref):
    step1, step2, step3, swapped1, swapped2, _ = take_tiles(ref, 0, 6)
    return (step1, step2, step3), (swapped1, swapped2, step3)


def turn_all(fields, both, first=0):
    return [turn(p, both[(first + i) % 2]) for i, p in enumerate(fields)]


def straight(frame, fields):
    return [frame.swap(p) if i % 2 else p for i, p in enumerate(fields)]


def stack_tiles(ref, tiles):
    for i, tile in enumerate(tiles):
        ref[8 * i : 8 * i + 8, :] = tile


def take_tiles(ref, first, last):
    return [ref[8 * i : 8 * i + 8, :] for i in range(first, last)]


def load_pair(ref, f):
    return [ref[f, 0:8, :], ref[f, 8:16, :]]


def load_state(ref):
    pairs = [load_pair(ref, f) for f in range(5)]
    return [[pairs[f][t] for f in range(5)] for t in range(2)]


def load_rows(ref, g):
    pairs = [load_pair(ref, 3 * g + d) for d in range(3)]
    return [[pairs[d][t] for d in range(3)] for t in range(2)]


def by_field(tiles):
    return [[tiles[0][f], tiles[1][f]] for f in range(len(tiles[0]))]


def lane_partner(frame, tile, flip):
    step = jnp.where(frame.point_lane == 3, 1, -1)
    other = lane_gather(tile, jnp.clip(frame.lane + step, 0, frame.lanes - 1))
    wall = (frame.lane == 0) | (frame.lane == frame.lanes - 1)
    return jnp.where(wall, -tile if flip else tile, other)


def lane_normal(frame, rows):
    take_before = (frame.point_lane == 0) & (frame.lane != 0)
    return [jnp.where(take_before, pltpu.roll(r, 1, 1), r) for r in rows]


def split_nodal(nodal):
    return nodal.at[0:5], nodal.at[5], nodal.at[6:15]


def first_kernel(
    cons_in, jac_in, met_in, xm_in, xf_in, zm_in, zf_in,
    nodal, flags, matrix_out, x_index, grad_out, low_out, up_out, sems,
):
    cons, jac, met = split_nodal(nodal)
    flag_moves = [(a, flags.at[i]) for i, a in enumerate((xf_in, zf_in, xm_in, zm_in))]
    moves = [(cons_in, cons), (jac_in, jac)]
    moves += [(met_in.at[3 * g : 3 * g + 3], met.at[3 * g : 3 * g + 3]) for g in range(3)]
    for a, b in flag_moves:
        pltpu.make_async_copy(a, b, sems.at[0]).start()
    for a, b in moves:
        pltpu.make_async_copy(a, b, sems.at[1]).start()
    frame = Frame(cons.shape[-1])
    frame.deriv_weights()
    matrix_out[...] = frame.lane_matrix()
    pltpu.make_async_copy(flags, flags, sems.at[0]).wait()
    x_turn = turn_indices(frame, spread_flags(frame, flags[0]), True)
    z_turn = turn_indices(frame, spread_flags(frame, flags[1]), True)
    master = spread_flags(frame, flags[2])
    store_indices(frame, x_index, x_turn, master)
    z_lead = spread_flags(frame, flags[3]) == 1
    pltpu.make_async_copy(nodal, nodal, sems.at[1]).wait()
    state = load_state(cons)
    state_f = by_field(state)
    lifted = []
    for t in range(2):
        velocity, _, theta = primitive(state[t])
        lifted.append(velocity + [theta])
    inverse = [1.0 / jac[0:8, :], 1.0 / jac[8:16, :]]
    z_turned = [turn(frame.face_z(p), z_turn) for p in state_f]
    x_turned = [turn(frame.face_x(p), x_turn) for p in state_f]
    rows = [load_rows(met, g) for g in range(3)]
    cx = by_field([combos(lifted[t], rows[0][t]) for t in range(2)])
    cz = by_field([combos(lifted[t], rows[1][t]) for t in range(2)])
    cy = by_field([combos(lifted[t], rows[2][t]) for t in range(2)])
    sign = frame.sign_lanes()
    lane_part = []
    for t in range(2):
        other = [lane_partner(frame, lifted[t][k], k < 3) for k in range(4)]
        mean = [0.5 * (lifted[t][k] + other[k]) for k in range(4)]
        lane_part.append(combos(mean, lane_normal(frame, rows[2][t])))
    grad = []
    dy = frame.deriv_lanes_all([cy[f][t] for f in range(9) for t in range(2)], matrix_out[...])
    for f in range(9):
        dx = frame.deriv_x(cx[f])
        grad.append(
            [
                dx[t]
                + frame.deriv_rows(cz[f][t])
                + dy[2 * f + t]
                + sign * lane_part[t][f]
                for t in range(2)
            ]
        )
    for f in range(9):
        for t in range(2):
            grad_out[f, 8 * t : 8 * t + 8, :] = grad[f][t]

    lead = master == 1
    own_rows = [frame.face_x(p) for p in by_field(rows[0])]
    turned_rows = [turn(p, x_turn) for p in own_rows]
    velocity, _, theta = primitive(x_turned)
    line = velocity + [theta]
    outer = (frame.point_row == 0) | (frame.point_row == 3)
    right = jnp.where(frame.point_row >= 2, 4, 0)
    picks = [right + jnp.where(frame.low_half, 3, 0), right + jnp.where(frame.low_half, 0, 3)]
    merge = lambda i, a, b: jnp.where(outer, sub_gather(a, picks[i % 2]), sub_gather(b, picks[i % 2]))
    zero = jnp.zeros_like(line[0])
    edges = [merge(1, line[0], line[1]), merge(0, line[2], line[3])]
    for d in range(3):
        edges.append(
            merge(d + 1, jnp.where(lead, turned_rows[d], zero), jnp.where(lead, own_rows[d], zero))
        )
    z_rows = [frame.face_z(p) for p in by_field(rows[1])]
    slots = [frame.face_z(p) for p in grad]
    known = [turn(p, z_turn) for p in z_rows] + traction(slots, z_rows)
    slots = [jnp.where(z_lead, a, b) for a, b in zip(known, slots)] + slots[7:]
    faces = z_turned + [frame.face_z(inverse)] + slots
    faces = [frame.swap(p) if i % 2 == 0 else p for i, p in enumerate(faces)]
    pack(frame, faces + edges, low_out, up_out)


def first_cover(
    nodal, flags, x_index, grad_in, z_index, x_back, face_out, near_out, far_out
):
    cons, jac, met = split_nodal(nodal)
    frame = Frame(cons.shape[-1])
    x_turn = load_indices(x_index)[0]
    fields = [load_pair(cons, f) for f in range(5)] + [load_pair(met, d) for d in range(3)]
    fields.append([1.0 / jac[0:8, :], 1.0 / jac[8:16, :]])
    fields = [turn(frame.face_x(p), x_turn) for p in fields]
    fields = [frame.swap(p) if i % 2 == 0 else p for i, p in enumerate(fields)]
    pack_pairs(frame, fields, near_out, far_out)
    for f in range(9):
        tile = frame.face_x(load_pair(grad_in, f))
        face_out[8 * f : 8 * f + 8, :] = frame.swap(tile) if f % 2 == 0 else tile
    z_turn = turn_indices(frame, spread_flags(frame, flags[1]), False)
    store_indices(frame, z_index, z_turn, spread_flags(frame, flags[3]))
    x_return = turn_indices(frame, spread_flags(frame, flags[0]), False)
    store_indices(frame, x_back, x_return, take_tiles(x_index, 5, 6)[0])


def mean_of(prim1, prim2):
    return [0.5 * (a + b) for a, b in zip(prim1[0] + [prim1[2]], prim2[0] + [prim2[2]])]


def second_kernel(
    nodal, z_index, grad_in, x_face, near_in, left, right,
    grad_out, part_out, near_out, far_out
):
    cons, _, met = split_nodal(nodal)
    frame = Frame(cons.shape[-1])
    lead = z_index[40:48, :] == 1
    got = unpack(frame, left, right, 20)
    other = straight(frame, got[:9])
    own = [frame.face_z(load_pair(cons, f)) for f in range(5)]
    own_rows = [frame.face_z(load_pair(met, 3 + d)) for d in range(3)]
    normal = [jnp.where(lead, own_rows[d], other[6 + d]) for d in range(3)]
    part = combos(mean_of(primitive(own), primitive(other[:5])), normal)
    stack_tiles(part_out, part)
    right = jnp.where(frame.point_row >= 2, 4, 0)
    across = [right + jnp.where(frame.low_half, 3, 0), right + jnp.where(frame.low_half, 0, 3)]
    sign = frame.sign_rows()
    fields = take_tiles(x_face, 0, 9)
    for f in range(9):
        fields[f] = fields[f] + sign * sub_gather(part[f], across[f % 2])
    odd = frame.point_row % 2
    high = jnp.where(frame.point_row >= 2, 4, 0)

    def passed(low):
        return high + jnp.where(low, odd, 3 - odd), high + jnp.where(low, 0, 3)

    pair_a, outer_a = passed(jnp.logical_not(frame.low_half))
    pair_b, outer_b = passed(frame.low_half)
    fields.append(sub_gather(got[15], pair_b ^ 4))
    fields.append(sub_gather(got[16], pair_a))
    fields.append(
        jnp.where(odd == 0, sub_gather(got[17], outer_b ^ 4), sub_gather(got[18], outer_b))
    )
    fields.append(sub_gather(got[19], outer_a ^ 4))
    static = near_in.shape[0]
    near_out[:static, :] = near_in[...]
    pack_pairs(frame, fields, near_out.at[static:], far_out)
    for f in range(9):
        spread = frame.spread_z(part[f])
        for t in range(2):
            grad_out[f, 8 * t : 8 * t + 8, :] = (
                grad_in[f, 8 * t : 8 * t + 8, :] + sign * spread[t]
            )


def plain_face(own, own_prim, other, other_prim, normal, side_sign):
    size = size_of(normal)
    flux1, speed1 = plain_flux(own, own_prim[0], own_prim[1], normal)
    flux2, speed2 = plain_flux(other, other_prim[0], other_prim[1], normal)
    fastest = jnp.maximum(wave(speed1, own_prim[2], size), wave(speed2, other_prim[2], size))
    half = 0.5 * side_sign * fastest
    return [0.5 * (flux1[c] + flux2[c]) - half * (other[c] - own[c]) for c in range(5)]


def second_cover(nodal, z_index, lift_in, left, right, part_out, face_out, normal_out):
    cons, _, met = split_nodal(nodal)
    frame = Frame(cons.shape[-1])
    lead = z_index[40:48, :] == 1
    both = load_indices(z_index)
    got = unpack(frame, left, right, 20)
    turned = straight(frame, got[:9])
    scale, *slots = turn_all(got[5:15], both, 5)
    other = turned[:5]
    other_prim = primitive(other)
    own = [frame.face_z(load_pair(cons, f)) for f in range(5)]
    own_rows = [frame.face_z(load_pair(met, 3 + d)) for d in range(3)]
    own_prim = primitive(own)
    normal = [jnp.where(lead, own_rows[d], turned[6 + d]) for d in range(3)]
    flux = plain_face(own, own_prim, other, other_prim, normal, frame.sides(-1.0, 1.0))
    sign = frame.sign_rows()
    plain_z = [frame.spread_z(flux[c]) for c in range(5)]
    face_sign = frame.sides(-lift, lift)
    forces = [jnp.where(lead, a, b) for a, b in zip(traction(slots, normal), slots[3:7])]
    lifts = traction([face_sign * p for p in take_tiles(lift_in, 0, 9)], normal)
    forces = [scale * (a - b) for a, b in zip(forces, lifts)]
    edge_scale = turn(sign, both[0]) * scale
    own_edge = jnp.where(frame.low_half, 0, 4) + jnp.where(frame.point_row >= 2, 2, 1)
    own_lines = [sub_gather(got[17 + d], own_edge if d == 1 else own_edge ^ 4) for d in range(3)]
    stack_tiles(
        face_out,
        own_prim[0]
        + other_prim[0]
        + [other_prim[2]]
        + normal
        + drag_of(other_prim[0], forces)
        + own_lines
        + [edge_scale],
    )

    frame.deriv_weights()
    state = load_state(cons)
    rows = [load_rows(met, g) for g in range(3)]
    sign_y = frame.sign_lanes()
    up_lane = frame.point_lane == 3
    wall = (frame.lane == 0) | (frame.lane == frame.lanes - 1)
    volume = []
    lane_flux = []
    for t in range(2):
        velocity, pressure, theta = primitive(state[t])
        volume.append([plain_flux(state[t], velocity, pressure, rows[g][t])[0] for g in range(3)])
        normal = lane_normal(frame, rows[2][t])
        for d in range(3):
            normal_out[d, 8 * t : 8 * t + 8, :] = normal[d]
        half, speed = plain_flux(state[t], velocity, pressure, normal)
        own_wave = wave(speed, theta, size_of(normal))
        fastest = jnp.maximum(own_wave, lane_partner(frame, own_wave, False))
        mirrored = [-half[0], half[1], half[2], half[3], -half[4]]
        direction = jnp.where(up_lane, jnp.float32(0.5), jnp.float32(-0.5)) * fastest
        result = []
        for c in range(5):
            other_half = jnp.where(wall, mirrored[c], lane_partner(frame, half[c], False))
            other_state = lane_partner(frame, state[t][c], 1 <= c <= 3)
            result.append(0.5 * (half[c] + other_half) - direction * (other_state - state[t][c]))
        lane_flux.append(result)
    for c in range(5):
        dx = frame.deriv_x([volume[t][0][c] for t in range(2)])
        for t in range(2):
            part_out[c, 8 * t : 8 * t + 8, :] = (
                sign * plain_z[c][t]
                + dx[t]
                + frame.deriv_rows(volume[t][1][c])
                + frame.deriv_lanes(volume[t][2][c])
                + sign_y * lane_flux[t][c]
            )


def third_cover(
    nodal, x_index, grad_in, part_in, z_face, y_normal, matrix, far_one, near_two, part_out, face_out
):
    cons, jac, met = split_nodal(nodal)
    frame = Frame(cons.shape[-1])
    frame.deriv_weights()
    state = load_state(cons)
    state_f = by_field(state)
    rows = [load_rows(met, g) for g in range(3)]
    inverse = [1.0 / jac[0:8, :], 1.0 / jac[8:16, :]]
    static = far_one.shape[0]
    x_lead = x_index[40:48, :] == 1
    turned = straight(frame, unpack_pairs(frame, near_two.at[:static], far_one, 9))
    face_sign = frame.sides(-lift, lift)

    own = [frame.face_x(p) for p in state_f]
    own_rows = [frame.face_x(p) for p in by_field(rows[0])]
    own_prim = primitive(own)
    other = turned[:5]
    other_prim = primitive(other)
    normal_x = [jnp.where(x_lead, own_rows[d], turned[5 + d]) for d in range(3)]
    part = combos(mean_of(own_prim, other_prim), normal_x)
    slopes = []
    for f in range(9):
        lifted_part = face_sign * part[f]
        zero = jnp.zeros_like(lifted_part)
        tiles = [
            grad_in[f, 0:8, :] + jnp.where(frame.low_half, lifted_part, zero),
            grad_in[f, 8:16, :] + jnp.where(frame.low_half, zero, lifted_part),
        ]
        slopes.append([tiles[t] * inverse[t] for t in range(2)])
    own_slopes = [frame.face_x(p) for p in slopes]
    flux_x = plain_face(own, own_prim, other, other_prim, normal_x, frame.sides(-1.0, 1.0))
    drag1 = drag_flux(own_prim[0], own_slopes, normal_x)[0]
    flux_x = [flux_x[0]] + [flux_x[1 + c] - 0.5 * drag1[c] for c in range(4)]
    lifts = traction([face_sign * p for p in part], normal_x)
    stack_tiles(face_out, other_prim[0] + normal_x + lifts + [turned[8]])

    face = take_tiles(z_face, 0, 18)
    normal_z = face[7:10]
    own_slopes = [frame.face_z(p) for p in slopes]
    drag1 = drag_flux(face[0:3], own_slopes, normal_z)[0]
    drag_z = [0.5 * (drag1[c] + face[10 + c]) for c in range(4)]

    slopes_t = [[slopes[f][t] for f in range(9)] for t in range(2)]
    sign_y = frame.sign_lanes()
    wall = (frame.lane == 0) | (frame.lane == frame.lanes - 1)
    volume = []
    lane_flux = []
    for t in range(2):
        velocity = primitive(state[t])[0]
        volume.append([drag_flux(velocity, slopes_t[t], rows[g][t])[0] for g in range(3)])
        normal = [y_normal[d, 8 * t : 8 * t + 8, :] for d in range(3)]
        half, heat = drag_flux(velocity, slopes_t[t], normal)
        mirrored = [half[0], half[1], half[2], 2.0 * heat - half[3]]
        result = []
        for c in range(4):
            other_half = jnp.where(wall, mirrored[c], lane_partner(frame, half[c], False))
            result.append(0.5 * (half[c] + other_half))
        lane_flux.append(result)
    row_sign = frame.sign_rows()
    dy = frame.deriv_lanes_all(
        [volume[t][2][k] for k in range(4) for t in range(2)], matrix[...]
    )
    for c in range(5):
        side = face_sign * flux_x[c]
        zero = jnp.zeros_like(side)
        sides = [jnp.where(frame.low_half, side, zero), jnp.where(frame.low_half, zero, side)]
        totals = [part_in[c, 8 * t : 8 * t + 8, :] + sides[t] for t in range(2)]
        if c > 0:
            k = c - 1
            dx = frame.deriv_x([volume[t][0][k] for t in range(2)])
            spread = frame.spread_z(drag_z[k])
            for t in range(2):
                totals[t] = totals[t] - (
                    dx[t]
                    + frame.deriv_rows(volume[t][1][k])
                    + dy[2 * k + t]
                    + sign_y * lane_flux[t][k]
                    + row_sign * spread[t]
                )
        for t in range(2):
            part_out[c, 8 * t : 8 * t + 8, :] = -totals[t] * inverse[t]


def edge_tiles(frame, face):
    zero = jnp.zeros_like(face)
    return [jnp.where(frame.low_half, face, zero), jnp.where(frame.low_half, zero, face)]


def third_kernel(nodal, x_index, z_index, part_in, x_face, z_face, near_two, far_two, out):
    _, jac, _ = split_nodal(nodal)
    frame = Frame(jac.shape[-1])
    static = near_two.shape[0] - far_two.shape[0]
    got = unpack_pairs(frame, near_two.at[static:], far_two, 13)
    other = take_tiles(x_face, 0, 11)
    slopes = turn_all(got[:9], load_indices(x_index))
    forces = traction(slopes, other[3:6])
    forces = [other[10] * (a - b) for a, b in zip(forces, other[6:10])]
    drag_x = drag_of(other[0:3], forces)

    edge_a = jnp.where(frame.low_half, 0, 2) + jnp.where(frame.point_row >= 2, 4, 0)
    edge_b = edge_a + 1
    lines = [
        sub_gather(got[9], edge_a ^ 4),
        sub_gather(got[9], edge_b ^ 4),
        sub_gather(got[10], edge_a),
        sub_gather(got[10], edge_b),
        sub_gather(got[11], edge_a ^ 4),
        sub_gather(got[11], edge_b ^ 4),
        sub_gather(got[12], edge_a),
    ]
    face = take_tiles(z_face, 0, 18)
    lines[4:] = [lines[4 + d] + face[14 + d] for d in range(3)]
    z_indices = load_indices(z_index)[0]
    lines = [turn(p, z_indices) for p in lines]
    mean = [0.5 * (a + b) for a, b in zip(face[3:7], lines[:4])]
    edge_slopes = [face[17] * p for p in combos(mean, lines[4:])]
    normal_z = face[7:10]
    drag_z = drag_flux(face[3:6], edge_slopes, normal_z)[0]
    half_sign = 0.5 * frame.sign_rows()
    half_face = frame.sides(-0.5 * lift, 0.5 * lift)
    for c in range(5):
        totals = [part_in[c, 8 * t : 8 * t + 8, :] for t in range(2)]
        if c > 0:
            spread = frame.spread_z(drag_z[c - 1])
            side = edge_tiles(frame, half_face * drag_x[c - 1])
            for t in range(2):
                scale = 1.0 / jac[8 * t : 8 * t + 8, :]
                totals[t] = totals[t] + scale * (half_sign * spread[t] + side[t])
        for t in range(2):
            out[c, 8 * t : 8 * t + 8, :] = totals[t]


def shaped(*shape, dtype=jnp.float32):
    return jax.ShapeDtypeStruct(shape, dtype)


def call(kernel, outs, *args, in_specs=None, scratch=()):
    return pl.pallas_call(
        kernel,
        out_shape=outs,
        in_specs=in_specs or [whole] * len(args),
        out_specs=[whole] * len(outs),
        scratch_shapes=scratch,
        compiler_params=pltpu.CompilerParams(vmem_limit_bytes=vmem_bytes),
        cost_estimate=pl.CostEstimate(flops=1_000_000, bytes_accessed=200_000, transcendentals=0),
    )(*args)


def exchange(low, up, axis):
    count = lax.axis_size(axis)
    from_left = lax.ppermute(up, axis, [(i, (i + 1) % count) for i in range(count)])
    from_right = lax.ppermute(low, axis, [((i + 1) % count, i) for i in range(count)])
    return from_left, from_right


def exchange_pairs(values, axis, far):
    count = lax.axis_size(axis)
    assert count % 2 == 0
    swaps = []
    for k in range(far, count, 2):
        a, b = k, (k + 1) % count
        swaps += [(a, b), (b, a)]
    return lax.ppermute(values, axis, swaps)


def local(conserved, jacobian, metric, x_master, x_flip, z_master, z_flip):
    lanes = conserved.shape[-1]
    nodes = conserved.shape[1] * conserved.shape[2]
    assert conserved.shape[1:3] == (4, 4)
    cons = conserved.reshape(5, nodes, lanes)
    jac = jacobian.reshape(nodes, lanes)
    met = metric.reshape(9, nodes, lanes)
    xm, xf, zm, zf = [a.reshape(2, a.shape[-1]) for a in (x_master, x_flip, z_master, z_flip)]
    flag = (2, xm.shape[-1])
    nodal9, nodal5 = shaped(9, nodes, lanes), shaped(5, nodes, lanes)
    index = shaped(48, lanes, dtype=jnp.int32)
    matrix_shape = shaped(2 * lanes, 3 * lanes, dtype=jnp.bfloat16)
    nodal, flags, matrix, x_index, grad, low_z, up_z = call(
        first_kernel,
        [
            shaped(15, nodes, lanes),
            shaped(4, *flag, dtype=jnp.int32),
            matrix_shape,
            index,
            nodal9,
            shaped(80, lanes),
            shaped(80, lanes),
        ],
        *[pltpu.with_memory_space_constraint(a, pltpu.HBM) for a in (cons, jac, met, xm, xf, zm, zf)],
        in_specs=[pl.BlockSpec(memory_space=pltpu.HBM)] * 7,
        scratch=[pltpu.SemaphoreType.DMA((2,))],
    )
    left_z, right_z = exchange(low_z, up_z, "gz")
    z_index, x_back, x_face, near_one, far_one = call(
        first_cover,
        [index, index, shaped(72, lanes)] + [shaped(40, lanes)] * 2,
        nodal, flags, x_index, grad,
    )
    far_one = exchange_pairs(far_one, "gx", 1)
    grad, lift_z, near_two, far_two = call(
        second_kernel,
        [nodal9, shaped(72, lanes), shaped(96, lanes), shaped(56, lanes)],
        nodal, z_index, grad, x_face, near_one, left_z, right_z,
    )
    far_two = exchange_pairs(far_two, "gx", 1)
    near_two = exchange_pairs(near_two, "gx", 0)
    part, z_face, y_normal = call(
        second_cover,
        [nodal5, shaped(144, lanes), shaped(3, nodes, lanes)],
        nodal, z_index, lift_z, left_z, right_z,
    )
    part, x_other = call(
        third_cover,
        [nodal5, shaped(88, lanes)],
        nodal, x_back, grad, part, z_face, y_normal, matrix, far_one, near_two,
    )
    (rhs,) = call(
        third_kernel,
        [nodal5],
        nodal, x_back, z_index, part, x_other, z_face, near_two, far_two,
    )
    return rhs.reshape(conserved.shape)


def solution(mesh):
    in_specs = (
        P(None, "gx", "gz", None),
        P("gx", "gz", None),
        P(None, None, "gx", "gz", None),
        P("gx", "gz", None),
        P("gx", "gz", None),
        P("gx", "gz", None),
        P("gx", "gz", None),
    )
    out_specs = P(None, "gx", "gz", None)
    return jax.shard_map(local, mesh=mesh, in_specs=in_specs, out_specs=out_specs, check_vma=False)
```

```python
import math

import jax
import jax.numpy as jnp
import numpy as np
from jax import lax
from jax.experimental import pallas as pl
from jax.experimental.pallas import tpu as pltpu
from jax.sharding import PartitionSpec as P


gamma_gas = 1.4
visc_coef = 0.1
prandtl = 0.72
lift = 6.0
heat_coef = visc_coef * gamma_gas / ((gamma_gas - 1.0) * prandtl)
vmem_bytes = 8 << 20
whole = pl.BlockSpec(memory_space=pltpu.VMEM)


def node_table():
    points = np.array([-1.0, -math.sqrt(0.2), math.sqrt(0.2), 1.0])
    scales = np.array([np.prod([points[i] - points[k] for k in range(4) if k != i]) for i in range(4)])
    table = np.zeros((4, 4))
    for i in range(4):
        for k in range(4):
            if i != k:
                table[i, k] = scales[i] / (scales[k] * (points[i] - points[k]))
        table[i, i] = -np.sum(table[i])
    return table


def weak_table():
    table = node_table()
    table[0, 0] += lift
    table[3, 3] -= lift
    return table


def rows_of(lanes):
    return lax.broadcasted_iota(jnp.int32, (8, lanes), 0)


def lanes_of(lanes):
    return lax.broadcasted_iota(jnp.int32, (8, lanes), 1)


def pick4(index, values):
    out = jnp.full(index.shape, values[3], jnp.float32)
    for k in (2, 1, 0):
        out = jnp.where(index == k, jnp.float32(values[k]), out)
    return out


def shift_weights(index, table):
    weights = {}
    for shift in range(-3, 4):
        weights[shift] = pick4(index, [table[j, j - shift] if 0 <= j - shift < 4 else 0.0 for j in range(4)])
    return weights


def three_parts(values):
    parts = []
    for _ in range(3):
        part = values.astype(jnp.bfloat16)
        values = values - part.astype(jnp.float32)
        parts.append(part)
    return parts


class Frame:
    def __init__(self, lanes):
        self.lanes = lanes
        row = rows_of(lanes)
        lane = lanes_of(lanes)
        self.row, self.lane = row, lane
        self.low_half = row < 4
        self.point_row = row % 4
        self.point_lane = lane % 4

    def deriv_weights(self):
        table = weak_table()
        self.weights_z = shift_weights(self.point_row, table)
        self.weights_y = shift_weights(self.point_lane, table)
        pair = lambda top, bottom: jnp.where(self.low_half, jnp.float32(top), jnp.float32(bottom))
        self.weights_x = [
            [
                pair(table[2 * t, 2 * s], table[2 * t + 1, 2 * s + 1]),
                pair(table[2 * t, 2 * s + 1], table[2 * t + 1, 2 * s]),
            ]
            for t in range(2)
            for s in range(2)
        ]

    def swap(self, tile):
        return pltpu.roll(tile, 4, 0)

    def deriv_x(self, pair):
        a, b = pair
        a2, b2 = self.swap(a), self.swap(b)
        w = self.weights_x
        return [
            w[2 * t][0] * a + w[2 * t][1] * a2 + w[2 * t + 1][0] * b + w[2 * t + 1][1] * b2
            for t in range(2)
        ]

    def deriv_rows(self, tile):
        out = self.weights_z[0] * tile
        for shift in (-3, -2, -1, 1, 2, 3):
            out = out + self.weights_z[shift] * pltpu.roll(tile, shift % 8, 0)
        return out

    def lane_matrix(self):
        shape = (self.lanes, self.lanes)
        to = lax.broadcasted_iota(jnp.int32, shape, 1)
        gap = to - lax.broadcasted_iota(jnp.int32, shape, 0)
        full = jnp.zeros(shape, jnp.float32)
        for shift in range(-3, 4):
            full = jnp.where(gap == shift, jnp.broadcast_to(self.weights_y[shift][0:1], shape), full)
        high, middle, low = three_parts(full)
        top = jnp.concatenate([high, middle, high], 1)
        bottom = jnp.concatenate([high, middle, low], 1)
        return jnp.concatenate([top, bottom], 0)

    def deriv_lanes_all(self, tiles, matrix):
        high, middle, low = three_parts(jnp.concatenate(tiles, 0))
        n = self.lanes
        wide = jnp.dot(
            jnp.concatenate([high, middle], 1), matrix[:, : 2 * n], preferred_element_type=jnp.float32
        )
        rest = jnp.dot(
            jnp.concatenate([low, high], 1), matrix[:, 2 * n :], preferred_element_type=jnp.float32
        )
        out = wide[:, :n] + (wide[:, n:] + rest)
        return [out[8 * i : 8 * i + 8] for i in range(len(tiles))]

    def deriv_lanes(self, tile):
        out = self.weights_y[0] * tile
        for shift in (-3, -2, -1, 1, 2, 3):
            out = out + self.weights_y[shift] * pltpu.roll(tile, shift % self.lanes, 1)
        return out

    def face_x(self, pair):
        return jnp.where(self.low_half, pair[0], pair[1])

    def face_z(self, pair, swapped=False):
        side = jnp.where(self.low_half, 3, 0) if swapped else jnp.where(self.low_half, 0, 3)
        index = side + 4 * (self.point_row % 2)
        return jnp.where(self.point_row < 2, sub_gather(pair[0], index), sub_gather(pair[1], index))

    def spread_z(self, face):
        upper = jnp.where(self.point_row == 3, 4, 0)
        inner = jnp.where(self.low_half, 0, 1)
        return [sub_gather(face, upper + inner + 2 * t) for t in range(2)]

    def sides(self, low, up):
        return jnp.where(self.low_half, jnp.float32(low), jnp.float32(up))

    def sign_lanes(self):
        return jnp.where(
            self.point_lane == 3, jnp.float32(lift), jnp.where(self.point_lane == 0, jnp.float32(-lift), 0.0)
        )

    def sign_rows(self):
        return jnp.where(
            self.point_row == 3, jnp.float32(lift), jnp.where(self.point_row == 0, jnp.float32(-lift), 0.0)
        )


def sub_gather(tile, index):
    return jnp.take_along_axis(tile, index, axis=0)


def lane_gather(tile, index):
    return jnp.take_along_axis(tile, index, axis=1)


def primitive(state):
    inverse = 1.0 / state[0]
    velocity = [state[1 + j] * inverse for j in range(3)]
    kinetic = state[1] * velocity[0] + state[2] * velocity[1] + state[3] * velocity[2]
    pressure = (gamma_gas - 1.0) * (state[4] - 0.5 * kinetic)
    return velocity, pressure, pressure * inverse


def combos(values, rows):
    w0, w1, w2, w3 = values
    m0, m1, m2 = rows
    return [
        w0 * m0,
        w1 * m1,
        w2 * m2,
        w0 * m1 + w1 * m0,
        w0 * m2 + w2 * m0,
        w1 * m2 + w2 * m1,
        w3 * m0,
        w3 * m1,
        w3 * m2,
    ]


def plain_flux(state, velocity, pressure, normal):
    speed = velocity[0] * normal[0] + velocity[1] * normal[1] + velocity[2] * normal[2]
    out = [state[0] * speed]
    for j in range(3):
        out.append(state[1 + j] * speed + pressure * normal[j])
    out.append((state[4] + pressure) * speed)
    return out, speed


def traction(slopes, normal):
    m0, m1, m2 = normal
    spread = (visc_coef * 2.0 / 3.0) * (slopes[0] + slopes[1] + slopes[2])
    t00, t11, t22 = [2.0 * visc_coef * slopes[d] - spread for d in range(3)]
    t01, t02, t12 = [visc_coef * slopes[3 + d] for d in range(3)]
    return [
        t00 * m0 + t01 * m1 + t02 * m2,
        t01 * m0 + t11 * m1 + t12 * m2,
        t02 * m0 + t12 * m1 + t22 * m2,
        heat_coef * (slopes[6] * m0 + slopes[7] * m1 + slopes[8] * m2),
    ]


def drag_of(velocity, forces):
    work = velocity[0] * forces[0] + velocity[1] * forces[1] + velocity[2] * forces[2]
    return forces[:3] + [work + forces[3]]


def drag_flux(velocity, slopes, normal):
    forces = traction(slopes, normal)
    return drag_of(velocity, forces), forces[3]


def wave(speed, theta, normal_size):
    return jnp.abs(speed) + jnp.sqrt(gamma_gas * theta) * normal_size


def size_of(normal):
    return jnp.sqrt(normal[0] * normal[0] + normal[1] * normal[1] + normal[2] * normal[2])


def paired(frame, swapped_a, b):
    low = jnp.where(frame.low_half, b, swapped_a)
    up = jnp.where(frame.low_half, swapped_a, b)
    return low, up


def pack(frame, fields, low_ref, up_ref):
    fields = list(fields)
    if len(fields) % 2:
        fields.append(fields[-1])
    for g in range(len(fields) // 2):
        low, up = paired(frame, fields[2 * g], fields[2 * g + 1])
        low_ref[8 * g : 8 * g + 8, :] = low
        up_ref[8 * g : 8 * g + 8, :] = up


def unpack(frame, left_ref, right_ref, count):
    fields = []
    for g in range((count + 1) // 2):
        left = left_ref[8 * g : 8 * g + 8, :]
        right = right_ref[8 * g : 8 * g + 8, :]
        fields.append(jnp.where(frame.low_half, left, right))
        fields.append(jnp.where(frame.low_half, right, left))
    return fields[:count]


def first_of_pair(frame):
    return jnp.full((8, frame.lanes), lax.axis_index("gx") % 2) == 0


def pack_pairs(frame, fields, near_ref, far_ref):
    lower = first_of_pair(frame)
    fields = fields + [fields[-1]] * (len(fields) % 2)
    for g in range(len(fields) // 2):
        low, up = paired(frame, fields[2 * g], fields[2 * g + 1])
        near_ref[8 * g : 8 * g + 8, :] = jnp.where(lower, up, low)
        far_ref[8 * g : 8 * g + 8, :] = jnp.where(lower, low, up)


def unpack_pairs(frame, near_ref, far_ref, count):
    straight = first_of_pair(frame) == frame.low_half
    fields = []
    for g in range((count + 1) // 2):
        near = near_ref[8 * g : 8 * g + 8, :]
        far = far_ref[8 * g : 8 * g + 8, :]
        fields.append(jnp.where(straight, far, near))
        fields.append(jnp.where(straight, near, far))
    return fields[:count]


def spread_flags(frame, flags):
    count = flags.shape[-1]
    hit = lax.broadcasted_iota(jnp.int32, (count, frame.lanes), 0) == (
        lax.broadcasted_iota(jnp.int32, (count, frame.lanes), 1) // 4
    )
    wide = jnp.dot(
        flags.astype(jnp.float32), hit.astype(jnp.float32), preferred_element_type=jnp.float32
    )
    wide = (wide + 0.5).astype(jnp.int32)
    shape = (8, frame.lanes)
    return jnp.where(
        frame.low_half, jnp.broadcast_to(wide[0:1], shape), jnp.broadcast_to(wide[1:2], shape)
    )


def turn_indices(frame, code, forward_low):
    swap = (code & 4) != 0
    first = (code & 1) * 3
    second = ((code >> 1) & 1) * 3
    forward = frame.low_half if forward_low else jnp.logical_not(frame.low_half)
    flip_a = jnp.where(forward, second, first)
    flip_b = jnp.where(forward, first, second)
    row4, lane4 = frame.point_row, frame.point_lane
    lane_base = frame.lane - lane4
    row_base = frame.row - row4
    step1 = row_base + jnp.where(swap, (row4 - lane4) & 3, row4 ^ first)
    step2 = lane_base + jnp.where(swap, (row4 - (lane4 ^ flip_a)) & 3, lane4 ^ second)
    step3 = row_base + jnp.where(swap, ((lane4 ^ flip_a) + (row4 ^ flip_b)) & 3, row4)
    return step1, step2, step3


def turn(tile, indices):
    return sub_gather(lane_gather(sub_gather(tile, indices[0]), indices[1]), indices[2])


def store_indices(ref, indices, master):
    step1, step2, step3 = indices
    stack_tiles(ref, [step1, step2, step3, step1 ^ 4, master])


def load_indices(ref):
    step1, step2, step3, swapped1 = take_tiles(ref, 0, 4)
    return (step1, step2, step3), (swapped1, step2, step3)


def turn_all(fields, both, first=0):
    return [turn(p, both[(first + i) % 2]) for i, p in enumerate(fields)]


def straight(frame, fields):
    return [frame.swap(p) if i % 2 else p for i, p in enumerate(fields)]


def stack_tiles(ref, tiles):
    for i, tile in enumerate(tiles):
        ref[8 * i : 8 * i + 8, :] = tile


def take_tiles(ref, first, last):
    return [ref[8 * i : 8 * i + 8, :] for i in range(first, last)]


def load_pair(ref, f):
    return [ref[f, 0:8, :], ref[f, 8:16, :]]


def load_state(ref):
    pairs = [load_pair(ref, f) for f in range(5)]
    return [[pairs[f][t] for f in range(5)] for t in range(2)]


def load_rows(ref, g):
    pairs = [load_pair(ref, 3 * g + d) for d in range(3)]
    return [[pairs[d][t] for d in range(3)] for t in range(2)]


def by_field(tiles):
    return [[tiles[0][f], tiles[1][f]] for f in range(len(tiles[0]))]


def lane_partner(frame, tile, flip):
    step = jnp.where(frame.point_lane == 3, 1, -1)
    other = lane_gather(tile, jnp.clip(frame.lane + step, 0, frame.lanes - 1))
    wall = (frame.lane == 0) | (frame.lane == frame.lanes - 1)
    return jnp.where(wall, -tile if flip else tile, other)


def lane_normal(frame, rows):
    take_before = (frame.point_lane == 0) & (frame.lane != 0)
    return [jnp.where(take_before, pltpu.roll(r, 1, 1), r) for r in rows]


def split_nodal(nodal):
    return nodal.at[0:5], nodal.at[5], nodal.at[6:15]


def first_kernel(
    cons_in, jac_in, met_in, xm_in, xf_in, zm_in, zf_in,
    nodal, flags, matrix_out, x_index, grad_out, low_out, up_out, sems,
):
    cons, jac, met = split_nodal(nodal)
    flag_moves = [(a, flags.at[i]) for i, a in enumerate((xf_in, zf_in, xm_in, zm_in))]
    moves = [(cons_in, cons), (jac_in, jac)]
    moves += [(met_in.at[3 * g : 3 * g + 3], met.at[3 * g : 3 * g + 3]) for g in range(3)]
    for a, b in flag_moves:
        pltpu.make_async_copy(a, b, sems.at[0]).start()
    for a, b in moves:
        pltpu.make_async_copy(a, b, sems.at[1]).start()
    frame = Frame(cons.shape[-1])
    frame.deriv_weights()
    matrix_out[...] = frame.lane_matrix()
    pltpu.make_async_copy(flags, flags, sems.at[0]).wait()
    x_turn = turn_indices(frame, spread_flags(frame, flags[0]), True)
    z_turn = turn_indices(frame, spread_flags(frame, flags[1]), True)
    master = spread_flags(frame, flags[2])
    store_indices(x_index, x_turn, master)
    z_lead = spread_flags(frame, flags[3]) == 1
    pltpu.make_async_copy(nodal, nodal, sems.at[1]).wait()
    state = load_state(cons)
    state_f = by_field(state)
    lifted = []
    for t in range(2):
        velocity, _, theta = primitive(state[t])
        lifted.append(velocity + [theta])
    inverse = [1.0 / jac[0:8, :], 1.0 / jac[8:16, :]]
    z_turned = [turn(frame.face_z(p), z_turn) for p in state_f]
    x_turned = [turn(frame.face_x(p), x_turn) for p in state_f]
    rows = [load_rows(met, g) for g in range(3)]
    cx = by_field([combos(lifted[t], rows[0][t]) for t in range(2)])
    cz = by_field([combos(lifted[t], rows[1][t]) for t in range(2)])
    cy = by_field([combos(lifted[t], rows[2][t]) for t in range(2)])
    sign = frame.sign_lanes()
    lane_part = []
    for t in range(2):
        other = [lane_partner(frame, lifted[t][k], k < 3) for k in range(4)]
        mean = [0.5 * (lifted[t][k] + other[k]) for k in range(4)]
        lane_part.append(combos(mean, lane_normal(frame, rows[2][t])))
    grad = []
    dy = frame.deriv_lanes_all([cy[f][t] for f in range(9) for t in range(2)], matrix_out[...])
    for f in range(9):
        dx = frame.deriv_x(cx[f])
        grad.append(
            [
                dx[t]
                + frame.deriv_rows(cz[f][t])
                + dy[2 * f + t]
                + sign * lane_part[t][f]
                for t in range(2)
            ]
        )
    for f in range(9):
        for t in range(2):
            grad_out[f, 8 * t : 8 * t + 8, :] = grad[f][t]

    lead = master == 1
    own_rows = [frame.face_x(p) for p in by_field(rows[0])]
    turned_rows = [turn(p, x_turn) for p in own_rows]
    velocity, _, theta = primitive(x_turned)
    line = velocity + [theta]
    outer = (frame.point_row == 0) | (frame.point_row == 3)
    right = jnp.where(frame.point_row >= 2, 4, 0)
    picks = [right + jnp.where(frame.low_half, 3, 0), right + jnp.where(frame.low_half, 0, 3)]
    merge = lambda i, a, b: jnp.where(outer, sub_gather(a, picks[i % 2]), sub_gather(b, picks[i % 2]))
    zero = jnp.zeros_like(line[0])
    edges = [merge(1, line[0], line[1]), merge(0, line[2], line[3])]
    for d in range(3):
        edges.append(
            merge(d + 1, jnp.where(lead, turned_rows[d], zero), jnp.where(lead, own_rows[d], zero))
        )
    z_rows = [frame.face_z(p) for p in by_field(rows[1])]
    slots = [frame.face_z(p) for p in grad]
    known = [turn(p, z_turn) for p in z_rows] + traction(slots, z_rows)
    slots = [jnp.where(z_lead, a, b) for a, b in zip(known, slots)] + slots[7:]
    faces = z_turned + [frame.face_z(inverse)] + slots
    faces = [frame.swap(p) if i % 2 == 0 else p for i, p in enumerate(faces)]
    pack(frame, faces + edges, low_out, up_out)


def first_cover(
    nodal, flags, x_index, grad_in, z_index, x_back, face_out, near_out, far_out
):
    cons, jac, met = split_nodal(nodal)
    frame = Frame(cons.shape[-1])
    x_turn = load_indices(x_index)[0]
    fields = [load_pair(cons, f) for f in range(5)] + [load_pair(met, d) for d in range(3)]
    fields.append([1.0 / jac[0:8, :], 1.0 / jac[8:16, :]])
    fields = [turn(frame.face_x(p), x_turn) for p in fields]
    fields = [frame.swap(p) if i % 2 == 0 else p for i, p in enumerate(fields)]
    pack_pairs(frame, fields, near_out, far_out)
    for f in range(9):
        tile = frame.face_x(load_pair(grad_in, f))
        face_out[8 * f : 8 * f + 8, :] = frame.swap(tile) if f % 2 == 0 else tile
    z_turn = turn_indices(frame, spread_flags(frame, flags[1]), False)
    store_indices(z_index, z_turn, spread_flags(frame, flags[3]))
    x_return = turn_indices(frame, spread_flags(frame, flags[0]), False)
    store_indices(x_back, x_return, take_tiles(x_index, 4, 5)[0])


def mean_of(prim1, prim2):
    return [0.5 * (a + b) for a, b in zip(prim1[0] + [prim1[2]], prim2[0] + [prim2[2]])]


def second_kernel(
    nodal, z_index, grad_in, x_face, near_in, left, right,
    grad_out, part_out, near_out, far_out
):
    cons, _, met = split_nodal(nodal)
    frame = Frame(cons.shape[-1])
    lead = z_index[32:40, :] == 1
    got = unpack(frame, left, right, 20)
    other = straight(frame, got[:9])
    own = [frame.face_z(load_pair(cons, f)) for f in range(5)]
    own_rows = [frame.face_z(load_pair(met, 3 + d)) for d in range(3)]
    normal = [jnp.where(lead, own_rows[d], other[6 + d]) for d in range(3)]
    part = combos(mean_of(primitive(own), primitive(other[:5])), normal)
    stack_tiles(part_out, part)
    right = jnp.where(frame.point_row >= 2, 4, 0)
    across = [right + jnp.where(frame.low_half, 3, 0), right + jnp.where(frame.low_half, 0, 3)]
    sign = frame.sign_rows()
    fields = take_tiles(x_face, 0, 9)
    for f in range(9):
        fields[f] = fields[f] + sign * sub_gather(part[f], across[f % 2])
    odd = frame.point_row % 2
    high = jnp.where(frame.point_row >= 2, 4, 0)

    def passed(low):
        return high + jnp.where(low, odd, 3 - odd), high + jnp.where(low, 0, 3)

    pair_a, outer_a = passed(jnp.logical_not(frame.low_half))
    pair_b, outer_b = passed(frame.low_half)
    fields.append(sub_gather(got[15], pair_b ^ 4))
    fields.append(sub_gather(got[16], pair_a))
    fields.append(
        jnp.where(odd == 0, sub_gather(got[17], outer_b ^ 4), sub_gather(got[18], outer_b))
    )
    fields.append(sub_gather(got[19], outer_a ^ 4))
    static = near_in.shape[0]
    near_out[:static, :] = near_in[...]
    pack_pairs(frame, fields, near_out.at[static:], far_out)
    for f in range(9):
        spread = frame.spread_z(part[f])
        for t in range(2):
            grad_out[f, 8 * t : 8 * t + 8, :] = (
                grad_in[f, 8 * t : 8 * t + 8, :] + sign * spread[t]
            )


def plain_face(own, own_prim, other, other_prim, normal, side_sign):
    size = size_of(normal)
    flux1, speed1 = plain_flux(own, own_prim[0], own_prim[1], normal)
    flux2, speed2 = plain_flux(other, other_prim[0], other_prim[1], normal)
    fastest = jnp.maximum(wave(speed1, own_prim[2], size), wave(speed2, other_prim[2], size))
    half = 0.5 * side_sign * fastest
    return [0.5 * (flux1[c] + flux2[c]) - half * (other[c] - own[c]) for c in range(5)]


def second_cover(nodal, z_index, lift_in, left, right, part_out, face_out, normal_out):
    cons, _, met = split_nodal(nodal)
    frame = Frame(cons.shape[-1])
    lead = z_index[32:40, :] == 1
    both = load_indices(z_index)
    got = unpack(frame, left, right, 20)
    turned = straight(frame, got[:9])
    scale, *slots = turn_all(got[5:15], both, 5)
    other = turned[:5]
    other_prim = primitive(other)
    own = [frame.face_z(load_pair(cons, f)) for f in range(5)]
    own_rows = [frame.face_z(load_pair(met, 3 + d)) for d in range(3)]
    own_prim = primitive(own)
    normal = [jnp.where(lead, own_rows[d], turned[6 + d]) for d in range(3)]
    flux = plain_face(own, own_prim, other, other_prim, normal, frame.sides(-1.0, 1.0))
    sign = frame.sign_rows()
    plain_z = [frame.spread_z(flux[c]) for c in range(5)]
    face_sign = frame.sides(-lift, lift)
    forces = [jnp.where(lead, a, b) for a, b in zip(traction(slots, normal), slots[3:7])]
    lifts = traction([face_sign * p for p in take_tiles(lift_in, 0, 9)], normal)
    forces = [scale * (a - b) for a, b in zip(forces, lifts)]
    edge_scale = turn(sign, both[0]) * scale
    own_edge = jnp.where(frame.low_half, 0, 4) + jnp.where(frame.point_row >= 2, 2, 1)
    own_lines = [sub_gather(got[17 + d], own_edge if d == 1 else own_edge ^ 4) for d in range(3)]
    stack_tiles(
        face_out,
        own_prim[0]
        + other_prim[0]
        + [other_prim[2]]
        + normal
        + drag_of(other_prim[0], forces)
        + own_lines
        + [edge_scale],
    )

    frame.deriv_weights()
    state = load_state(cons)
    rows = [load_rows(met, g) for g in range(3)]
    sign_y = frame.sign_lanes()
    up_lane = frame.point_lane == 3
    wall = (frame.lane == 0) | (frame.lane == frame.lanes - 1)
    volume = []
    lane_flux = []
    for t in range(2):
        velocity, pressure, theta = primitive(state[t])
        volume.append([plain_flux(state[t], velocity, pressure, rows[g][t])[0] for g in range(3)])
        normal = lane_normal(frame, rows[2][t])
        for d in range(3):
            normal_out[d, 8 * t : 8 * t + 8, :] = normal[d]
        half, speed = plain_flux(state[t], velocity, pressure, normal)
        own_wave = wave(speed, theta, size_of(normal))
        fastest = jnp.maximum(own_wave, lane_partner(frame, own_wave, False))
        mirrored = [-half[0], half[1], half[2], half[3], -half[4]]
        direction = jnp.where(up_lane, jnp.float32(0.5), jnp.float32(-0.5)) * fastest
        result = []
        for c in range(5):
            other_half = jnp.where(wall, mirrored[c], lane_partner(frame, half[c], False))
            other_state = lane_partner(frame, state[t][c], 1 <= c <= 3)
            result.append(0.5 * (half[c] + other_half) - direction * (other_state - state[t][c]))
        lane_flux.append(result)
    for c in range(5):
        dx = frame.deriv_x([volume[t][0][c] for t in range(2)])
        for t in range(2):
            part_out[c, 8 * t : 8 * t + 8, :] = (
                sign * plain_z[c][t]
                + dx[t]
                + frame.deriv_rows(volume[t][1][c])
                + frame.deriv_lanes(volume[t][2][c])
                + sign_y * lane_flux[t][c]
            )


def third_cover(
    nodal, x_index, grad_in, part_in, z_face, y_normal, matrix, far_one, near_two, part_out, face_out
):
    cons, jac, met = split_nodal(nodal)
    frame = Frame(cons.shape[-1])
    frame.deriv_weights()
    state = load_state(cons)
    state_f = by_field(state)
    rows = [load_rows(met, g) for g in range(3)]
    inverse = [1.0 / jac[0:8, :], 1.0 / jac[8:16, :]]
    static = far_one.shape[0]
    x_lead = x_index[32:40, :] == 1
    turned = straight(frame, unpack_pairs(frame, near_two.at[:static], far_one, 9))
    face_sign = frame.sides(-lift, lift)

    own = [frame.face_x(p) for p in state_f]
    own_rows = [frame.face_x(p) for p in by_field(rows[0])]
    own_prim = primitive(own)
    other = turned[:5]
    other_prim = primitive(other)
    normal_x = [jnp.where(x_lead, own_rows[d], turned[5 + d]) for d in range(3)]
    part = combos(mean_of(own_prim, other_prim), normal_x)
    slopes = []
    for f in range(9):
        lifted_part = face_sign * part[f]
        zero = jnp.zeros_like(lifted_part)
        tiles = [
            grad_in[f, 0:8, :] + jnp.where(frame.low_half, lifted_part, zero),
            grad_in[f, 8:16, :] + jnp.where(frame.low_half, zero, lifted_part),
        ]
        slopes.append([tiles[t] * inverse[t] for t in range(2)])
    own_slopes = [frame.face_x(p) for p in slopes]
    flux_x = plain_face(own, own_prim, other, other_prim, normal_x, frame.sides(-1.0, 1.0))
    drag1 = drag_flux(own_prim[0], own_slopes, normal_x)[0]
    flux_x = [flux_x[0]] + [flux_x[1 + c] - 0.5 * drag1[c] for c in range(4)]
    lifts = traction([face_sign * p for p in part], normal_x)
    stack_tiles(face_out, other_prim[0] + normal_x + lifts + [turned[8]])

    face = take_tiles(z_face, 0, 18)
    normal_z = face[7:10]
    own_slopes = [frame.face_z(p) for p in slopes]
    drag1 = drag_flux(face[0:3], own_slopes, normal_z)[0]
    drag_z = [0.5 * (drag1[c] + face[10 + c]) for c in range(4)]

    slopes_t = [[slopes[f][t] for f in range(9)] for t in range(2)]
    sign_y = frame.sign_lanes()
    wall = (frame.lane == 0) | (frame.lane == frame.lanes - 1)
    volume = []
    lane_flux = []
    for t in range(2):
        velocity = primitive(state[t])[0]
        volume.append([drag_flux(velocity, slopes_t[t], rows[g][t])[0] for g in range(3)])
        normal = [y_normal[d, 8 * t : 8 * t + 8, :] for d in range(3)]
        half, heat = drag_flux(velocity, slopes_t[t], normal)
        mirrored = [half[0], half[1], half[2], 2.0 * heat - half[3]]
        result = []
        for c in range(4):
            other_half = jnp.where(wall, mirrored[c], lane_partner(frame, half[c], False))
            result.append(0.5 * (half[c] + other_half))
        lane_flux.append(result)
    row_sign = frame.sign_rows()
    dy = frame.deriv_lanes_all(
        [volume[t][2][k] for k in range(4) for t in range(2)], matrix[...]
    )
    for c in range(5):
        side = face_sign * flux_x[c]
        zero = jnp.zeros_like(side)
        sides = [jnp.where(frame.low_half, side, zero), jnp.where(frame.low_half, zero, side)]
        totals = [part_in[c, 8 * t : 8 * t + 8, :] + sides[t] for t in range(2)]
        if c > 0:
            k = c - 1
            dx = frame.deriv_x([volume[t][0][k] for t in range(2)])
            spread = frame.spread_z(drag_z[k])
            for t in range(2):
                totals[t] = totals[t] - (
                    dx[t]
                    + frame.deriv_rows(volume[t][1][k])
                    + dy[2 * k + t]
                    + sign_y * lane_flux[t][k]
                    + row_sign * spread[t]
                )
        for t in range(2):
            part_out[c, 8 * t : 8 * t + 8, :] = -totals[t] * inverse[t]


def edge_tiles(frame, face):
    zero = jnp.zeros_like(face)
    return [jnp.where(frame.low_half, face, zero), jnp.where(frame.low_half, zero, face)]


def third_kernel(nodal, x_index, z_index, part_in, x_face, z_face, near_two, far_two, out):
    _, jac, _ = split_nodal(nodal)
    frame = Frame(jac.shape[-1])
    static = near_two.shape[0] - far_two.shape[0]
    got = unpack_pairs(frame, near_two.at[static:], far_two, 13)
    other = take_tiles(x_face, 0, 11)
    slopes = turn_all(got[:9], load_indices(x_index))
    forces = traction(slopes, other[3:6])
    forces = [other[10] * (a - b) for a, b in zip(forces, other[6:10])]
    drag_x = drag_of(other[0:3], forces)

    edge_a = jnp.where(frame.low_half, 0, 2) + jnp.where(frame.point_row >= 2, 4, 0)
    edge_b = edge_a + 1
    lines = [
        sub_gather(got[9], edge_a ^ 4),
        sub_gather(got[9], edge_b ^ 4),
        sub_gather(got[10], edge_a),
        sub_gather(got[10], edge_b),
        sub_gather(got[11], edge_a ^ 4),
        sub_gather(got[11], edge_b ^ 4),
        sub_gather(got[12], edge_a),
    ]
    face = take_tiles(z_face, 0, 18)
    lines[4:] = [lines[4 + d] + face[14 + d] for d in range(3)]
    z_indices = load_indices(z_index)[0]
    lines = [turn(p, z_indices) for p in lines]
    mean = [0.5 * (a + b) for a, b in zip(face[3:7], lines[:4])]
    edge_slopes = [face[17] * p for p in combos(mean, lines[4:])]
    normal_z = face[7:10]
    drag_z = drag_flux(face[3:6], edge_slopes, normal_z)[0]
    half_sign = 0.5 * frame.sign_rows()
    half_face = frame.sides(-0.5 * lift, 0.5 * lift)
    for c in range(5):
        totals = [part_in[c, 8 * t : 8 * t + 8, :] for t in range(2)]
        if c > 0:
            spread = frame.spread_z(drag_z[c - 1])
            side = edge_tiles(frame, half_face * drag_x[c - 1])
            for t in range(2):
                scale = 1.0 / jac[8 * t : 8 * t + 8, :]
                totals[t] = totals[t] + scale * (half_sign * spread[t] + side[t])
        for t in range(2):
            out[c, 8 * t : 8 * t + 8, :] = totals[t]


def shaped(*shape, dtype=jnp.float32):
    return jax.ShapeDtypeStruct(shape, dtype)


def call(kernel, outs, *args, in_specs=None, scratch=()):
    return pl.pallas_call(
        kernel,
        out_shape=outs,
        in_specs=in_specs or [whole] * len(args),
        out_specs=[whole] * len(outs),
        scratch_shapes=scratch,
        compiler_params=pltpu.CompilerParams(vmem_limit_bytes=vmem_bytes),
        cost_estimate=pl.CostEstimate(flops=1_000_000, bytes_accessed=200_000, transcendentals=0),
    )(*args)


def exchange(low, up, axis):
    count = lax.axis_size(axis)
    from_left = lax.ppermute(up, axis, [(i, (i + 1) % count) for i in range(count)])
    from_right = lax.ppermute(low, axis, [((i + 1) % count, i) for i in range(count)])
    return from_left, from_right


def exchange_pairs(values, axis, far):
    count = lax.axis_size(axis)
    assert count % 2 == 0
    swaps = []
    for k in range(far, count, 2):
        a, b = k, (k + 1) % count
        swaps += [(a, b), (b, a)]
    return lax.ppermute(values, axis, swaps)


def local(conserved, jacobian, metric, x_master, x_flip, z_master, z_flip):
    lanes = conserved.shape[-1]
    nodes = conserved.shape[1] * conserved.shape[2]
    assert conserved.shape[1:3] == (4, 4)
    cons = conserved.reshape(5, nodes, lanes)
    jac = jacobian.reshape(nodes, lanes)
    met = metric.reshape(9, nodes, lanes)
    xm, xf, zm, zf = [a.reshape(2, a.shape[-1]) for a in (x_master, x_flip, z_master, z_flip)]
    flag = (2, xm.shape[-1])
    nodal9, nodal5 = shaped(9, nodes, lanes), shaped(5, nodes, lanes)
    index = shaped(40, lanes, dtype=jnp.int32)
    matrix_shape = shaped(2 * lanes, 3 * lanes, dtype=jnp.bfloat16)
    nodal, flags, matrix, x_index, grad, low_z, up_z = call(
        first_kernel,
        [
            shaped(15, nodes, lanes),
            shaped(4, *flag, dtype=jnp.int32),
            matrix_shape,
            index,
            nodal9,
            shaped(80, lanes),
            shaped(80, lanes),
        ],
        *[pltpu.with_memory_space_constraint(a, pltpu.HBM) for a in (cons, jac, met, xm, xf, zm, zf)],
        in_specs=[pl.BlockSpec(memory_space=pltpu.HBM)] * 7,
        scratch=[pltpu.SemaphoreType.DMA((2,))],
    )
    left_z, right_z = exchange(low_z, up_z, "gz")
    z_index, x_back, x_face, near_one, far_one = call(
        first_cover,
        [index, index, shaped(72, lanes)] + [shaped(40, lanes)] * 2,
        nodal, flags, x_index, grad,
    )
    far_one = exchange_pairs(far_one, "gx", 1)
    grad, lift_z, near_two, far_two = call(
        second_kernel,
        [nodal9, shaped(72, lanes), shaped(96, lanes), shaped(56, lanes)],
        nodal, z_index, grad, x_face, near_one, left_z, right_z,
    )
    far_two = exchange_pairs(far_two, "gx", 1)
    near_two = exchange_pairs(near_two, "gx", 0)
    part, z_face, y_normal = call(
        second_cover,
        [nodal5, shaped(144, lanes), shaped(3, nodes, lanes)],
        nodal, z_index, lift_z, left_z, right_z,
    )
    part, x_other = call(
        third_cover,
        [nodal5, shaped(88, lanes)],
        nodal, x_back, grad, part, z_face, y_normal, matrix, far_one, near_two,
    )
    (rhs,) = call(
        third_kernel,
        [nodal5],
        nodal, x_back, z_index, part, x_other, z_face, near_two, far_two,
    )
    return rhs.reshape(conserved.shape)


def solution(mesh):
    in_specs = (
        P(None, "gx", "gz", None),
        P("gx", "gz", None),
        P(None, None, "gx", "gz", None),
        P("gx", "gz", None),
        P("gx", "gz", None),
        P("gx", "gz", None),
        P("gx", "gz", None),
    )
    out_specs = P(None, "gx", "gz", None)
    return jax.shard_map(local, mesh=mesh, in_specs=in_specs, out_specs=out_specs, check_vma=False)
```

```python
import math

import jax
import jax.numpy as jnp
import numpy as np
from jax import lax
from jax.experimental import pallas as pl
from jax.experimental.pallas import tpu as pltpu
from jax.sharding import PartitionSpec as P


gamma_gas = 1.4
visc_coef = 0.1
prandtl = 0.72
lift = 6.0
heat_coef = visc_coef * gamma_gas / ((gamma_gas - 1.0) * prandtl)
vmem_bytes = 8 << 20
whole = pl.BlockSpec(memory_space=pltpu.VMEM)


def node_table():
    points = np.array([-1.0, -math.sqrt(0.2), math.sqrt(0.2), 1.0])
    scales = np.array([np.prod([points[i] - points[k] for k in range(4) if k != i]) for i in range(4)])
    table = np.zeros((4, 4))
    for i in range(4):
        for k in range(4):
            if i != k:
                table[i, k] = scales[i] / (scales[k] * (points[i] - points[k]))
        table[i, i] = -np.sum(table[i])
    return table


def weak_table():
    table = node_table()
    table[0, 0] += lift
    table[3, 3] -= lift
    return table


def rows_of(lanes):
    return lax.broadcasted_iota(jnp.int32, (8, lanes), 0)


def lanes_of(lanes):
    return lax.broadcasted_iota(jnp.int32, (8, lanes), 1)


def pick4(index, values):
    out = jnp.full(index.shape, values[3], jnp.float32)
    for k in (2, 1, 0):
        out = jnp.where(index == k, jnp.float32(values[k]), out)
    return out


def shift_weights(index, table):
    weights = {}
    for shift in range(-3, 4):
        weights[shift] = pick4(index, [table[j, j - shift] if 0 <= j - shift < 4 else 0.0 for j in range(4)])
    return weights


def three_parts(values):
    parts = []
    for _ in range(3):
        part = values.astype(jnp.bfloat16)
        values = values - part.astype(jnp.float32)
        parts.append(part)
    return parts


class Frame:
    def __init__(self, lanes):
        self.lanes = lanes
        row = rows_of(lanes)
        lane = lanes_of(lanes)
        self.row, self.lane = row, lane
        self.low_half = row < 4
        self.point_row = row % 4
        self.point_lane = lane % 4

    def deriv_weights(self):
        table = weak_table()
        self.weights_z = shift_weights(self.point_row, table)
        self.weights_y = shift_weights(self.point_lane, table)
        pair = lambda top, bottom: jnp.where(self.low_half, jnp.float32(top), jnp.float32(bottom))
        self.weights_x = [
            [
                pair(table[2 * t, 2 * s], table[2 * t + 1, 2 * s + 1]),
                pair(table[2 * t, 2 * s + 1], table[2 * t + 1, 2 * s]),
            ]
            for t in range(2)
            for s in range(2)
        ]

    def swap(self, tile):
        return pltpu.roll(tile, 4, 0)

    def deriv_x(self, pair):
        a, b = pair
        a2, b2 = self.swap(a), self.swap(b)
        w = self.weights_x
        return [
            w[2 * t][0] * a + w[2 * t][1] * a2 + w[2 * t + 1][0] * b + w[2 * t + 1][1] * b2
            for t in range(2)
        ]

    def deriv_rows(self, tile):
        out = self.weights_z[0] * tile
        for shift in (-3, -2, -1, 1, 2, 3):
            out = out + self.weights_z[shift] * pltpu.roll(tile, shift % 8, 0)
        return out

    def lane_matrix(self):
        shape = (self.lanes, self.lanes)
        to = lax.broadcasted_iota(jnp.int32, shape, 1)
        gap = to - lax.broadcasted_iota(jnp.int32, shape, 0)
        full = jnp.zeros(shape, jnp.float32)
        for shift in range(-3, 4):
            full = jnp.where(gap == shift, jnp.broadcast_to(self.weights_y[shift][0:1], shape), full)
        high, middle, low = three_parts(full)
        top = jnp.concatenate([high, middle, high], 1)
        bottom = jnp.concatenate([high, middle, low], 1)
        return jnp.concatenate([top, bottom], 0)

    def deriv_lanes_all(self, tiles, matrix):
        high, middle, low = three_parts(jnp.concatenate(tiles, 0))
        n = self.lanes
        wide = jnp.dot(
            jnp.concatenate([high, middle], 1), matrix[:, : 2 * n], preferred_element_type=jnp.float32
        )
        rest = jnp.dot(
            jnp.concatenate([low, high], 1), matrix[:, 2 * n :], preferred_element_type=jnp.float32
        )
        out = wide[:, :n] + (wide[:, n:] + rest)
        return [out[8 * i : 8 * i + 8] for i in range(len(tiles))]

    def deriv_lanes(self, tile):
        out = self.weights_y[0] * tile
        for shift in (-3, -2, -1, 1, 2, 3):
            out = out + self.weights_y[shift] * pltpu.roll(tile, shift % self.lanes, 1)
        return out

    def face_x(self, pair):
        return jnp.where(self.low_half, pair[0], pair[1])

    def face_z(self, pair, swapped=False):
        side = jnp.where(self.low_half, 3, 0) if swapped else jnp.where(self.low_half, 0, 3)
        index = side + 4 * (self.point_row % 2)
        return jnp.where(self.point_row < 2, sub_gather(pair[0], index), sub_gather(pair[1], index))

    def spread_z(self, face):
        upper = jnp.where(self.point_row == 3, 4, 0)
        inner = jnp.where(self.low_half, 0, 1)
        return [sub_gather(face, upper + inner + 2 * t) for t in range(2)]

    def sides(self, low, up):
        return jnp.where(self.low_half, jnp.float32(low), jnp.float32(up))

    def sign_lanes(self):
        return jnp.where(
            self.point_lane == 3, jnp.float32(lift), jnp.where(self.point_lane == 0, jnp.float32(-lift), 0.0)
        )

    def sign_rows(self):
        return jnp.where(
            self.point_row == 3, jnp.float32(lift), jnp.where(self.point_row == 0, jnp.float32(-lift), 0.0)
        )


def sub_gather(tile, index):
    return jnp.take_along_axis(tile, index, axis=0)


def lane_gather(tile, index):
    return jnp.take_along_axis(tile, index, axis=1)


def primitive(state):
    inverse = 1.0 / state[0]
    velocity = [state[1 + j] * inverse for j in range(3)]
    kinetic = state[1] * velocity[0] + state[2] * velocity[1] + state[3] * velocity[2]
    pressure = (gamma_gas - 1.0) * (state[4] - 0.5 * kinetic)
    return velocity, pressure, pressure * inverse


def combos(values, rows):
    w0, w1, w2, w3 = values
    m0, m1, m2 = rows
    return [
        w0 * m0,
        w1 * m1,
        w2 * m2,
        w0 * m1 + w1 * m0,
        w0 * m2 + w2 * m0,
        w1 * m2 + w2 * m1,
        w3 * m0,
        w3 * m1,
        w3 * m2,
    ]


def plain_flux(state, velocity, pressure, normal):
    speed = velocity[0] * normal[0] + velocity[1] * normal[1] + velocity[2] * normal[2]
    out = [state[0] * speed]
    for j in range(3):
        out.append(state[1 + j] * speed + pressure * normal[j])
    out.append((state[4] + pressure) * speed)
    return out, speed


def traction(slopes, normal):
    m0, m1, m2 = normal
    spread = (visc_coef * 2.0 / 3.0) * (slopes[0] + slopes[1] + slopes[2])
    t00, t11, t22 = [2.0 * visc_coef * slopes[d] - spread for d in range(3)]
    t01, t02, t12 = [visc_coef * slopes[3 + d] for d in range(3)]
    return [
        t00 * m0 + t01 * m1 + t02 * m2,
        t01 * m0 + t11 * m1 + t12 * m2,
        t02 * m0 + t12 * m1 + t22 * m2,
        heat_coef * (slopes[6] * m0 + slopes[7] * m1 + slopes[8] * m2),
    ]


def drag_of(velocity, forces):
    work = velocity[0] * forces[0] + velocity[1] * forces[1] + velocity[2] * forces[2]
    return forces[:3] + [work + forces[3]]


def drag_flux(velocity, slopes, normal):
    forces = traction(slopes, normal)
    return drag_of(velocity, forces), forces[3]


def wave(speed, theta, normal_size):
    return jnp.abs(speed) + jnp.sqrt(gamma_gas * theta) * normal_size


def size_of(normal):
    return jnp.sqrt(normal[0] * normal[0] + normal[1] * normal[1] + normal[2] * normal[2])


def paired(frame, swapped_a, b):
    low = jnp.where(frame.low_half, b, swapped_a)
    up = jnp.where(frame.low_half, swapped_a, b)
    return low, up


def pack(frame, fields, low_ref, up_ref):
    fields = list(fields)
    if len(fields) % 2:
        fields.append(fields[-1])
    for g in range(len(fields) // 2):
        low, up = paired(frame, fields[2 * g], fields[2 * g + 1])
        low_ref[8 * g : 8 * g + 8, :] = low
        up_ref[8 * g : 8 * g + 8, :] = up


def unpack(frame, left_ref, right_ref, count):
    fields = []
    for g in range((count + 1) // 2):
        left = left_ref[8 * g : 8 * g + 8, :]
        right = right_ref[8 * g : 8 * g + 8, :]
        fields.append(jnp.where(frame.low_half, left, right))
        fields.append(jnp.where(frame.low_half, right, left))
    return fields[:count]


def first_of_pair(frame):
    return jnp.full((8, frame.lanes), lax.axis_index("gx") & 1) == 0


def pack_pairs(frame, fields, near_ref, far_ref):
    lower = first_of_pair(frame)
    fields = fields + [fields[-1]] * (len(fields) % 2)
    for g in range(len(fields) // 2):
        low, up = paired(frame, fields[2 * g], fields[2 * g + 1])
        near_ref[8 * g : 8 * g + 8, :] = jnp.where(lower, up, low)
        far_ref[8 * g : 8 * g + 8, :] = jnp.where(lower, low, up)


def unpack_pairs(frame, near_ref, far_ref, count):
    straight = first_of_pair(frame) == frame.low_half
    fields = []
    for g in range((count + 1) // 2):
        near = near_ref[8 * g : 8 * g + 8, :]
        far = far_ref[8 * g : 8 * g + 8, :]
        fields.append(jnp.where(straight, far, near))
        fields.append(jnp.where(straight, near, far))
    return fields[:count]


def spread_flags(frame, flags):
    count = flags.shape[-1]
    hit = lax.broadcasted_iota(jnp.int32, (count, frame.lanes), 0) == (
        lax.broadcasted_iota(jnp.int32, (count, frame.lanes), 1) // 4
    )
    wide = jnp.dot(
        flags.astype(jnp.float32), hit.astype(jnp.float32), preferred_element_type=jnp.float32
    )
    wide = (wide + 0.5).astype(jnp.int32)
    shape = (8, frame.lanes)
    return jnp.where(
        frame.low_half, jnp.broadcast_to(wide[0:1], shape), jnp.broadcast_to(wide[1:2], shape)
    )


def turn_indices(frame, code, forward_low):
    swap = (code & 4) != 0
    first = (code & 1) * 3
    second = ((code >> 1) & 1) * 3
    forward = frame.low_half if forward_low else jnp.logical_not(frame.low_half)
    flip_a = jnp.where(forward, second, first)
    flip_b = jnp.where(forward, first, second)
    row4, lane4 = frame.point_row, frame.point_lane
    lane_base = frame.lane - lane4
    row_base = frame.row - row4
    step1 = row_base + jnp.where(swap, (row4 - lane4) & 3, row4 ^ first)
    step2 = lane_base + jnp.where(swap, (row4 - (lane4 ^ flip_a)) & 3, lane4 ^ second)
    step3 = row_base + jnp.where(swap, ((lane4 ^ flip_a) + (row4 ^ flip_b)) & 3, row4)
    return step1, step2, step3


def turn(tile, indices):
    return sub_gather(lane_gather(sub_gather(tile, indices[0]), indices[1]), indices[2])


def store_indices(ref, indices, master):
    step1, step2, step3 = indices
    stack_tiles(ref, [step1, step2, step3, step1 ^ 4, master])


def load_indices(ref):
    step1, step2, step3, swapped1 = take_tiles(ref, 0, 4)
    return (step1, step2, step3), (swapped1, step2, step3)


def turn_all(fields, both, first=0):
    return [turn(p, both[(first + i) % 2]) for i, p in enumerate(fields)]


def straight(frame, fields):
    return [frame.swap(p) if i % 2 else p for i, p in enumerate(fields)]


def stack_tiles(ref, tiles):
    for i, tile in enumerate(tiles):
        ref[8 * i : 8 * i + 8, :] = tile


def take_tiles(ref, first, last):
    return [ref[8 * i : 8 * i + 8, :] for i in range(first, last)]


def load_pair(ref, f):
    return [ref[f, 0:8, :], ref[f, 8:16, :]]


def load_state(ref):
    pairs = [load_pair(ref, f) for f in range(5)]
    return [[pairs[f][t] for f in range(5)] for t in range(2)]


def load_rows(ref, g):
    pairs = [load_pair(ref, 3 * g + d) for d in range(3)]
    return [[pairs[d][t] for d in range(3)] for t in range(2)]


def by_field(tiles):
    return [[tiles[0][f], tiles[1][f]] for f in range(len(tiles[0]))]


def lane_partner(frame, tile, flip):
    step = jnp.where(frame.point_lane == 3, 1, -1)
    other = lane_gather(tile, jnp.clip(frame.lane + step, 0, frame.lanes - 1))
    wall = (frame.lane == 0) | (frame.lane == frame.lanes - 1)
    return jnp.where(wall, -tile if flip else tile, other)


def lane_normal(frame, rows):
    take_before = (frame.point_lane == 0) & (frame.lane != 0)
    return [jnp.where(take_before, pltpu.roll(r, 1, 1), r) for r in rows]


def split_nodal(nodal):
    return nodal.at[0:5], nodal.at[5], nodal.at[6:15]


def first_kernel(
    cons_in, jac_in, met_in, xm_in, xf_in, zm_in, zf_in,
    nodal, flags, matrix_out, x_index, low_out, up_out, sems,
):
    cons, jac, met = split_nodal(nodal)
    flag_moves = [(a, flags.at[i]) for i, a in enumerate((xf_in, zf_in, xm_in, zm_in))]
    moves = [(cons_in, cons), (jac_in, jac)]
    moves += [(met_in.at[3 * g : 3 * g + 3], met.at[3 * g : 3 * g + 3]) for g in range(3)]
    for a, b in flag_moves:
        pltpu.make_async_copy(a, b, sems.at[0]).start()
    for a, b in moves:
        pltpu.make_async_copy(a, b, sems.at[1]).start()
    frame = Frame(cons.shape[-1])
    frame.deriv_weights()
    matrix_out[...] = frame.lane_matrix()
    pltpu.make_async_copy(flags, flags, sems.at[0]).wait()
    x_turn = turn_indices(frame, spread_flags(frame, flags[0]), True)
    z_turn = turn_indices(frame, spread_flags(frame, flags[1]), True)
    master = spread_flags(frame, flags[2])
    store_indices(x_index, x_turn, master)
    z_lead = spread_flags(frame, flags[3]) == 1
    pltpu.make_async_copy(nodal, nodal, sems.at[1]).wait()
    state_f = by_field(load_state(cons))
    rows_f = [by_field(load_rows(met, g)) for g in range(3)]
    inverse = [1.0 / jac[0:8, :], 1.0 / jac[8:16, :]]
    own_z = [frame.face_z(p) for p in state_f]
    z_turned = [turn(p, z_turn) for p in own_z]
    x_turned = [turn(frame.face_x(p), x_turn) for p in state_f]
    velocity, _, theta = primitive(own_z)
    lifted = velocity + [theta]
    face_rows = [[frame.face_z(p) for p in rows_f[g]] for g in range(3)]
    across = frame.deriv_lanes_all(combos(lifted, face_rows[2]), matrix_out[...])
    along = [frame.deriv_rows(p) for p in combos(lifted, face_rows[0])]
    through = []
    for t in range(2):
        velocity, _, theta = primitive([p[t] for p in state_f])
        through.append(combos(velocity + [theta], [p[t] for p in rows_f[1]]))
    through = [frame.face_z([frame.deriv_rows(p) for p in pair]) for pair in by_field(through)]
    other = [lane_partner(frame, lifted[k], k < 3) for k in range(4)]
    mean = [0.5 * (a + b) for a, b in zip(lifted, other)]
    walls = combos(mean, lane_normal(frame, face_rows[2]))
    sign = frame.sign_lanes()
    slots = [
        a + b + c + sign * d for a, b, c, d in zip(along, through, across, walls)
    ]

    lead = master == 1
    own_rows = [frame.face_x(p) for p in rows_f[0]]
    turned_rows = [turn(p, x_turn) for p in own_rows]
    velocity, _, theta = primitive(x_turned)
    line = velocity + [theta]
    outer = (frame.point_row == 0) | (frame.point_row == 3)
    right = jnp.where(frame.point_row >= 2, 4, 0)
    picks = [right + jnp.where(frame.low_half, 3, 0), right + jnp.where(frame.low_half, 0, 3)]
    merge = lambda i, a, b: jnp.where(outer, sub_gather(a, picks[i % 2]), sub_gather(b, picks[i % 2]))
    zero = jnp.zeros_like(line[0])
    edges = [merge(1, line[0], line[1]), merge(0, line[2], line[3])]
    for d in range(3):
        edges.append(
            merge(d + 1, jnp.where(lead, turned_rows[d], zero), jnp.where(lead, own_rows[d], zero))
        )
    z_rows = face_rows[1]
    known = [turn(p, z_turn) for p in z_rows] + traction(slots, z_rows)
    slots = [jnp.where(z_lead, a, b) for a, b in zip(known, slots)] + slots[7:]
    faces = z_turned + [frame.face_z(inverse)] + slots
    faces = [frame.swap(p) if i % 2 == 0 else p for i, p in enumerate(faces)]
    pack(frame, faces + edges, low_out, up_out)


def first_cover(
    nodal, flags, matrix, x_index, grad_out, z_index, x_back, face_out, near_out, far_out
):
    cons, jac, met = split_nodal(nodal)
    frame = Frame(cons.shape[-1])
    x_turn = load_indices(x_index)[0]
    fields = [load_pair(cons, f) for f in range(5)] + [load_pair(met, d) for d in range(3)]
    fields.append([1.0 / jac[0:8, :], 1.0 / jac[8:16, :]])
    fields = [turn(frame.face_x(p), x_turn) for p in fields]
    fields = [frame.swap(p) if i % 2 == 0 else p for i, p in enumerate(fields)]
    pack_pairs(frame, fields, near_out, far_out)
    frame.deriv_weights()
    state = load_state(cons)
    rows = [load_rows(met, g) for g in range(3)]
    lifted = []
    for t in range(2):
        velocity, _, theta = primitive(state[t])
        lifted.append(velocity + [theta])
    cx = by_field([combos(lifted[t], rows[0][t]) for t in range(2)])
    cz = by_field([combos(lifted[t], rows[1][t]) for t in range(2)])
    cy = by_field([combos(lifted[t], rows[2][t]) for t in range(2)])
    sign = frame.sign_lanes()
    lane_part = []
    for t in range(2):
        other = [lane_partner(frame, lifted[t][k], k < 3) for k in range(4)]
        mean = [0.5 * (lifted[t][k] + other[k]) for k in range(4)]
        lane_part.append(combos(mean, lane_normal(frame, rows[2][t])))
    grad = []
    dy = frame.deriv_lanes_all([cy[f][t] for f in range(9) for t in range(2)], matrix[...])
    for f in range(9):
        dx = frame.deriv_x(cx[f])
        grad.append(
            [
                dx[t]
                + frame.deriv_rows(cz[f][t])
                + dy[2 * f + t]
                + sign * lane_part[t][f]
                for t in range(2)
            ]
        )
    for f in range(9):
        for t in range(2):
            grad_out[f, 8 * t : 8 * t + 8, :] = grad[f][t]
    for f in range(9):
        tile = frame.face_x(grad[f])
        face_out[8 * f : 8 * f + 8, :] = frame.swap(tile) if f % 2 == 0 else tile
    z_turn = turn_indices(frame, spread_flags(frame, flags[1]), False)
    store_indices(z_index, z_turn, spread_flags(frame, flags[3]))
    x_return = turn_indices(frame, spread_flags(frame, flags[0]), False)
    store_indices(x_back, x_return, take_tiles(x_index, 4, 5)[0])


def mean_of(prim1, prim2):
    return [0.5 * (a + b) for a, b in zip(prim1[0] + [prim1[2]], prim2[0] + [prim2[2]])]


def second_kernel(
    nodal, z_index, grad_in, x_face, near_in, left, right,
    grad_out, part_out, near_out, far_out
):
    cons, _, met = split_nodal(nodal)
    frame = Frame(cons.shape[-1])
    lead = z_index[32:40, :] == 1
    got = unpack(frame, left, right, 20)
    other = straight(frame, got[:9])
    own = [frame.face_z(load_pair(cons, f)) for f in range(5)]
    own_rows = [frame.face_z(load_pair(met, 3 + d)) for d in range(3)]
    normal = [jnp.where(lead, own_rows[d], other[6 + d]) for d in range(3)]
    part = combos(mean_of(primitive(own), primitive(other[:5])), normal)
    stack_tiles(part_out, part)
    right = jnp.where(frame.point_row >= 2, 4, 0)
    across = [right + jnp.where(frame.low_half, 3, 0), right + jnp.where(frame.low_half, 0, 3)]
    sign = frame.sign_rows()
    fields = take_tiles(x_face, 0, 9)
    for f in range(9):
        fields[f] = fields[f] + sign * sub_gather(part[f], across[f % 2])
    odd = frame.point_row % 2
    high = jnp.where(frame.point_row >= 2, 4, 0)

    def passed(low):
        return high + jnp.where(low, odd, 3 - odd), high + jnp.where(low, 0, 3)

    pair_a, outer_a = passed(jnp.logical_not(frame.low_half))
    pair_b, outer_b = passed(frame.low_half)
    fields.append(sub_gather(got[15], pair_b ^ 4))
    fields.append(sub_gather(got[16], pair_a))
    fields.append(
        jnp.where(odd == 0, sub_gather(got[17], outer_b ^ 4), sub_gather(got[18], outer_b))
    )
    fields.append(sub_gather(got[19], outer_a ^ 4))
    static = near_in.shape[0]
    near_out[:static, :] = near_in[...]
    pack_pairs(frame, fields, near_out.at[static:], far_out)
    for f in range(9):
        spread = frame.spread_z(part[f])
        for t in range(2):
            grad_out[f, 8 * t : 8 * t + 8, :] = (
                grad_in[f, 8 * t : 8 * t + 8, :] + sign * spread[t]
            )


def plain_face(own, own_prim, other, other_prim, normal, side_sign):
    size = size_of(normal)
    flux1, speed1 = plain_flux(own, own_prim[0], own_prim[1], normal)
    flux2, speed2 = plain_flux(other, other_prim[0], other_prim[1], normal)
    fastest = jnp.maximum(wave(speed1, own_prim[2], size), wave(speed2, other_prim[2], size))
    half = 0.5 * side_sign * fastest
    return [0.5 * (flux1[c] + flux2[c]) - half * (other[c] - own[c]) for c in range(5)]


def second_cover(nodal, z_index, lift_in, left, right, part_out, face_out, normal_out):
    cons, _, met = split_nodal(nodal)
    frame = Frame(cons.shape[-1])
    lead = z_index[32:40, :] == 1
    both = load_indices(z_index)
    got = unpack(frame, left, right, 20)
    turned = straight(frame, got[:9])
    scale, *slots = turn_all(got[5:15], both, 5)
    other = turned[:5]
    other_prim = primitive(other)
    own = [frame.face_z(load_pair(cons, f)) for f in range(5)]
    own_rows = [frame.face_z(load_pair(met, 3 + d)) for d in range(3)]
    own_prim = primitive(own)
    normal = [jnp.where(lead, own_rows[d], turned[6 + d]) for d in range(3)]
    flux = plain_face(own, own_prim, other, other_prim, normal, frame.sides(-1.0, 1.0))
    sign = frame.sign_rows()
    plain_z = [frame.spread_z(flux[c]) for c in range(5)]
    face_sign = frame.sides(-lift, lift)
    forces = [jnp.where(lead, a, b) for a, b in zip(traction(slots, normal), slots[3:7])]
    lifts = traction([face_sign * p for p in take_tiles(lift_in, 0, 9)], normal)
    forces = [scale * (a - b) for a, b in zip(forces, lifts)]
    edge_scale = turn(sign, both[0]) * scale
    own_edge = jnp.where(frame.low_half, 0, 4) + jnp.where(frame.point_row >= 2, 2, 1)
    own_lines = [sub_gather(got[17 + d], own_edge if d == 1 else own_edge ^ 4) for d in range(3)]
    stack_tiles(
        face_out,
        own_prim[0]
        + other_prim[0]
        + [other_prim[2]]
        + normal
        + drag_of(other_prim[0], forces)
        + own_lines
        + [edge_scale],
    )

    frame.deriv_weights()
    state = load_state(cons)
    rows = [load_rows(met, g) for g in range(3)]
    sign_y = frame.sign_lanes()
    up_lane = frame.point_lane == 3
    wall = (frame.lane == 0) | (frame.lane == frame.lanes - 1)
    volume = []
    lane_flux = []
    for t in range(2):
        velocity, pressure, theta = primitive(state[t])
        volume.append([plain_flux(state[t], velocity, pressure, rows[g][t])[0] for g in range(3)])
        normal = lane_normal(frame, rows[2][t])
        for d in range(3):
            normal_out[d, 8 * t : 8 * t + 8, :] = normal[d]
        half, speed = plain_flux(state[t], velocity, pressure, normal)
        own_wave = wave(speed, theta, size_of(normal))
        fastest = jnp.maximum(own_wave, lane_partner(frame, own_wave, False))
        mirrored = [-half[0], half[1], half[2], half[3], -half[4]]
        direction = jnp.where(up_lane, jnp.float32(0.5), jnp.float32(-0.5)) * fastest
        result = []
        for c in range(5):
            other_half = jnp.where(wall, mirrored[c], lane_partner(frame, half[c], False))
            other_state = lane_partner(frame, state[t][c], 1 <= c <= 3)
            result.append(0.5 * (half[c] + other_half) - direction * (other_state - state[t][c]))
        lane_flux.append(result)
    for c in range(5):
        dx = frame.deriv_x([volume[t][0][c] for t in range(2)])
        for t in range(2):
            part_out[c, 8 * t : 8 * t + 8, :] = (
                sign * plain_z[c][t]
                + dx[t]
                + frame.deriv_rows(volume[t][1][c])
                + frame.deriv_lanes(volume[t][2][c])
                + sign_y * lane_flux[t][c]
            )


def third_cover(
    nodal, x_index, grad_in, part_in, z_face, y_normal, matrix, far_one, near_two, part_out, face_out
):
    cons, jac, met = split_nodal(nodal)
    frame = Frame(cons.shape[-1])
    frame.deriv_weights()
    state = load_state(cons)
    state_f = by_field(state)
    rows = [load_rows(met, g) for g in range(3)]
    inverse = [1.0 / jac[0:8, :], 1.0 / jac[8:16, :]]
    static = far_one.shape[0]
    x_lead = x_index[32:40, :] == 1
    turned = straight(frame, unpack_pairs(frame, near_two.at[:static], far_one, 9))
    face_sign = frame.sides(-lift, lift)

    own = [frame.face_x(p) for p in state_f]
    own_rows = [frame.face_x(p) for p in by_field(rows[0])]
    own_prim = primitive(own)
    other = turned[:5]
    other_prim = primitive(other)
    normal_x = [jnp.where(x_lead, own_rows[d], turned[5 + d]) for d in range(3)]
    part = combos(mean_of(own_prim, other_prim), normal_x)
    slopes = []
    for f in range(9):
        lifted_part = face_sign * part[f]
        zero = jnp.zeros_like(lifted_part)
        tiles = [
            grad_in[f, 0:8, :] + jnp.where(frame.low_half, lifted_part, zero),
            grad_in[f, 8:16, :] + jnp.where(frame.low_half, zero, lifted_part),
        ]
        slopes.append([tiles[t] * inverse[t] for t in range(2)])
    own_slopes = [frame.face_x(p) for p in slopes]
    flux_x = plain_face(own, own_prim, other, other_prim, normal_x, frame.sides(-1.0, 1.0))
    drag1 = drag_flux(own_prim[0], own_slopes, normal_x)[0]
    flux_x = [flux_x[0]] + [flux_x[1 + c] - 0.5 * drag1[c] for c in range(4)]
    lifts = traction([face_sign * p for p in part], normal_x)
    stack_tiles(face_out, other_prim[0] + normal_x + lifts + [turned[8]])

    face = take_tiles(z_face, 0, 18)
    normal_z = face[7:10]
    own_slopes = [frame.face_z(p) for p in slopes]
    drag1 = drag_flux(face[0:3], own_slopes, normal_z)[0]
    drag_z = [0.5 * (drag1[c] + face[10 + c]) for c in range(4)]

    slopes_t = [[slopes[f][t] for f in range(9)] for t in range(2)]
    sign_y = frame.sign_lanes()
    wall = (frame.lane == 0) | (frame.lane == frame.lanes - 1)
    volume = []
    lane_flux = []
    for t in range(2):
        velocity = primitive(state[t])[0]
        volume.append([drag_flux(velocity, slopes_t[t], rows[g][t])[0] for g in range(3)])
        normal = [y_normal[d, 8 * t : 8 * t + 8, :] for d in range(3)]
        half, heat = drag_flux(velocity, slopes_t[t], normal)
        mirrored = [half[0], half[1], half[2], 2.0 * heat - half[3]]
        result = []
        for c in range(4):
            other_half = jnp.where(wall, mirrored[c], lane_partner(frame, half[c], False))
            result.append(0.5 * (half[c] + other_half))
        lane_flux.append(result)
    row_sign = frame.sign_rows()
    dy = frame.deriv_lanes_all(
        [volume[t][2][k] for k in range(4) for t in range(2)], matrix[...]
    )
    for c in range(5):
        side = face_sign * flux_x[c]
        zero = jnp.zeros_like(side)
        sides = [jnp.where(frame.low_half, side, zero), jnp.where(frame.low_half, zero, side)]
        totals = [part_in[c, 8 * t : 8 * t + 8, :] + sides[t] for t in range(2)]
        if c > 0:
            k = c - 1
            dx = frame.deriv_x([volume[t][0][k] for t in range(2)])
            spread = frame.spread_z(drag_z[k])
            for t in range(2):
                totals[t] = totals[t] - (
                    dx[t]
                    + frame.deriv_rows(volume[t][1][k])
                    + dy[2 * k + t]
                    + sign_y * lane_flux[t][k]
                    + row_sign * spread[t]
                )
        for t in range(2):
            part_out[c, 8 * t : 8 * t + 8, :] = -totals[t] * inverse[t]


def edge_tiles(frame, face):
    zero = jnp.zeros_like(face)
    return [jnp.where(frame.low_half, face, zero), jnp.where(frame.low_half, zero, face)]


def third_kernel(nodal, x_index, z_index, part_in, x_face, z_face, near_two, far_two, out):
    _, jac, _ = split_nodal(nodal)
    frame = Frame(jac.shape[-1])
    static = near_two.shape[0] - far_two.shape[0]
    got = unpack_pairs(frame, near_two.at[static:], far_two, 13)
    other = take_tiles(x_face, 0, 11)
    slopes = turn_all(got[:9], load_indices(x_index))
    forces = traction(slopes, other[3:6])
    forces = [other[10] * (a - b) for a, b in zip(forces, other[6:10])]
    drag_x = drag_of(other[0:3], forces)

    edge_a = jnp.where(frame.low_half, 0, 2) + jnp.where(frame.point_row >= 2, 4, 0)
    edge_b = edge_a + 1
    lines = [
        sub_gather(got[9], edge_a ^ 4),
        sub_gather(got[9], edge_b ^ 4),
        sub_gather(got[10], edge_a),
        sub_gather(got[10], edge_b),
        sub_gather(got[11], edge_a ^ 4),
        sub_gather(got[11], edge_b ^ 4),
        sub_gather(got[12], edge_a),
    ]
    face = take_tiles(z_face, 0, 18)
    lines[4:] = [lines[4 + d] + face[14 + d] for d in range(3)]
    z_indices = load_indices(z_index)[0]
    lines = [turn(p, z_indices) for p in lines]
    mean = [0.5 * (a + b) for a, b in zip(face[3:7], lines[:4])]
    edge_slopes = [face[17] * p for p in combos(mean, lines[4:])]
    normal_z = face[7:10]
    drag_z = drag_flux(face[3:6], edge_slopes, normal_z)[0]
    half_sign = 0.5 * frame.sign_rows()
    half_face = frame.sides(-0.5 * lift, 0.5 * lift)
    for c in range(5):
        totals = [part_in[c, 8 * t : 8 * t + 8, :] for t in range(2)]
        if c > 0:
            spread = frame.spread_z(drag_z[c - 1])
            side = edge_tiles(frame, half_face * drag_x[c - 1])
            for t in range(2):
                scale = 1.0 / jac[8 * t : 8 * t + 8, :]
                totals[t] = totals[t] + scale * (half_sign * spread[t] + side[t])
        for t in range(2):
            out[c, 8 * t : 8 * t + 8, :] = totals[t]


def shaped(*shape, dtype=jnp.float32):
    return jax.ShapeDtypeStruct(shape, dtype)


def call(kernel, outs, *args, in_specs=None, scratch=()):
    return pl.pallas_call(
        kernel,
        out_shape=outs,
        in_specs=in_specs or [whole] * len(args),
        out_specs=[whole] * len(outs),
        scratch_shapes=scratch,
        compiler_params=pltpu.CompilerParams(vmem_limit_bytes=vmem_bytes),
        cost_estimate=pl.CostEstimate(flops=1_000_000, bytes_accessed=200_000, transcendentals=0),
    )(*args)


def exchange(low, up, axis):
    count = lax.axis_size(axis)
    from_left = lax.ppermute(up, axis, [(i, (i + 1) % count) for i in range(count)])
    from_right = lax.ppermute(low, axis, [((i + 1) % count, i) for i in range(count)])
    return from_left, from_right


def exchange_pairs(values, axis, far):
    count = lax.axis_size(axis)
    assert count % 2 == 0
    swaps = []
    for k in range(far, count, 2):
        a, b = k, (k + 1) % count
        swaps += [(a, b), (b, a)]
    return lax.ppermute(values, axis, swaps)


def local(conserved, jacobian, metric, x_master, x_flip, z_master, z_flip):
    lanes = conserved.shape[-1]
    nodes = conserved.shape[1] * conserved.shape[2]
    assert conserved.shape[1:3] == (4, 4)
    cons = conserved.reshape(5, nodes, lanes)
    jac = jacobian.reshape(nodes, lanes)
    met = metric.reshape(9, nodes, lanes)
    xm, xf, zm, zf = [a.reshape(2, a.shape[-1]) for a in (x_master, x_flip, z_master, z_flip)]
    flag = (2, xm.shape[-1])
    nodal9, nodal5 = shaped(9, nodes, lanes), shaped(5, nodes, lanes)
    index = shaped(40, lanes, dtype=jnp.int32)
    matrix_shape = shaped(2 * lanes, 3 * lanes, dtype=jnp.bfloat16)
    nodal, flags, matrix, x_index, low_z, up_z = call(
        first_kernel,
        [
            shaped(15, nodes, lanes),
            shaped(4, *flag, dtype=jnp.int32),
            matrix_shape,
            index,
            shaped(80, lanes),
            shaped(80, lanes),
        ],
        *[pltpu.with_memory_space_constraint(a, pltpu.HBM) for a in (cons, jac, met, xm, xf, zm, zf)],
        in_specs=[pl.BlockSpec(memory_space=pltpu.HBM)] * 7,
        scratch=[pltpu.SemaphoreType.DMA((2,))],
    )
    left_z, right_z = exchange(low_z, up_z, "gz")
    grad, z_index, x_back, x_face, near_one, far_one = call(
        first_cover,
        [nodal9, index, index, shaped(72, lanes)] + [shaped(40, lanes)] * 2,
        nodal, flags, matrix, x_index,
    )
    far_one = exchange_pairs(far_one, "gx", 1)
    grad, lift_z, near_two, far_two = call(
        second_kernel,
        [nodal9, shaped(72, lanes), shaped(96, lanes), shaped(56, lanes)],
        nodal, z_index, grad, x_face, near_one, left_z, right_z,
    )
    far_two = exchange_pairs(far_two, "gx", 1)
    near_two = exchange_pairs(near_two, "gx", 0)
    part, z_face, y_normal = call(
        second_cover,
        [nodal5, shaped(144, lanes), shaped(3, nodes, lanes)],
        nodal, z_index, lift_z, left_z, right_z,
    )
    part, x_other = call(
        third_cover,
        [nodal5, shaped(88, lanes)],
        nodal, x_back, grad, part, z_face, y_normal, matrix, far_one, near_two,
    )
    (rhs,) = call(
        third_kernel,
        [nodal5],
        nodal, x_back, z_index, part, x_other, z_face, near_two, far_two,
    )
    return rhs.reshape(conserved.shape)


def solution(mesh):
    in_specs = (
        P(None, "gx", "gz", None),
        P("gx", "gz", None),
        P(None, None, "gx", "gz", None),
        P("gx", "gz", None),
        P("gx", "gz", None),
        P("gx", "gz", None),
        P("gx", "gz", None),
    )
    out_specs = P(None, "gx", "gz", None)
    return jax.shard_map(local, mesh=mesh, in_specs=in_specs, out_specs=out_specs, check_vma=False)
```
